32 devices in a mesh: frames: 8 (over z, x), edges: 4 (over y, core).
Axes of the slice: x: 2, y: 2, z: 4, core: 2. Of those that a mesh axis runs over, the one named last changes fastest.
Arguments:
- fmap: bfloat16 [8, 3072, 128], P('frames'), may hold values from -6 to 6
- context: bfloat16 [8, 3072, 256], P('frames'), may hold values from -6 to 6
- poses: float32 [6, 8], P(None, 'frames'), may hold values from -0.05 to 0.05
- inv_depth: float32 [8, 3072], P('frames'), may hold values from 0.2 to 1
- targets: int32 [32], P(('frames', 'edges')), may hold values from 0 to 7, as said below
- w_corr: bfloat16 [196, 128], replicated, may hold values from -0.4375 to 0.4375
- w_gates: bfloat16 [3, 3, 256, 256], replicated, may hold values from -0.125 to 0.125
- w_cand: bfloat16 [3, 3, 256, 128], replicated, may hold values from -0.125 to 0.125
- w_head: bfloat16 [128, 4], replicated, may hold values from -0.5 to 0.5
Outputs:
- new_poses: float32 [6, 8], P(None, 'frames')
- new_depth: float32 [8, 3072], P('frames')
- hidden: bfloat16 [32, 3072, 128], P(('frames', 'edges'))
The draws below stay inside these ranges and needn't reach their ends.
Inputs may be any that keep to these rules, and one draw needn't show every extreme that they name: `targets`: every edge held by the devices of frames index f has source keyframe f and a target keyframe other than f.
All inputs are finite; a program needn't handle non-finite values.
Results may differ from the reference program's by a relative error of at most 0.0048.
Values may be sent and summed in bfloat16 or wider, within the bound.
No kernel may reach another device: no remote copies, remote signals or barrier semaphores. Data moves between devices by JAX's collectives and lax.ppermute only.
A program may use at most 128 MiB of HBM per device.

```python
import math
import jax
import jax.numpy as jnp
from jax import lax

HGT = 48
WID = 64
CH = 128
HID = 128
LEVELS = 4
RADIUS = 3
ITERS = 2
PIX = 3072
CORR = 196
NF = 8
GROUP_EDGES = 4
NE = 32


def draw_targets(key, part):
    offsets = jax.random.randint(key, (NE,), 1, NF)
    edge_rows = jnp.arange(NE)
    owner_frame = edge_rows // GROUP_EDGES
    offsets = jnp.where(edge_rows % GROUP_EDGES == 0, 1, offsets)
    return ((owner_frame + offsets) % NF).astype(jnp.int32)


def levels(own_key, shape, shards, smallest, high):
    def one(position, parts):
        draws = jax.random.uniform(jax.random.fold_in(jax.random.fold_in(own_key, 6), position), (parts,), jnp.float32, smallest / len(shards), high / len(shards))
        return jnp.repeat(jnp.exp(draws), shape[position] // parts).reshape((-1,) + (1,) * (len(shape) - position - 1))

    loudness = one(*shards[0])
    for cut in shards[1:]:
        loudness = loudness * one(*cut)
    return loudness


def normal_values(stream_key, dims, scale, bound, cuts=(), kind=jnp.bfloat16):
    values = scale * jax.random.normal(stream_key, dims, jnp.float32)
    if cuts:
        values = values * levels(stream_key, dims, cuts, -0.22, 0.18)
    return jnp.clip(values, -bound, bound).astype(kind)


def setup_inputs(seed: int = 0) -> dict:
    splits = jax.random.split(jax.random.key(seed), 10)
    fmap = normal_values(splits[0], (NF, PIX, CH), 1.0, 6.0, ((0, 8),))
    context = normal_values(splits[1], (NF, PIX, 2 * HID), 1.0, 6.0, ((0, 8),))
    poses = jnp.clip(jax.random.uniform(splits[2], (6, NF), jnp.float32, -0.05, 0.05) * levels(splits[2], (6, NF), ((1, 8),), -0.4, 0.0), -0.05, 0.05)
    inv_depth = jnp.clip(0.2 + 0.8 * jax.random.uniform(splits[3], (NF, PIX), jnp.float32) ** levels(splits[3], (NF, PIX), ((0, 8),), -0.2, 0.2), 0.2, 1.0)
    targets = draw_targets(jax.random.fold_in(splits[9], 71), 0)
    w_corr = normal_values(splits[5], (CORR, HID), CORR ** -0.5, 0.4375)
    w_gates = normal_values(splits[6], (3, 3, 2 * HID, 2 * HID), (18 * HID) ** -0.5, 0.125)
    w_cand = normal_values(splits[7], (3, 3, 2 * HID, HID), (18 * HID) ** -0.5, 0.125)
    w_head = normal_values(splits[8], (HID, 4), HID ** -0.5, 0.5)
    return dict(fmap=fmap, context=context, poses=poses, inv_depth=inv_depth, targets=targets, w_corr=w_corr, w_gates=w_gates, w_cand=w_cand, w_head=w_head)


focal = 50.0
pose_damping = 0.1
pose_floor = 1.0
depth_damping = 0.1
depth_floor = 1.0
highest = lax.Precision.HIGHEST

def pyramid_lookup(source, target):
    edge_count, hgt, wid, channels = target.shape
    span = 2 * RADIUS + 1
    offsets = jnp.arange(span) - RADIUS
    scale = 1.0 / math.sqrt(channels)
    source_wide = source.astype(jnp.float32)
    level_feat = target.astype(jnp.float32)
    collected = []
    for level_index in range(LEVELS):
        stride = 2 ** level_index
        if level_index > 0:
            shape_now = level_feat.shape
            level_feat = level_feat.reshape(edge_count, shape_now[1] // 2, 2, shape_now[2] // 2, 2, channels).mean(axis=(2, 4))
        coarse = level_feat.astype(jnp.bfloat16).astype(jnp.float32)
        coarse_cols = coarse.shape[2]
        padded = jnp.pad(coarse, ((0, 0), (RADIUS, RADIUS), (0, 0), (0, 0)))
        spread = jnp.repeat(padded, stride, axis=1)
        col_target = jnp.arange(wid)[:, None] // stride + offsets[None, :]
        picker = (col_target[:, None, :] == jnp.arange(coarse_cols)[None, :, None]).astype(jnp.float32)
        for row_shift in range(-RADIUS, RADIUS + 1):
            begin = (RADIUS + row_shift) * stride
            band = lax.slice_in_dim(spread, begin, begin + hgt, axis=1)
            volume = jnp.einsum('hwc,ehvc->ehwv', source_wide, band, precision=highest)
            collected.append(jnp.einsum('ehwv,wvk->ehwk', volume, picker, precision=highest) * scale)
    return jnp.concatenate(collected, axis=3)

def conv_same(inputs, kernel):
    return lax.conv_general_dilated(inputs.astype(jnp.float32), kernel.astype(jnp.float32), (1, 1), 'SAME', dimension_numbers=('NHWC', 'HWIO', 'NHWC'), precision=highest)

def recurrent_update(source, target, ctx, w_corr, w_gates, w_cand, w_head):
    edge_count, hgt, wid, channels = target.shape
    width = w_head.shape[0]
    corr = pyramid_lookup(source, target).astype(jnp.bfloat16)
    encoded = jax.nn.relu(jnp.dot(corr.reshape(-1, corr.shape[3]).astype(jnp.float32), w_corr.astype(jnp.float32), preferred_element_type=jnp.float32))
    net_state = jnp.tanh(ctx[:, :width].astype(jnp.float32)).astype(jnp.bfloat16)
    inject = jax.nn.relu(ctx[:, width:].astype(jnp.float32))
    motion = (encoded.reshape(edge_count, -1, width) + inject[None]).astype(jnp.bfloat16)
    motion_map = motion.reshape(edge_count, hgt, wid, width)
    state_map = jnp.broadcast_to(net_state[None], motion.shape).reshape(edge_count, hgt, wid, width)
    gates = conv_same(jnp.concatenate([state_map, motion_map], axis=3), w_gates)
    update_gate = jax.nn.sigmoid(gates[..., :width])
    reset_gate = jax.nn.sigmoid(gates[..., width:])
    reset_state = (reset_gate * state_map.astype(jnp.float32)).astype(jnp.bfloat16)
    candidate = jnp.tanh(conv_same(jnp.concatenate([reset_state, motion_map], axis=3), w_cand))
    new_state = ((1.0 - update_gate) * state_map.astype(jnp.float32) + update_gate * candidate).astype(jnp.bfloat16)
    heads = jnp.dot(new_state.reshape(-1, width).astype(jnp.float32), w_head.astype(jnp.float32), preferred_element_type=jnp.float32)
    heads = heads.reshape(edge_count, -1, 4).transpose(0, 2, 1)
    return (new_state.reshape(edge_count, -1, width), heads)

def edge_terms(relative, depth_rows, flow, confidence, hgt, wid):
    pixel_ids = jnp.arange(hgt * wid)
    col_pos = (pixel_ids % wid).astype(jnp.float32)
    row_pos = (pixel_ids // wid).astype(jnp.float32)
    center_x = (wid - 1) / 2.0
    center_y = (hgt - 1) / 2.0
    ray_x = (col_pos - center_x) / focal
    ray_y = (row_pos - center_y) / focal
    move_x, move_y, move_z, turn_x, turn_y, turn_z = [relative[index][:, None] for index in range(6)]
    point_x = ray_x + turn_y - turn_z * ray_y + depth_rows * move_x
    point_y = ray_y + turn_z * ray_x - turn_x + depth_rows * move_y
    point_z = 1.0 + turn_x * ray_y - turn_y * ray_x + depth_rows * move_z
    inverse_z = 1.0 / point_z
    slope = focal * inverse_z
    bend_u = -focal * point_x * inverse_z * inverse_z
    bend_v = -focal * point_y * inverse_z * inverse_z
    resid_u = col_pos + flow[:, 0] - (focal * point_x * inverse_z + center_x)
    resid_v = row_pos + flow[:, 1] - (focal * point_y * inverse_z + center_y)
    blank = jnp.zeros_like(slope)
    jac_u = jnp.stack([depth_rows * slope, blank, depth_rows * bend_u, bend_u * ray_y, slope - bend_u * ray_x, -slope * ray_y], axis=1)
    jac_v = jnp.stack([blank, depth_rows * slope, depth_rows * bend_v, bend_v * ray_y - slope, -bend_v * ray_x, slope * ray_x], axis=1)
    depth_u = slope * move_x + bend_u * move_z
    depth_v = slope * move_y + bend_v * move_z
    weight_u = confidence[:, 0]
    weight_v = confidence[:, 1]
    hess = jnp.einsum('ekp,elp->ekl', jac_u * weight_u[:, None], jac_u, precision=highest)
    hess = hess + jnp.einsum('ekp,elp->ekl', jac_v * weight_v[:, None], jac_v, precision=highest)
    grad = lax.optimization_barrier(jnp.sum(jac_u * (weight_u * resid_u)[:, None] + jac_v * (weight_v * resid_v)[:, None], axis=2))
    cross = jac_u * (weight_u * depth_u)[:, None] + jac_v * (weight_v * depth_v)[:, None]
    curve = weight_u * depth_u * depth_u + weight_v * depth_v * depth_v
    depth_grad = weight_u * depth_u * resid_u + weight_v * depth_v * resid_v
    return (hess, grad, cross, curve, depth_grad)

def place_edges(source_ids, target_ids, frames_total):
    frame_ids = jnp.arange(frames_total)
    sign = (target_ids[:, None] == frame_ids[None, :]).astype(jnp.float32) - (source_ids[:, None] == frame_ids[None, :]).astype(jnp.float32)
    eye_six = jnp.eye(6, dtype=jnp.float32)
    return (sign[:, None, :, None] * eye_six[None, :, None, :]).reshape(source_ids.shape[0], 6, frames_total * 6)

def solve_poses(system, rhs):
    sym = 0.5 * (system + system.T)
    damped = sym + jnp.diag(pose_damping * jnp.diagonal(sym) + pose_floor)
    factor = jnp.linalg.cholesky(damped)
    middle = lax.linalg.triangular_solve(factor, rhs[:, None], left_side=True, lower=True)
    return lax.linalg.triangular_solve(factor, middle, left_side=True, lower=True, transpose_a=True)[:, 0]

def reference(fmap, context, poses, inv_depth, targets, w_corr, w_gates, w_cand, w_head):
    frames_total, pixel_count, channels = fmap.shape
    edges_total = targets.shape[0]
    per_frame = edges_total // frames_total
    sources = (jnp.arange(edges_total) // per_frame).astype(jnp.int32)

    def one_edge(pair):
        source_id, target_id = pair
        source = fmap[source_id].reshape(HGT, WID, channels)
        target = fmap[target_id].reshape(1, HGT, WID, channels)
        return recurrent_update(source, target, context[source_id], w_corr, w_gates, w_cand, w_head)
    hidden, heads = lax.map(one_edge, (sources, targets))
    hidden = hidden.reshape(edges_total, pixel_count, -1)
    heads = heads.reshape(edges_total, 4, pixel_count)
    flow = heads[:, 0:2]
    confidence = jax.nn.sigmoid(heads[:, 2:4])
    placement = place_edges(sources, targets, frames_total)
    for step_index in range(ITERS):
        relative = jnp.take(poses, targets, axis=1) - jnp.take(poses, sources, axis=1)
        depth_rows = jnp.take(inv_depth, sources, axis=0)
        hess, grad, cross, curve, depth_grad = edge_terms(relative, depth_rows, flow, confidence, HGT, WID)
        system = jnp.einsum('ekm,ekl,eln->mn', placement, hess, placement, precision=highest)
        rhs = jnp.einsum('ekm,ek->m', placement, grad, precision=highest)
        curve_frame = curve.reshape(frames_total, per_frame, pixel_count).sum(axis=1)
        grad_frame = depth_grad.reshape(frames_total, per_frame, pixel_count).sum(axis=1)
        damped_curve = (1.0 + depth_damping) * curve_frame + depth_floor

        def coupling_of(index):
            rows_place = lax.dynamic_slice_in_dim(placement, index * per_frame, per_frame, 0)
            rows_cross = lax.dynamic_slice_in_dim(cross, index * per_frame, per_frame, 0)
            return jnp.einsum('ekm,ekp->mp', rows_place, rows_cross, precision=highest)

        def frame_schur(index):
            coupling = coupling_of(index)
            scaled = coupling / damped_curve[index][None, :]
            return (jnp.dot(scaled, coupling.T, precision=highest), jnp.dot(scaled, grad_frame[index], precision=highest))
        frame_index = jnp.arange(frames_total).astype(jnp.int32)
        schur_parts, rhs_parts = lax.map(frame_schur, frame_index)
        reduced = system - lax.optimization_barrier(jnp.sum(schur_parts, axis=0))
        reduced_rhs = rhs - lax.optimization_barrier(jnp.sum(rhs_parts, axis=0))
        step = solve_poses(reduced, reduced_rhs)
        along = lax.map(lambda index: jnp.dot(step, coupling_of(index), precision=highest), frame_index)
        poses = poses + step.reshape(frames_total, 6).T
        inv_depth = inv_depth + (grad_frame - along) / damped_curve
    return (poses, inv_depth, hidden)
```

```python
import math

import numpy as np
import jax
import jax.numpy as jnp
from jax import lax
from jax.experimental import pallas as pl
from jax.experimental.pallas import tpu as pltpu
from jax.sharding import PartitionSpec as P

HGT = 48
WID = 64
LEVELS = 4
RADIUS = 3
ITERS = 2
SPAN = 2 * RADIUS + 1
POSE = 6
LANES = 128
SUB = 8

focal = 50.0
pose_damping = 0.1
pose_floor = 1.0
depth_damping = 0.1
depth_floor = 1.0
highest = lax.Precision.HIGHEST


PITCH = (64, 32, 16, 16)
WINDOW = tuple(8 * p for p in PITCH)
START = (0, 512, 768, 896)
TOTAL = 1024
PAD_ROWS = (54, 31, 19, 13)


def column_order():
    slot = np.arange(WID)
    return 8 * (7 - slot % 8) + slot // 8


def lookup_tables():
    cols = column_order()
    perm = np.zeros((2 * WID, 2 * WID), np.float32)
    for half in range(2):
        perm[half * WID + np.arange(WID), half * WID + cols] = 1.0
    mask = np.zeros((LEVELS, 2 * WID, LANES), np.float32)
    place = np.zeros((2 * TOTAL, LEVELS * SPAN * SPAN), np.float32)
    for level in range(LEVELS):
        pitch, width = PITCH[level], WID >> level
        per_block = LANES // pitch
        for y in range(8):
            block, first = y // per_block, (y % per_block) * pitch
            for b in range(-RADIUS, RADIUS + 1):
                lane = (first + b) % LANES
                reach = (cols >> level) + b
                ok = ((reach >= 0) & (reach < width)).astype(np.float32)
                mask[level, :, lane] = np.concatenate([ok, ok])
                row = START[level] + block * LANES + lane
                for odd in range(2):
                    a = y - RADIUS - (odd if level == 0 else 0)
                    if -RADIUS <= a <= RADIUS:
                        source = level * SPAN * SPAN + (a + RADIUS) * SPAN + b + RADIUS
                        place[odd * TOTAL + row, source] = 1.0
    pools = []
    for level in range(1, LEVELS):
        step = 1 << level
        pool = np.zeros((PITCH[level], step * WID), np.float32)
        for col in range(WID):
            pool[col // step, np.arange(step) * WID + col] = 1.0 / (step * step)
        pools.append(pool)
    return perm, mask, place, pools


PERM, MASK, PLACE, POOLS = lookup_tables()


def nt_dot(a, b, **kw):
    return lax.dot_general(a, b, (((1,), (1,)), ((), ())), preferred_element_type=jnp.float32, **kw)


def nn_dot(a, b, **kw):
    return lax.dot_general(a, b, (((1,), (0,)), ((), ())), preferred_element_type=jnp.float32, **kw)


def lookup_kernel(
    where_ref, src_ref, band_ref, ctx_ref, w_ref, perm_ref, back_ref, mask_ref, pool1_ref, pool2_ref, pool3_ref,
    out_ref, pad0, pad1, pad2, pad3, corr_ref,
):
    ways, share, _ = band_ref.shape
    scale = 1.0 / math.sqrt(src_ref.shape[1])
    pads = (pad0, pad1, pad2, pad3)
    for level, pad in enumerate(pads):
        lead = RADIUS * PITCH[level]
        body = (HGT >> level) * PITCH[level]
        pad[0:lead] = jnp.zeros((lead, pad.shape[1]), pad.dtype)
        pad[lead + body :] = jnp.zeros((pad.shape[0] - lead - body, pad.shape[1]), pad.dtype)
    for slot in range(ways):
        at = pl.multiple_of(where_ref[slot] * share + RADIUS * WID, WID)
        pad0[pl.ds(at, share), :] = band_ref[slot]
    for level, pool_ref in ((1, pool1_ref), (2, pool2_ref), (3, pool3_ref)):
        rows = 1 << level
        pool = pool_ref[...]
        for row in range(HGT >> level):
            first = (RADIUS + row * rows) * WID
            pooled = nn_dot(pool, pad0[first : first + rows * WID, :])
            at = (RADIUS + row) * PITCH[level]
            pads[level][at : at + PITCH[level], :] = pooled.astype(jnp.bfloat16)

    def pair_step(pair):
        first = pl.multiple_of(pair * 2 * WID, 2 * WID)
        source = nn_dot(perm_ref[...], src_ref[pl.ds(first, 2 * WID), :]).astype(jnp.bfloat16)
        for level in range(LEVELS):
            shift = max(level - 1, 0)
            base = (pair >> shift) * PITCH[level] * (2 if level == 0 else 1)
            window = pads[level][pl.ds(pl.multiple_of(base, 16), WINDOW[level]), :]
            volume = nt_dot(source, window) * scale
            keep = mask_ref[level]
            for block in range(WINDOW[level] // LANES):
                part = volume[:, block * LANES : (block + 1) * LANES]
                rolled = []
                for group in range(2 * SUB):
                    turn = (8 >> level) * 7 + ((group % SUB) >> level)
                    rolled.append(
                        pltpu.roll(
                            part[group * SUB : (group + 1) * SUB, :],
                            (LANES - turn) % LANES,
                            1,
                            stride=8 >> level,
                            stride_axis=0,
                        )
                    )
                value = jnp.concatenate(rolled, axis=0).astype(jnp.bfloat16) * keep
                at = START[level] + block * LANES
                corr_ref[pl.ds(first, 2 * WID), at : at + LANES] = value

    def pair_loop(index, carry):
        pair_step(index * 2)
        pair_step(index * 2 + 1)
        return carry

    lax.fori_loop(0, HGT // 4, pair_loop, 0)

    rows = 8 * WID

    def block_loop(index, carry):
        first = pl.multiple_of(index * rows, rows)
        both = nn_dot(corr_ref[pl.ds(first, rows), :], w_ref[...])
        inject = jnp.maximum(ctx_ref[pl.ds(first, rows), :], 0)
        for pair in range(4):
            at = pair * 2 * WID
            encoded = jnp.concatenate(
                [both[at : at + WID, :LANES], both[at + WID : at + 2 * WID, LANES:]], axis=0
            )
            moved = nn_dot(perm_ref[...], inject[at : at + 2 * WID, :])
            motion = (jnp.maximum(encoded, 0.0) + moved).astype(jnp.bfloat16)
            restored = nn_dot(back_ref[...], motion).astype(jnp.bfloat16)
            out_ref[pl.ds(pl.multiple_of(first + at, 2 * WID), 2 * WID), :] = restored
        return carry

    lax.fori_loop(0, HGT // 8, block_loop, 0)


def lookup(where, source, bands, context, w_place):
    channels = source.shape[1]
    vmem = pl.BlockSpec(memory_space=pltpu.VMEM)
    half = lambda dtype, x: jnp.asarray(x, dtype)
    bf = jnp.bfloat16
    tables = (
        half(bf, PERM), half(bf, PERM.T), half(bf, MASK), half(bf, POOLS[0]), half(bf, POOLS[1]), half(bf, POOLS[2]),
    )
    return pl.pallas_call(
        lookup_kernel,
        grid=(1,),
        out_shape=jax.ShapeDtypeStruct((source.shape[0], w_place.shape[1] // 2), bf),
        in_specs=[
            pl.BlockSpec(memory_space=pltpu.SMEM),
            vmem,
            vmem,
            pl.BlockSpec((context.shape[0], context.shape[1] // 2), lambda i: (0, 1)),
        ]
        + [vmem] * 7,
        out_specs=vmem,
        scratch_shapes=[pltpu.VMEM((PAD_ROWS[l] * PITCH[l], channels), bf) for l in range(LEVELS)]
        + [pltpu.VMEM((source.shape[0], TOTAL), bf)],
        compiler_params=pltpu.CompilerParams(vmem_limit_bytes=48 << 20),
        name="lookup",
    )(where, source, bands, context, w_place, *tables)


def gauss_newton_terms(heads, depth_ref, rel, lift_ref, spread_ref, gram_ref, damp_ref, total_ref):
    pixels = depth_ref.shape[1]
    rows = POSE * SUB
    sublane = lax.broadcasted_iota(jnp.int32, (SUB, LANES), 0)
    lane = lax.broadcasted_iota(jnp.int32, (SUB, LANES), 1)
    col_pos = (lane % WID).astype(jnp.float32)
    lane_row = lane // WID
    center_x = (WID - 1) / 2.0
    center_y = (HGT - 1) / 2.0
    ray_x = (col_pos - center_x) / focal
    move_x, move_y, move_z, turn_x, turn_y, turn_z = rel
    pairs_u = [(a, b) for a in (0, 2, 3, 4, 5) for b in (0, 2, 3, 4, 5) if a <= b]
    pairs_v = [(a, b) for a in (1, 2, 3, 4, 5) for b in (1, 2, 3, 4, 5) if a <= b]
    keys = sorted(set(pairs_u) | set(pairs_v))

    def chunk(index, carry):
        hess, grad = dict(zip(keys, carry[0])), list(carry[1])
        at = pl.ds(pl.multiple_of(index * LANES, LANES), LANES)
        depth = jnp.broadcast_to(depth_ref[:, at], (SUB, LANES))
        flow_u, flow_v, weight_u, weight_v = [heads[i, :, at] for i in range(4)]
        row_pos = (lane_row + index * (LANES // WID)).astype(jnp.float32)
        ray_y = (row_pos - center_y) / focal
        point_x = ray_x + turn_y - turn_z * ray_y + depth * move_x
        point_y = ray_y + turn_z * ray_x - turn_x + depth * move_y
        point_z = 1.0 + turn_x * ray_y - turn_y * ray_x + depth * move_z
        inverse_z = 1.0 / point_z
        slope = focal * inverse_z
        shift_u = slope * point_x
        shift_v = slope * point_y
        bend_u = -shift_u * inverse_z
        bend_v = -shift_v * inverse_z
        resid_u = col_pos + flow_u - (shift_u + center_x)
        resid_v = row_pos + flow_v - (shift_v + center_y)
        jac_u = [depth * slope, None, depth * bend_u, bend_u * ray_y, slope - bend_u * ray_x, -slope * ray_y]
        jac_v = [None, jac_u[0], depth * bend_v, bend_v * ray_y - slope, -bend_v * ray_x, slope * ray_x]
        depth_u = slope * move_x + bend_u * move_z
        depth_v = slope * move_y + bend_v * move_z
        scaled_u = [None if j is None else weight_u * j for j in jac_u]
        scaled_v = [None if j is None else weight_v * j for j in jac_v]
        for a, b in pairs_u:
            hess[a, b] = hess[a, b] + scaled_u[a] * jac_u[b]
        for a, b in pairs_v:
            hess[a, b] = hess[a, b] + scaled_v[a] * jac_v[b]
        for c in range(POSE):
            cross = None
            for scaled, resid, along in ((scaled_u, resid_u, depth_u), (scaled_v, resid_v, depth_v)):
                if scaled[c] is not None:
                    grad[c] = grad[c] + scaled[c] * resid
                    term = scaled[c] * along
                    cross = term if cross is None else cross + term
            gram_ref[c * SUB : (c + 1) * SUB, at] = cross
        pull_u = weight_u * depth_u
        pull_v = weight_v * depth_v
        curve = jnp.sum(pull_u * depth_u + pull_v * depth_v, axis=0, keepdims=True)
        slide = jnp.sum(pull_u * resid_u + pull_v * resid_v, axis=0, keepdims=True)
        gram_ref[rows : rows + SUB, at] = jnp.where(sublane == 0, slide, 0.0)
        damp_ref[:, at] = (1.0 + depth_damping) * curve + depth_floor
        return tuple(hess[k] for k in keys), tuple(grad)

    zero = jnp.zeros((SUB, LANES), jnp.float32)
    hess, grad = lax.fori_loop(
        0, pixels // LANES, chunk, (tuple(zero for _ in keys), tuple(zero for _ in range(POSE))), unroll=2
    )
    table = {k: jnp.sum(h, axis=1, keepdims=True) for k, h in zip(keys, hess)}
    slabs = []
    for c in range(POSE):
        slab = jnp.where(lane == rows, jnp.sum(grad[c], axis=1, keepdims=True), 0.0)
        for other in range(POSE):
            key = (min(c, other), max(c, other))
            if key in table:
                slab = jnp.where(lane == sublane + other * SUB, table[key], slab)
        slabs.append(slab)
    local = jnp.concatenate(slabs, axis=0)
    gram = gram_ref[...]
    scaled = gram[0:rows, :] / damp_ref[...]
    schur = nt_dot(scaled, gram, precision=highest)
    schur = jnp.concatenate([schur, jnp.zeros((rows, LANES - rows - SUB), jnp.float32)], axis=1)
    lifted = nn_dot(lift_ref[...], local - schur, precision=highest)
    total_ref[...] = nn_dot(lifted, spread_ref[...], precision=highest)


def solve_step(parts, unknowns):
    system = parts[0][...]
    for part in parts[1:]:
        system = system + part[...]
    width = system.shape[1]
    lane = lax.broadcasted_iota(jnp.int32, (SUB, width), 1)
    sublane = lax.broadcasted_iota(jnp.int32, (SUB, width), 0)
    groups = []
    for g in range(unknowns // SUB):
        block = system[g * SUB : (g + 1) * SUB, :]
        block = jnp.where(lane == sublane + g * SUB, block * (1.0 + pose_damping) + pose_floor, block)
        groups.append(block)
    for k in range(unknowns):
        g, s = divmod(k, SUB)
        columns = [jnp.broadcast_to(block[:, k : k + 1], block.shape) for block in groups]
        pivot_row = groups[g][s : s + 1, :] / columns[g][s : s + 1, :]
        for i in range(len(groups)):
            update = groups[i] - columns[i] * pivot_row
            groups[i] = jnp.where(sublane == s, pivot_row, update) if i == g else update
    return jnp.concatenate([jnp.broadcast_to(b[:, unknowns : unknowns + 1], (SUB, LANES)) for b in groups], axis=0)


def place_heads(where_ref, slots_ref, heads):
    ways = slots_ref.shape[0]
    heads[...] = jnp.zeros(heads.shape, jnp.float32)
    for slot in range(ways):
        edge = where_ref[slot]
        for i in range(4):
            value = slots_ref[slot, i : i + 1, :]
            if i >= 2:
                value = jax.nn.sigmoid(value)
            heads[i, pl.ds(edge, 1), :] = value


def split_rel(rel_ref):
    return [rel_ref[c * SUB : (c + 1) * SUB, :] for c in range(POSE)]


def first_kernel(where_ref, slots_ref, depth_ref, rel_ref, lift_ref, spread_ref, heads, gram_ref, damp_ref, total_ref):
    place_heads(where_ref, slots_ref, heads)
    gauss_newton_terms(heads, depth_ref, split_rel(rel_ref), lift_ref, spread_ref, gram_ref, damp_ref, total_ref)


def take_step(parts, place_ref, gram_ref, damp_ref, depth_ref, out_depth_ref):
    unknowns = parts[0].shape[0]
    step = solve_step(parts, unknowns)
    edge_step = nn_dot(place_ref[...], step, precision=highest)
    slices = [edge_step[c * SUB : (c + 1) * SUB, :] for c in range(POSE)]
    rows = POSE * SUB

    def chunk(index, carry):
        at = pl.ds(pl.multiple_of(index * LANES, LANES), LANES)
        total = slices[0] * gram_ref[0:SUB, at]
        for c in range(1, POSE):
            total = total + slices[c] * gram_ref[c * SUB : (c + 1) * SUB, at]
        along = jnp.sum(total, axis=0, keepdims=True)
        out_depth_ref[:, at] = depth_ref[:, at] + (gram_ref[rows : rows + 1, at] - along) / damp_ref[:, at]
        return carry

    lax.fori_loop(0, depth_ref.shape[1] // LANES, chunk, 0, unroll=4)
    return step, edge_step


def middle_kernel(count, *refs):
    parts, refs = refs[:count], refs[count:]
    (heads, gram_ref, damp_ref, depth_ref, rel_ref, place_ref, lift_ref, spread_ref,
     out_gram, out_damp, out_total, out_depth, out_step, out_rel) = refs
    step, edge_step = take_step(parts, place_ref, gram_ref, damp_ref, depth_ref, out_depth)
    out_step[...] = step
    out_rel[...] = rel_ref[...] + edge_step
    gauss_newton_terms(heads, out_depth, split_rel(out_rel), lift_ref, spread_ref, out_gram, out_damp, out_total)


def last_kernel(count, *refs):
    parts, refs = refs[:count], refs[count:]
    gram_ref, damp_ref, depth_ref, place_ref, before_ref, out_depth, out_step = refs
    step, _ = take_step(parts, place_ref, gram_ref, damp_ref, depth_ref, out_depth)
    out_step[...] = before_ref[...] + step


def call(kernel, shapes, inputs, name, smem=0):
    vmem = pl.BlockSpec(memory_space=pltpu.VMEM)
    f32 = lambda shape: jax.ShapeDtypeStruct(shape, jnp.float32)
    return pl.pallas_call(
        kernel,
        out_shape=[f32(s) for s in shapes],
        in_specs=[pl.BlockSpec(memory_space=pltpu.SMEM)] * smem + [vmem] * (len(inputs) - smem),
        out_specs=[vmem] * len(shapes),
        compiler_params=pltpu.CompilerParams(vmem_limit_bytes=32 << 20),
        name=name,
    )(*inputs)


def sum_over(value, axis):
    size = lax.axis_size(axis)
    if size & (size - 1):
        parts = [value]
        for s in range(1, size):
            parts.append(lax.ppermute(value, axis, [(i, (i + s) % size) for i in range(size)]))
        return parts
    radices, left = [], size
    while left > 1:
        radix = 2 if left in (2, 8, 32) else 4
        radices.append(radix)
        left //= radix
    stride, parts = 1, [value]
    for radix in radices:
        value = sum(parts[1:], parts[0])
        parts = [value]
        for s in range(1, radix):
            parts.append(lax.ppermute(value, axis, [(i, i ^ (s * stride)) for i in range(size)]))
        stride *= radix
    return parts


def peer(index, slot, size):
    return index ^ slot if size & (size - 1) == 0 else (index + slot) % size


def exchange(values, axis):
    size = lax.axis_size(axis)
    out = [values[0]]
    for s in range(1, size):
        if size & (size - 1) == 0:
            pairs = [(i, i ^ s) for i in range(size)]
        else:
            pairs = [((i + s) % size, i) for i in range(size)]
        out.append(lax.ppermute(values[s], axis, pairs))
    return out


def ring_order(size):
    if size % 2:
        return list(range(size))
    return list(range(0, size, 2)) + list(range(size - 1, 0, -2))


def ring_gather(value, axis):
    size = lax.axis_size(axis)
    order = ring_order(size)
    ahead = [(order[(i + 1) % size], order[i]) for i in range(size)]
    behind = [(order[i], order[(i + 1) % size]) for i in range(size)]
    out = [None] * size
    out[0] = value
    up = down = value
    for s in range(1, size // 2 + 1):
        up = lax.ppermute(up, axis, ahead)
        out[s] = up
        if size - s > size // 2:
            down = lax.ppermute(down, axis, behind)
            out[size - s] = down
    return out


def conv_same(inputs, kernel):
    return lax.conv_general_dilated(
        inputs,
        kernel,
        (1, 1),
        "SAME",
        dimension_numbers=("NHWC", "HWIO", "NHWC"),
        preferred_element_type=jnp.float32,
    )


def recurrent_update(motion, ctx, w_gates, w_cand, w_head):
    width = w_head.shape[0]
    net_state = jnp.tanh(ctx[:, :width].astype(jnp.float32)).astype(jnp.bfloat16)
    motion_map = motion.reshape(1, HGT, WID, width)
    state_map = net_state.reshape(1, HGT, WID, width)
    gates = conv_same(jnp.concatenate([state_map, motion_map], axis=3), w_gates)
    update_gate = jax.nn.sigmoid(gates[..., :width])
    reset_gate = jax.nn.sigmoid(gates[..., width:])
    state_wide = state_map.astype(jnp.float32)
    reset_state = (reset_gate * state_wide).astype(jnp.bfloat16)
    candidate = jnp.tanh(conv_same(jnp.concatenate([reset_state, motion_map], axis=3), w_cand))
    new_state = ((1.0 - update_gate) * state_wide + update_gate * candidate).astype(jnp.bfloat16)
    hidden = new_state.reshape(-1, width)
    heads = lax.dot_general(w_head, hidden, (((0,), (1,)), ((), ())), preferred_element_type=jnp.float32)
    return hidden, heads


def per_device(fmap, context, poses, inv_depth, targets, w_corr, w_gates, w_cand, w_head):
    group = lax.axis_index("frames")
    edge_slot = lax.axis_index("edges")
    ways = lax.axis_size("edges")
    owned = poses.shape[1]
    frames_total = owned * lax.axis_size("frames")
    pixel_count = fmap.shape[1]
    channels = fmap.shape[2]
    share = pixel_count // ways
    bf = jnp.bfloat16
    where = jnp.stack([peer(edge_slot, s, ways) for s in range(ways)]).astype(jnp.int32)
    high = poses.astype(bf)
    rest = poses - high.astype(jnp.float32)
    mid = rest.astype(bf)
    low = (rest - mid.astype(jnp.float32)).astype(bf)
    terms = jnp.concatenate([high, mid, low], axis=0).reshape(1, 3 * POSE)
    tail = jnp.pad(terms, ((0, 15), (0, channels - 3 * POSE)))
    own_band = lax.dynamic_slice_in_dim(fmap[0], edge_slot * share, share, 0)
    blocks = ring_gather(jnp.concatenate([own_band, tail], axis=0), "frames")
    asked = jnp.stack(exchange([targets] * ways, "edges"))[:, 0]
    order = jnp.asarray(ring_order(frames_total), jnp.int32)
    inverse = np.argsort(np.array(ring_order(frames_total)))
    inverse = jnp.asarray(inverse, jnp.int32)
    place_now = inverse[group]
    stacked = jnp.stack(blocks)
    distance = (inverse[asked] - place_now) % frames_total
    outgoing = [
        lax.dynamic_slice(stacked, (distance[s], 0, 0), (1, share, channels))[0] for s in range(ways)
    ]
    bands = jnp.stack(exchange(outgoing, "edges"))
    pose_terms = stacked[:, share, : 3 * POSE].astype(jnp.float32)
    pose_ring = pose_terms[:, :POSE] + pose_terms[:, POSE : 2 * POSE] + pose_terms[:, 2 * POSE :]
    ring_frames = order[(place_now + jnp.arange(frames_total)) % frames_total]

    w_place = jnp.dot(jnp.asarray(PLACE, bf), w_corr, preferred_element_type=jnp.float32).astype(bf)
    w_place = jnp.concatenate([w_place[:TOTAL], w_place[TOTAL:]], axis=1)
    motion = lookup(where, fmap[0], bands, context[0], w_place)
    hidden, heads = recurrent_update(motion, context[0], w_gates, w_cand, w_head)
    slots = jnp.stack(exchange([heads] * ways, "edges"))

    unknowns = POSE * frames_total
    width = -(-(unknowns + 1) // LANES) * LANES
    rows = POSE * SUB
    edge_target = jnp.full((SUB,), -1, jnp.int32).at[where].set(asked)
    frame_ids = jnp.arange(frames_total)
    real = (jnp.arange(SUB) < ways)[:, None]
    sign = jnp.where(
        real,
        (edge_target[:, None] == frame_ids[None, :]).astype(jnp.float32)
        - (frame_ids[None, :] == group).astype(jnp.float32),
        0.0,
    )
    eye = jnp.eye(POSE, dtype=jnp.float32)
    place = (eye[:, None, :, None] * sign[None, :, None, :]).reshape(rows, unknowns)
    lift = place.T
    spread = jnp.pad(place, ((0, LANES - rows), (0, width - unknowns)))
    spread = spread + (
        (jnp.arange(LANES)[:, None] == rows) & (jnp.arange(width)[None, :] == unknowns)
    ).astype(jnp.float32)
    ring_sign = (
        (edge_target[:, None] == ring_frames[None, :]).astype(jnp.float32)
        - (ring_frames[None, :] == group).astype(jnp.float32)
    ) * real
    rel = jnp.sum(ring_sign[None] * pose_ring.T[:, None, :], axis=2)
    rel = jnp.broadcast_to(rel.reshape(rows, 1), (rows, LANES))

    big = (rows + SUB, pixel_count)
    heads_all, gram, damp, total = call(
        first_kernel,
        [(4, SUB, pixel_count), big, (1, pixel_count), (unknowns, width)],
        (where, slots, inv_depth, rel, lift, spread),
        "terms",
        smem=1,
    )
    depth = inv_depth
    step_sum = None
    for index in range(ITERS - 1):
        parts = sum_over(total, "frames")
        count = len(parts)
        gram, damp, total, depth, step, rel = call(
            lambda *refs: middle_kernel(count, *refs),
            [big, (1, pixel_count), (unknowns, width), (1, pixel_count), (unknowns, LANES), (rows, LANES)],
            (*parts, heads_all, gram, damp, depth, rel, place, lift, spread),
            "step",
        )
        step_sum = step if step_sum is None else step_sum + step
    parts = sum_over(total, "frames")
    count = len(parts)
    depth, step_sum = call(
        lambda *refs: last_kernel(count, *refs),
        [(1, pixel_count), (unknowns, LANES)],
        (*parts, gram, damp, depth, place, step_sum),
        "final",
    )
    moved = lax.dynamic_slice_in_dim(step_sum[:, 0].reshape(POSE, frames_total), group * owned, owned, 1)
    return (poses + moved, depth, hidden[None])


def solution(mesh):
    return jax.shard_map(
        per_device,
        mesh=mesh,
        in_specs=(
            P("frames", None, None),
            P("frames", None, None),
            P(None, "frames"),
            P("frames", None),
            P(("frames", "edges")),
            P(),
            P(),
            P(),
            P(),
        ),
        out_specs=(P(None, "frames"), P("frames", None), P(("frames", "edges"), None, None)),
        check_vma=False,
    )
```

```python
import math

import numpy as np
import jax
import jax.numpy as jnp
from jax import lax
from jax.experimental import pallas as pl
from jax.experimental.pallas import tpu as pltpu
from jax.sharding import PartitionSpec as P

HGT = 48
WID = 64
LEVELS = 4
RADIUS = 3
ITERS = 2
SPAN = 2 * RADIUS + 1
POSE = 6
LANES = 128
SUB = 8

focal = 50.0
pose_damping = 0.1
pose_floor = 1.0
depth_damping = 0.1
depth_floor = 1.0
highest = lax.Precision.HIGHEST


PITCH = (64, 32, 16, 16)
WINDOW = tuple(8 * p for p in PITCH)
START = (0, 512, 768, 896)
TOTAL = 1024
PAD_ROWS = (54, 31, 19, 13)


def column_order():
    slot = np.arange(WID)
    return 8 * (7 - slot % 8) + slot // 8


def lookup_tables():
    cols = column_order()
    perm = np.zeros((2 * WID, 2 * WID), np.float32)
    for half in range(2):
        perm[half * WID + np.arange(WID), half * WID + cols] = 1.0
    mask = np.zeros((LEVELS, 2 * WID, LANES), np.float32)
    place = np.zeros((2 * TOTAL, LEVELS * SPAN * SPAN), np.float32)
    for level in range(LEVELS):
        pitch, width = PITCH[level], WID >> level
        per_block = LANES // pitch
        for y in range(8):
            block, first = y // per_block, (y % per_block) * pitch
            for b in range(-RADIUS, RADIUS + 1):
                lane = (first + b) % LANES
                reach = (cols >> level) + b
                ok = ((reach >= 0) & (reach < width)).astype(np.float32)
                mask[level, :, lane] = np.concatenate([ok, ok])
                row = START[level] + block * LANES + lane
                for odd in range(2):
                    a = y - RADIUS - (odd if level == 0 else 0)
                    if -RADIUS <= a <= RADIUS:
                        source = level * SPAN * SPAN + (a + RADIUS) * SPAN + b + RADIUS
                        place[odd * TOTAL + row, source] = 1.0
    pools = []
    for level in range(1, LEVELS):
        step = 1 << level
        pool = np.zeros((PITCH[level], step * WID), np.float32)
        for col in range(WID):
            pool[col // step, np.arange(step) * WID + col] = 1.0 / (step * step)
        pools.append(pool)
    return perm, mask, place, pools


PERM, MASK, PLACE, POOLS = lookup_tables()


def nt_dot(a, b, **kw):
    return lax.dot_general(a, b, (((1,), (1,)), ((), ())), preferred_element_type=jnp.float32, **kw)


def nn_dot(a, b, **kw):
    return lax.dot_general(a, b, (((1,), (0,)), ((), ())), preferred_element_type=jnp.float32, **kw)


def edge_kernel(
    src_ref, *refs,
):
    ways = lax.axis_size("edges")
    band_refs, refs = refs[:ways], refs[ways:]
    (ctx_ref, w_ref, head_ref, perm_ref, back_ref, mask_ref, pool1_ref, pool2_ref, pool3_ref, gates_hbm, cand_hbm,
     out_ref, heads_ref, pad0, pad1, pad2, pad3, corr_ref, feat_ref, update_ref, gates_ref, cand_ref, sems) = refs
    copies = [
        pltpu.make_async_copy(gates_hbm, gates_ref, sems.at[0]),
        pltpu.make_async_copy(cand_hbm, cand_ref, sems.at[1]),
    ]
    for copy in copies:
        copy.start()
    width = out_ref.shape[1]
    edge = lax.axis_index("edges")
    share = band_refs[0].shape[0]
    scale = 1.0 / math.sqrt(src_ref.shape[1])
    pads = (pad0, pad1, pad2, pad3)
    for level, pad in enumerate(pads):
        lead = RADIUS * PITCH[level]
        body = (HGT >> level) * PITCH[level]
        pad[0:lead] = jnp.zeros((lead, pad.shape[1]), pad.dtype)
        pad[lead + body :] = jnp.zeros((pad.shape[0] - lead - body, pad.shape[1]), pad.dtype)
    for slot in range(ways):
        at = pl.multiple_of(peer(edge, slot, ways) * share + RADIUS * WID, WID)
        pad0[pl.ds(at, share), :] = band_refs[slot][...]
    for level, pool_ref in ((1, pool1_ref), (2, pool2_ref), (3, pool3_ref)):
        rows = 1 << level
        pool = pool_ref[...]
        for row in range(HGT >> level):
            first = (RADIUS + row * rows) * WID
            pooled = nn_dot(pool, pad0[first : first + rows * WID, :])
            at = (RADIUS + row) * PITCH[level]
            pads[level][at : at + PITCH[level], :] = pooled.astype(jnp.bfloat16)

    def pair_step(pair):
        first = pl.multiple_of(pair * 2 * WID, 2 * WID)
        source = nn_dot(perm_ref[...], src_ref[pl.ds(first, 2 * WID), :]).astype(jnp.bfloat16)
        for level in range(LEVELS):
            shift = max(level - 1, 0)
            base = (pair >> shift) * PITCH[level] * (2 if level == 0 else 1)
            window = pads[level][pl.ds(pl.multiple_of(base, 16), WINDOW[level]), :]
            volume = nt_dot(source, window) * scale
            keep = mask_ref[level]
            for block in range(WINDOW[level] // LANES):
                part = volume[:, block * LANES : (block + 1) * LANES]
                rolled = []
                for group in range(2 * SUB):
                    turn = (8 >> level) * 7 + ((group % SUB) >> level)
                    rolled.append(
                        pltpu.roll(
                            part[group * SUB : (group + 1) * SUB, :],
                            (LANES - turn) % LANES,
                            1,
                            stride=8 >> level,
                            stride_axis=0,
                        )
                    )
                value = jnp.concatenate(rolled, axis=0).astype(jnp.bfloat16) * keep
                at = START[level] + block * LANES
                corr_ref[pl.ds(first, 2 * WID), at : at + LANES] = value

    def pair_loop(index, carry):
        pair_step(index * 2)
        pair_step(index * 2 + 1)
        return carry

    lax.fori_loop(0, HGT // 4, pair_loop, 0)

    zero_row = jnp.zeros((WID, feat_ref.shape[1]), feat_ref.dtype)
    feat_ref[0:WID, :] = zero_row
    feat_ref[(HGT + 1) * WID :, :] = zero_row
    rows = 8 * WID

    def block_loop(index, carry):
        first = pl.multiple_of(index * rows, rows)
        both = nn_dot(corr_ref[pl.ds(first, rows), :], w_ref[...])
        inject = jnp.maximum(ctx_ref[pl.ds(first, rows), width:], 0)
        state = jnp.tanh(ctx_ref[pl.ds(first, rows), :width].astype(jnp.float32)).astype(jnp.bfloat16)
        feat_ref[pl.ds(first + WID, rows), 0:width] = state
        for pair in range(4):
            at = pair * 2 * WID
            encoded = jnp.concatenate(
                [both[at : at + WID, :LANES], both[at + WID : at + 2 * WID, LANES:]], axis=0
            )
            moved = nn_dot(perm_ref[...], inject[at : at + 2 * WID, :])
            motion = (jnp.maximum(encoded, 0.0) + moved).astype(jnp.bfloat16)
            restored = nn_dot(back_ref[...], motion).astype(jnp.bfloat16)
            feat_ref[pl.ds(pl.multiple_of(first + WID + at, WID), 2 * WID), width : 2 * width] = restored
        return carry

    lax.fori_loop(0, HGT // 8, block_loop, 0)
    for copy in copies:
        copy.wait()

    tile = 4 * WID
    column = lax.broadcasted_iota(jnp.int32, (tile, width), 0) % WID
    last_col = column == WID - 1
    first_col = column == 0

    def convolve(first, weights, lanes):
        inputs = [feat_ref[pl.ds(pl.multiple_of(first + row * WID, WID), tile), lanes] for row in range(3)]
        taps = []
        for cols in ((0, 1), (2,)) if weights(0, 0).shape[1] == LANES else ((0,), (1,), (2,)):
            total = None
            for row in range(3):
                mats = [weights(row, col) for col in cols]
                mat = mats[0] if len(mats) == 1 else jnp.concatenate(mats, axis=1)
                part = nn_dot(inputs[row], mat)
                total = part if total is None else total + part
            size = total.shape[1] // len(cols)
            taps += [total[:, i * size : (i + 1) * size] for i in range(len(cols))]
        out = []
        for half in range(taps[0].shape[1] // width):
            left, mid, right = [t[:, half * width : (half + 1) * width] for t in taps]
            left = jnp.where(first_col, 0.0, pltpu.roll(left, 1, 0))
            right = jnp.where(last_col, 0.0, pltpu.roll(right, tile - 1, 0))
            out.append(mid + left + right)
        return out

    def gates_step(index, carry):
        first = pl.multiple_of(index * tile, tile)
        update, reset = convolve(first, lambda r, c: gates_ref[r, c], slice(0, 2 * width))
        update_ref[pl.ds(first, tile), :] = jax.nn.sigmoid(update)
        state = feat_ref[pl.ds(pl.multiple_of(first + WID, WID), tile), 0:width].astype(jnp.float32)
        feat_ref[pl.ds(pl.multiple_of(first + WID, WID), tile), 2 * width :] = (
            jax.nn.sigmoid(reset) * state
        ).astype(jnp.bfloat16)
        return carry

    lax.fori_loop(0, HGT * WID // tile, gates_step, 0)

    def cand_weights(row, col):
        return jnp.concatenate([cand_ref[row, col, width:, :], cand_ref[row, col, :width, :]], axis=0)

    def cand_step(index, carry):
        first = pl.multiple_of(index * tile, tile)
        (total,) = convolve(first, cand_weights, slice(width, 3 * width))
        candidate = jnp.tanh(total)
        update = update_ref[pl.ds(first, tile), :]
        state = feat_ref[pl.ds(pl.multiple_of(first + WID, WID), tile), 0:width].astype(jnp.float32)
        hidden = ((1.0 - update) * state + update * candidate).astype(jnp.bfloat16)
        out_ref[pl.ds(first, tile), :] = hidden
        heads_ref[:, pl.ds(first, tile)] = nt_dot(head_ref[...], hidden)
        return carry

    lax.fori_loop(0, HGT * WID // tile, cand_step, 0)


def edge_update(source, bands, context, w_place, w_gates, w_cand, w_head):
    pixels, channels = source.shape
    width = w_head.shape[0]
    vmem = pl.BlockSpec(memory_space=pltpu.VMEM)
    hbm = pl.BlockSpec(memory_space=pl.ANY)
    bf, f32 = jnp.bfloat16, jnp.float32
    tables = [jnp.asarray(x, bf) for x in (PERM, PERM.T, MASK, *POOLS)]
    return pl.pallas_call(
        edge_kernel,
        out_shape=[
            jax.ShapeDtypeStruct((pixels, width), bf),
            jax.ShapeDtypeStruct((w_head.shape[1], pixels), f32),
        ],
        in_specs=[vmem] * (1 + len(bands) + 3 + len(tables)) + [hbm] * 2,
        out_specs=[vmem, vmem],
        scratch_shapes=[pltpu.VMEM((PAD_ROWS[l] * PITCH[l], channels), bf) for l in range(LEVELS)]
        + [
            pltpu.VMEM((pixels, TOTAL), bf),
            pltpu.VMEM(((HGT + 2) * WID, 3 * width), bf),
            pltpu.VMEM((pixels, width), f32),
            pltpu.VMEM(w_gates.shape, bf),
            pltpu.VMEM(w_cand.shape, bf),
            pltpu.SemaphoreType.DMA((2,)),
        ],
        compiler_params=pltpu.CompilerParams(vmem_limit_bytes=48 << 20),
        name="edge_update",
    )(source, *bands, context, w_place, w_head.T, *tables, w_gates, w_cand)


def ring_place(frame, size):
    if size % 2:
        return frame
    return jnp.where(frame % 2 == 0, frame // 2, size - (frame + 1) // 2)


def pack_kernel(pose_ref, band_ref, out_ref, sem):
    share = out_ref.shape[0] - 16
    first = pl.multiple_of(lax.axis_index("edges") * share, share)
    copy = pltpu.make_async_copy(band_ref.at[0, pl.ds(first, share), :], out_ref.at[pl.ds(0, share), :], sem)
    copy.start()
    lane = lax.broadcasted_iota(jnp.int32, (SUB, LANES), 1)
    sublane = lax.broadcasted_iota(jnp.int32, (SUB, LANES), 0)
    pose = jnp.zeros((SUB, LANES), jnp.float32)
    for c in range(POSE):
        pose = jnp.where(lane == c, pose_ref[c, 0], pose)
    high = pose.astype(jnp.bfloat16).astype(jnp.float32)
    mid = (pose - high).astype(jnp.bfloat16).astype(jnp.float32)
    low = pose - high - mid
    tail = jnp.where(sublane == 0, high, jnp.where(sublane == 1, mid, jnp.where(sublane == 2, low, 0.0)))
    tail = jnp.concatenate([tail, jnp.zeros((SUB, LANES), jnp.float32)], axis=0)
    out_ref[share:, :] = tail.astype(jnp.bfloat16)
    copy.wait()


def pack(poses, fmap, share):
    return pl.pallas_call(
        pack_kernel,
        out_shape=jax.ShapeDtypeStruct((share + 16, fmap.shape[2]), jnp.bfloat16),
        in_specs=[pl.BlockSpec(memory_space=pltpu.SMEM), pl.BlockSpec(memory_space=pl.ANY)],
        out_specs=pl.BlockSpec(memory_space=pltpu.VMEM),
        scratch_shapes=[pltpu.SemaphoreType.DMA],
        name="pack",
    )(poses, fmap)


def pick_kernel(size, ways, *refs):
    asked, blocks, outs = refs[:ways], refs[ways : ways + size], refs[ways + size : 2 * ways + size]
    pose_ref, tails, sems, tail_sem = refs[2 * ways + size :]
    share = outs[0].shape[0]
    here = ring_place(lax.axis_index("frames"), size)
    far = [lax.rem(ring_place(a[0], size) - here + size, size) for a in asked]
    for d in range(size):
        pltpu.make_async_copy(blocks[d].at[pl.ds(share, 16), :], tails.at[d], tail_sem.at[d]).start()
    for s in range(ways):
        for d in range(size):

            @pl.when(far[s] == d)
            def _(s=s, d=d):
                pltpu.make_async_copy(blocks[d].at[pl.ds(0, share), :], outs[s], sems.at[s]).start()

    for d in range(size):
        pltpu.make_async_copy(blocks[d].at[pl.ds(share, 16), :], tails.at[d], tail_sem.at[d]).wait()
    for d in range(size):
        terms = tails[d].astype(jnp.float32)
        pose_ref[d : d + 1, :] = terms[0:1, :] + terms[1:2, :] + terms[2:3, :]
    for s in range(ways):
        pltpu.make_async_copy(blocks[0].at[pl.ds(0, share), :], outs[s], sems.at[s]).wait()


def pick(asked, blocks):
    ways, size = len(asked), len(blocks)
    share, channels = blocks[0].shape[0] - 16, blocks[0].shape[1]
    vmem = pl.BlockSpec(memory_space=pltpu.VMEM)
    out = pl.pallas_call(
        lambda *refs: pick_kernel(size, ways, *refs),
        out_shape=[jax.ShapeDtypeStruct((share, channels), jnp.bfloat16)] * ways
        + [jax.ShapeDtypeStruct((size, channels), jnp.float32)],
        in_specs=[pl.BlockSpec(memory_space=pltpu.SMEM)] * ways + [pl.BlockSpec(memory_space=pl.ANY)] * size,
        out_specs=[vmem] * (ways + 1),
        scratch_shapes=[
            pltpu.VMEM((size, 16, channels), jnp.bfloat16),
            pltpu.SemaphoreType.DMA((ways,)),
            pltpu.SemaphoreType.DMA((size,)),
        ],
        name="pick",
    )(*asked, *blocks)
    return out[:ways], out[ways]


def gauss_newton_terms(heads, depth_ref, rel, lift_ref, spread_ref, gram_ref, damp_ref, total_ref):
    pixels = depth_ref.shape[1]
    rows = POSE * SUB
    sublane = lax.broadcasted_iota(jnp.int32, (SUB, LANES), 0)
    lane = lax.broadcasted_iota(jnp.int32, (SUB, LANES), 1)
    col_pos = (lane % WID).astype(jnp.float32)
    lane_row = lane // WID
    center_x = (WID - 1) / 2.0
    center_y = (HGT - 1) / 2.0
    ray_x = (col_pos - center_x) / focal
    move_x, move_y, move_z, turn_x, turn_y, turn_z = rel
    pairs_u = [(a, b) for a in (0, 2, 3, 4, 5) for b in (0, 2, 3, 4, 5) if a <= b]
    pairs_v = [(a, b) for a in (1, 2, 3, 4, 5) for b in (1, 2, 3, 4, 5) if a <= b]
    keys = sorted(set(pairs_u) | set(pairs_v))

    def chunk(index, carry):
        hess, grad = dict(zip(keys, carry[0])), list(carry[1])
        at = pl.ds(pl.multiple_of(index * LANES, LANES), LANES)
        depth = jnp.broadcast_to(depth_ref[:, at], (SUB, LANES))
        flow_u, flow_v, weight_u, weight_v = [heads[i, :, at] for i in range(4)]
        row_pos = (lane_row + index * (LANES // WID)).astype(jnp.float32)
        ray_y = (row_pos - center_y) / focal
        point_x = ray_x + turn_y - turn_z * ray_y + depth * move_x
        point_y = ray_y + turn_z * ray_x - turn_x + depth * move_y
        point_z = 1.0 + turn_x * ray_y - turn_y * ray_x + depth * move_z
        inverse_z = 1.0 / point_z
        slope = focal * inverse_z
        shift_u = slope * point_x
        shift_v = slope * point_y
        bend_u = -shift_u * inverse_z
        bend_v = -shift_v * inverse_z
        resid_u = col_pos + flow_u - (shift_u + center_x)
        resid_v = row_pos + flow_v - (shift_v + center_y)
        jac_u = [depth * slope, None, depth * bend_u, bend_u * ray_y, slope - bend_u * ray_x, -slope * ray_y]
        jac_v = [None, jac_u[0], depth * bend_v, bend_v * ray_y - slope, -bend_v * ray_x, slope * ray_x]
        depth_u = slope * move_x + bend_u * move_z
        depth_v = slope * move_y + bend_v * move_z
        scaled_u = [None if j is None else weight_u * j for j in jac_u]
        scaled_v = [None if j is None else weight_v * j for j in jac_v]
        for a, b in pairs_u:
            hess[a, b] = hess[a, b] + scaled_u[a] * jac_u[b]
        for a, b in pairs_v:
            hess[a, b] = hess[a, b] + scaled_v[a] * jac_v[b]
        for c in range(POSE):
            cross = None
            for scaled, resid, along in ((scaled_u, resid_u, depth_u), (scaled_v, resid_v, depth_v)):
                if scaled[c] is not None:
                    grad[c] = grad[c] + scaled[c] * resid
                    term = scaled[c] * along
                    cross = term if cross is None else cross + term
            gram_ref[c * SUB : (c + 1) * SUB, at] = cross
        pull_u = weight_u * depth_u
        pull_v = weight_v * depth_v
        curve = jnp.sum(pull_u * depth_u + pull_v * depth_v, axis=0, keepdims=True)
        slide = jnp.sum(pull_u * resid_u + pull_v * resid_v, axis=0, keepdims=True)
        gram_ref[rows : rows + SUB, at] = jnp.where(sublane == 0, slide, 0.0)
        damp_ref[:, at] = (1.0 + depth_damping) * curve + depth_floor
        return tuple(hess[k] for k in keys), tuple(grad)

    zero = jnp.zeros((SUB, LANES), jnp.float32)
    hess, grad = lax.fori_loop(
        0, pixels // LANES, chunk, (tuple(zero for _ in keys), tuple(zero for _ in range(POSE))), unroll=2
    )
    table = {k: jnp.sum(h, axis=1, keepdims=True) for k, h in zip(keys, hess)}
    slabs = []
    for c in range(POSE):
        slab = jnp.where(lane == rows, jnp.sum(grad[c], axis=1, keepdims=True), 0.0)
        for other in range(POSE):
            key = (min(c, other), max(c, other))
            if key in table:
                slab = jnp.where(lane == sublane + other * SUB, table[key], slab)
        slabs.append(slab)
    local = jnp.concatenate(slabs, axis=0)
    gram = gram_ref[...]
    scaled = gram[0:rows, :] / damp_ref[...]
    schur = nt_dot(scaled, gram, precision=highest)
    schur = jnp.concatenate([schur, jnp.zeros((rows, LANES - rows - SUB), jnp.float32)], axis=1)
    lifted = nn_dot(lift_ref[:, :rows], local - schur, precision=highest)
    total_ref[...] = nn_dot(lifted, spread_ref[...], precision=highest)


def solve_step(parts, unknowns):
    system = parts[0][...]
    for part in parts[1:]:
        system = system + part[...]
    width = system.shape[1]
    lane = lax.broadcasted_iota(jnp.int32, (SUB, width), 1)
    sublane = lax.broadcasted_iota(jnp.int32, (SUB, width), 0)
    groups = []
    for g in range(unknowns // SUB):
        block = system[g * SUB : (g + 1) * SUB, :]
        block = jnp.where(lane == sublane + g * SUB, block * (1.0 + pose_damping) + pose_floor, block)
        groups.append(block)
    for k in range(unknowns):
        g, s = divmod(k, SUB)
        columns = [jnp.broadcast_to(block[:, k : k + 1], block.shape) for block in groups]
        pivot_row = groups[g][s : s + 1, :] / columns[g][s : s + 1, :]
        for i in range(len(groups)):
            update = groups[i] - columns[i] * pivot_row
            groups[i] = jnp.where(sublane == s, pivot_row, update) if i == g else update
    return jnp.concatenate([jnp.broadcast_to(b[:, unknowns : unknowns + 1], (SUB, LANES)) for b in groups], axis=0)


def split_rel(rel_ref):
    return [rel_ref[c * SUB : (c + 1) * SUB, :] for c in range(POSE)]


def first_kernel(ways, *refs):
    asked, slots, refs = refs[:ways], refs[ways : 2 * ways], refs[2 * ways :]
    (pose_ref, depth_ref, heads, gram_ref, damp_ref, total_ref, rel_ref, place_ref, lift_ref, spread_ref) = refs
    frames = lax.axis_size("frames")
    group = lax.axis_index("frames")
    here = ring_place(group, frames)
    unknowns, width = total_ref.shape
    rows = POSE * SUB
    edge_slot = lax.axis_index("edges")
    heads[...] = jnp.zeros(heads.shape, jnp.float32)
    sublane = lax.broadcasted_iota(jnp.int32, (SUB, LANES), 0)
    lane = lax.broadcasted_iota(jnp.int32, (SUB, LANES), 1)
    wide_sub = lax.broadcasted_iota(jnp.int32, (SUB, width), 0)
    wide_lane = lax.broadcasted_iota(jnp.int32, (SUB, width), 1)
    rel = [jnp.zeros((SUB, LANES), jnp.float32) for _ in range(POSE)]
    place = [jnp.zeros((SUB, width), jnp.float32) for _ in range(POSE)]
    lift = [jnp.zeros((SUB, LANES), jnp.float32) for _ in range(unknowns // SUB)]
    for slot in range(ways):
        edge = peer(edge_slot, slot, ways)
        target = asked[slot][0]
        far = lax.rem(ring_place(target, frames) - here + frames, frames)
        for i in range(4):
            value = slots[slot][i : i + 1, :]
            if i >= 2:
                value = jax.nn.sigmoid(value)
            heads[i, pl.ds(edge, 1), :] = value
        for c in range(POSE):
            rel[c] = jnp.where(sublane == edge, pose_ref[far, c] - pose_ref[0, c], rel[c])
            at_target = (wide_lane == c * frames + target).astype(jnp.float32)
            at_source = (wide_lane == c * frames + group).astype(jnp.float32)
            place[c] = jnp.where(wide_sub == edge, at_target - at_source, place[c])
        for g in range(unknowns // SUB):
            c, n = divmod(g * SUB, frames)
            frame = sublane + n
            hit = (frame == target).astype(jnp.float32) - (frame == group).astype(jnp.float32)
            lift[g] = jnp.where(lane == c * SUB + edge, hit, lift[g])
    for c in range(POSE):
        rel_ref[c * SUB : (c + 1) * SUB, :] = rel[c]
        place_ref[c * SUB : (c + 1) * SUB, :] = place[c]
        spread_ref[c * SUB : (c + 1) * SUB, :] = place[c]
    spread_ref[rows : rows + SUB, :] = ((wide_lane == unknowns) & (wide_sub == 0)).astype(jnp.float32)
    spread_ref[rows + SUB :, :] = jnp.zeros((LANES - rows - SUB, width), jnp.float32)
    for g in range(unknowns // SUB):
        lift_ref[g * SUB : (g + 1) * SUB, :] = lift[g]
    gauss_newton_terms(heads, depth_ref, split_rel(rel_ref), lift_ref, spread_ref, gram_ref, damp_ref, total_ref)


def take_step(parts, place_ref, gram_ref, damp_ref, depth_ref, out_depth_ref):
    unknowns = parts[0].shape[0]
    step = solve_step(parts, unknowns)
    edge_step = nn_dot(place_ref[:, :unknowns], step, precision=highest)
    slices = [edge_step[c * SUB : (c + 1) * SUB, :] for c in range(POSE)]
    rows = POSE * SUB

    def chunk(index, carry):
        at = pl.ds(pl.multiple_of(index * LANES, LANES), LANES)
        total = slices[0] * gram_ref[0:SUB, at]
        for c in range(1, POSE):
            total = total + slices[c] * gram_ref[c * SUB : (c + 1) * SUB, at]
        along = jnp.sum(total, axis=0, keepdims=True)
        out_depth_ref[:, at] = depth_ref[:, at] + (gram_ref[rows : rows + 1, at] - along) / damp_ref[:, at]
        return carry

    lax.fori_loop(0, depth_ref.shape[1] // LANES, chunk, 0, unroll=4)
    return step, edge_step


def middle_kernel(count, *refs):
    parts, refs = refs[:count], refs[count:]
    (heads, gram_ref, damp_ref, depth_ref, rel_ref, place_ref, lift_ref, spread_ref,
     out_gram, out_damp, out_total, out_depth, out_step, out_rel) = refs
    step, edge_step = take_step(parts, place_ref, gram_ref, damp_ref, depth_ref, out_depth)
    out_step[...] = step
    out_rel[...] = rel_ref[...] + edge_step
    gauss_newton_terms(heads, out_depth, split_rel(out_rel), lift_ref, spread_ref, out_gram, out_damp, out_total)


def last_kernel(count, *refs):
    own_ref, parts, refs = refs[0], refs[1 : count + 1], refs[count + 1 :]
    before, refs = refs[: ITERS - 1], refs[ITERS - 1 :]
    gram_ref, damp_ref, depth_ref, place_ref, out_depth, out_pose, held = refs
    step, _ = take_step(parts, place_ref, gram_ref, damp_ref, depth_ref, out_depth)
    for other in before:
        step = step + other[...]
    held[...] = step
    frames, group = lax.axis_size("frames"), lax.axis_index("frames")
    for c in range(POSE):
        out_pose[c : c + 1, :] = own_ref[c : c + 1, :] + held[pl.ds(c * frames + group, 1), :][:, :1]


def call(kernel, shapes, inputs, name, smem=(), scratch=()):
    vmem = pl.BlockSpec(memory_space=pltpu.VMEM)
    f32 = lambda shape: jax.ShapeDtypeStruct(shape, jnp.float32)
    return pl.pallas_call(
        kernel,
        out_shape=[f32(s) for s in shapes],
        in_specs=[
            pl.BlockSpec(memory_space=pltpu.SMEM if i in smem else pltpu.VMEM) for i in range(len(inputs))
        ],
        out_specs=[vmem] * len(shapes),
        scratch_shapes=[pltpu.VMEM(s, jnp.float32) for s in scratch],
        compiler_params=pltpu.CompilerParams(vmem_limit_bytes=32 << 20),
        name=name,
    )(*inputs)


def sum_over(value, axis):
    size = lax.axis_size(axis)
    if size & (size - 1):
        parts = [value]
        for s in range(1, size):
            parts.append(lax.ppermute(value, axis, [(i, (i + s) % size) for i in range(size)]))
        return parts
    radices, left = [], size
    while left > 1:
        radix = 2 if left in (2, 8, 32) else 4
        radices.append(radix)
        left //= radix
    stride, parts = 1, [value]
    for radix in radices:
        value = sum(parts[1:], parts[0])
        parts = [value]
        for s in range(1, radix):
            parts.append(lax.ppermute(value, axis, [(i, i ^ (s * stride)) for i in range(size)]))
        stride *= radix
    return parts


def peer(index, slot, size):
    return index ^ slot if size & (size - 1) == 0 else (index + slot) % size


def exchange(values, axis):
    size = lax.axis_size(axis)
    out = [values[0]]
    for s in range(1, size):
        if size & (size - 1) == 0:
            pairs = [(i, i ^ s) for i in range(size)]
        else:
            pairs = [((i + s) % size, i) for i in range(size)]
        out.append(lax.ppermute(values[s], axis, pairs))
    return out


def ring_order(size):
    if size % 2:
        return list(range(size))
    return list(range(0, size, 2)) + list(range(size - 1, 0, -2))


def ring_gather(value, axis):
    size = lax.axis_size(axis)
    order = ring_order(size)
    ahead = [(order[(i + 1) % size], order[i]) for i in range(size)]
    behind = [(order[i], order[(i + 1) % size]) for i in range(size)]
    out = [None] * size
    out[0] = value
    up = down = value
    for s in range(1, size // 2 + 1):
        up = lax.ppermute(up, axis, ahead)
        out[s] = up
        if size - s > size // 2:
            down = lax.ppermute(down, axis, behind)
            out[size - s] = down
    return out


def per_device(fmap, context, poses, inv_depth, targets, w_corr, w_gates, w_cand, w_head):
    ways = lax.axis_size("edges")
    frames_total = lax.axis_size("frames")
    pixel_count = fmap.shape[1]
    share = pixel_count // ways
    bf = jnp.bfloat16
    blocks = ring_gather(pack(poses, fmap, share), "frames")
    asked = exchange([targets] * ways, "edges")
    outgoing, pose_table = pick(asked, blocks)
    bands = exchange(outgoing, "edges")

    w_place = jnp.dot(jnp.asarray(PLACE, bf), w_corr, preferred_element_type=jnp.float32).astype(bf)
    w_place = jnp.concatenate([w_place[:TOTAL], w_place[TOTAL:]], axis=1)
    hidden, heads = edge_update(fmap[0], bands, context[0], w_place, w_gates, w_cand, w_head)
    slots = exchange([heads] * ways, "edges")

    unknowns = POSE * frames_total
    width = -(-(unknowns + 1) // LANES) * LANES
    rows = POSE * SUB
    big, line = (rows + SUB, pixel_count), (1, pixel_count)
    heads_all, gram, damp, total, rel, place, lift, spread = call(
        lambda *refs: first_kernel(ways, *refs),
        [(4, SUB, pixel_count), big, line, (unknowns, width), (rows, LANES), (rows, width), (unknowns, LANES), (LANES, width)],
        (*asked, *slots, pose_table, inv_depth),
        "terms",
        smem=(*range(ways), 2 * ways),
    )
    depth = inv_depth
    steps = []
    for index in range(ITERS - 1):
        parts = sum_over(total, "frames")
        count = len(parts)
        gram, damp, total, depth, step, rel = call(
            lambda *refs: middle_kernel(count, *refs),
            [big, line, (unknowns, width), line, (unknowns, LANES), (rows, LANES)],
            (*parts, heads_all, gram, damp, depth, rel, place, lift, spread),
            "step",
        )
        steps.append(step)
    parts = sum_over(total, "frames")
    count = len(parts)
    depth, new_poses = call(
        lambda *refs: last_kernel(count, *refs),
        [line, poses.shape],
        (poses, *parts, *steps, gram, damp, depth, place),
        "final",
        scratch=[(unknowns, LANES)],
    )
    return (new_poses, depth, hidden[None])


def solution(mesh):
    return jax.shard_map(
        per_device,
        mesh=mesh,
        in_specs=(
            P("frames", None, None),
            P("frames", None, None),
            P(None, "frames"),
            P("frames", None),
            P(("frames", "edges")),
            P(),
            P(),
            P(),
            P(),
        ),
        out_specs=(P(None, "frames"), P("frames", None), P(("frames", "edges"), None, None)),
        check_vma=False,
    )
```

```python
import math

import numpy as np
import jax
import jax.numpy as jnp
from jax import lax
from jax.experimental import pallas as pl
from jax.experimental.pallas import tpu as pltpu
from jax.sharding import PartitionSpec as P

HGT = 48
WID = 64
LEVELS = 4
RADIUS = 3
ITERS = 2
SPAN = 2 * RADIUS + 1
POSE = 6
LANES = 128
SUB = 8
PIVOTS = 8

focal = 50.0
pose_damping = 0.1
pose_floor = 1.0
depth_damping = 0.1
depth_floor = 1.0
highest = lax.Precision.HIGHEST


PITCH = (64, 32, 16, 16)
WINDOW = tuple(8 * p for p in PITCH)
START = (0, 512, 768, 896)
TOTAL = 1024
PAD_ROWS = (54, 31, 19, 13)


def column_order():
    slot = np.arange(WID)
    return 8 * (7 - slot % 8) + slot // 8


def lookup_tables():
    cols = column_order()
    perm = np.zeros((2 * WID, 2 * WID), np.float32)
    for half in range(2):
        perm[half * WID + np.arange(WID), half * WID + cols] = 1.0
    mask = np.zeros((LEVELS, 2 * WID, LANES), np.float32)
    place = np.zeros((2 * TOTAL, LEVELS * SPAN * SPAN), np.float32)
    for level in range(LEVELS):
        pitch, width = PITCH[level], WID >> level
        per_block = LANES // pitch
        for y in range(8):
            block, first = y // per_block, (y % per_block) * pitch
            for b in range(-RADIUS, RADIUS + 1):
                lane = (first + b) % LANES
                reach = (cols >> level) + b
                ok = ((reach >= 0) & (reach < width)).astype(np.float32)
                mask[level, :, lane] = np.concatenate([ok, ok])
                row = START[level] + block * LANES + lane
                for odd in range(2):
                    a = y - RADIUS - (odd if level == 0 else 0)
                    if -RADIUS <= a <= RADIUS:
                        source = level * SPAN * SPAN + (a + RADIUS) * SPAN + b + RADIUS
                        place[odd * TOTAL + row, source] = 1.0
    pools = []
    for level in range(1, LEVELS):
        step = 1 << level
        pool = np.zeros((PITCH[level], step * WID), np.float32)
        for col in range(WID):
            pool[col // step, np.arange(step) * WID + col] = 1.0 / (step * step)
        pools.append(pool)
    return perm, mask, place, pools


PERM, MASK, PLACE, POOLS = lookup_tables()


def nt_dot(a, b, **kw):
    return lax.dot_general(a, b, (((1,), (1,)), ((), ())), preferred_element_type=jnp.float32, **kw)


def nn_dot(a, b, **kw):
    return lax.dot_general(a, b, (((1,), (0,)), ((), ())), preferred_element_type=jnp.float32, **kw)


def prepare_kernel(src_ref, ctx_ref, perm_ref, out_src, out_state, out_inject):
    width = out_state.shape[1]
    perm = perm_ref[...]

    def pair_loop(index, carry):
        at = pl.ds(pl.multiple_of(index * 2 * WID, 2 * WID), 2 * WID)
        out_src[at, :] = nn_dot(perm, src_ref[at, :]).astype(jnp.bfloat16)
        context = nn_dot(perm, ctx_ref[at, :])
        out_state[at, :] = jnp.tanh(context[:, :width]).astype(jnp.bfloat16)
        out_inject[at, :] = jnp.maximum(context[:, width:], 0.0).astype(jnp.bfloat16)
        return carry

    lax.fori_loop(0, HGT // 2, pair_loop, 0, unroll=4)


def prepare(source, context):
    vmem = pl.BlockSpec(memory_space=pltpu.VMEM)
    pixels, channels = source.shape
    half = context.shape[1] // 2
    return pl.pallas_call(
        prepare_kernel,
        out_shape=[jax.ShapeDtypeStruct((pixels, n), jnp.bfloat16) for n in (channels, half, half)],
        in_specs=[vmem] * 3,
        out_specs=[vmem] * 3,
        compiler_params=pltpu.CompilerParams(vmem_limit_bytes=16 << 20),
        name="prepare",
    )(source, context, jnp.asarray(PERM, jnp.bfloat16))


def edge_kernel(ways, *refs):
    band_refs, refs = refs[:ways], refs[ways:]
    (src_ref, state_in, inject_ref, w_ref, head_ref, back_ref, mask_ref, pool1_ref, pool2_ref, pool3_ref, gates_hbm,
     cand_hbm, out_ref, heads_ref, pad0, pad1, pad2, pad3, corr_ref, state_ref, motion_ref, reset_ref, update_ref,
     gates_ref, cand_ref, sems) = refs
    copies = [
        pltpu.make_async_copy(gates_hbm, gates_ref, sems.at[0]),
        pltpu.make_async_copy(cand_hbm, cand_ref, sems.at[1]),
    ]
    for copy in copies:
        copy.start()
    width = out_ref.shape[1]
    edge = lax.axis_index("edges")
    share = band_refs[0].shape[0]
    scale = 1.0 / math.sqrt(src_ref.shape[1])
    pads = (pad0, pad1, pad2, pad3)
    for level, pad in enumerate(pads):
        lead = RADIUS * PITCH[level]
        body = (HGT >> level) * PITCH[level]
        pad[0:lead] = jnp.zeros((lead, pad.shape[1]), pad.dtype)
        pad[lead + body :] = jnp.zeros((pad.shape[0] - lead - body, pad.shape[1]), pad.dtype)
    for ref in (state_ref, motion_ref, reset_ref):
        ref[0:WID, :] = jnp.zeros((WID, width), ref.dtype)
        ref[(HGT + 1) * WID :, :] = jnp.zeros((WID, width), ref.dtype)
    state_ref[WID : (HGT + 1) * WID, :] = state_in[...]
    for slot in range(ways):
        at = pl.multiple_of(peer(edge, slot, ways) * share + RADIUS * WID, WID)
        pad0[pl.ds(at, share), :] = band_refs[slot][...]
    for level, pool_ref in ((1, pool1_ref), (2, pool2_ref), (3, pool3_ref)):
        rows = 1 << level
        pool = pool_ref[...]
        for row in range(HGT >> level):
            first = (RADIUS + row * rows) * WID
            pooled = nn_dot(pool, pad0[first : first + rows * WID, :])
            at = (RADIUS + row) * PITCH[level]
            pads[level][at : at + PITCH[level], :] = pooled.astype(jnp.bfloat16)

    tile = 8 * WID
    blocks = HGT // 8
    start = lambda block: block * tile if isinstance(block, int) else pl.multiple_of(block * tile, tile)

    def look_up(block):
        for inner in range(4):
            pair = block * 4 + inner
            first = start(block) + inner * 2 * WID
            source = src_ref[pl.ds(first, 2 * WID), :]
            for level in range(LEVELS):
                shift = max(level - 1, 0)
                base = (pair >> shift) * PITCH[level] * (2 if level == 0 else 1)
                base = base if isinstance(base, int) else pl.multiple_of(base, 16)
                volume = nt_dot(source, pads[level][pl.ds(base, WINDOW[level]), :]) * scale
                keep = mask_ref[level]
                for lanes in range(WINDOW[level] // LANES):
                    part = volume[:, lanes * LANES : (lanes + 1) * LANES]
                    rolled = []
                    for group in range(2 * SUB):
                        turn = (8 >> level) * 7 + ((group % SUB) >> level)
                        rolled.append(
                            pltpu.roll(
                                part[group * SUB : (group + 1) * SUB, :],
                                (LANES - turn) % LANES,
                                1,
                                stride=8 >> level,
                                stride_axis=0,
                            )
                        )
                    value = jnp.concatenate(rolled, axis=0).astype(jnp.bfloat16) * keep
                    at = START[level] + lanes * LANES
                    corr_ref[pl.ds(first, 2 * WID), at : at + LANES] = value

    def encode(block):
        first = start(block)
        both = nn_dot(corr_ref[pl.ds(first, tile), :], w_ref[...])
        both = both.reshape(4, 2, WID, 2 * width)
        encoded = jnp.concatenate([both[:, :1, :, :width], both[:, 1:, :, width:]], axis=1).reshape(tile, width)
        inject = inject_ref[pl.ds(first, tile), :].astype(jnp.float32)
        motion_ref[pl.ds(first + WID, tile), :] = (jnp.maximum(encoded, 0.0) + inject).astype(jnp.bfloat16)

    sub = lax.broadcasted_iota(jnp.int32, (8, SUB, width), 1)

    def convolve(block, left_ref, right_ref, weights, columns):
        first = start(block)
        inputs = []
        for row in range(3):
            at = pl.ds(first + row * WID, tile)
            inputs.append(jnp.concatenate([left_ref[at, :], right_ref[at, :]], axis=1))
        taps = []
        for cols in columns:
            total = None
            for row in range(3):
                mats = [weights(row, col) for col in cols]
                mat = mats[0] if len(mats) == 1 else jnp.concatenate(mats, axis=1)
                part = nn_dot(inputs[row], mat)
                total = part if total is None else total + part
            size = total.shape[1] // len(cols)
            taps += [total[:, i * size : (i + 1) * size] for i in range(len(cols))]
        out = []
        for half in range(taps[0].shape[1] // width):
            left, mid, right = [t[:, half * width : (half + 1) * width].reshape(8, WID, width) for t in taps]
            wrapped = jnp.where(sub == SUB - 1, 0.0, jnp.roll(left[:, WID - SUB :], -1, axis=1))
            before = jnp.concatenate([wrapped, left[:, : WID - SUB]], axis=1)
            wrapped = jnp.where(sub == 0, 0.0, jnp.roll(right[:, :SUB], 1, axis=1))
            after = jnp.concatenate([right[:, SUB:], wrapped], axis=1)
            out.append((mid + before + after).reshape(tile, width))
        return out

    def gates(block):
        first = start(block)
        update, reset = convolve(
            block, state_ref, motion_ref, lambda r, c: gates_ref[r, c], ((0,), (1,), (2,))
        )
        update_ref[pl.ds(first, tile), :] = jax.nn.sigmoid(update)
        state = state_ref[pl.ds(first + WID, tile), :].astype(jnp.float32)
        reset_ref[pl.ds(first + WID, tile), :] = (jax.nn.sigmoid(reset) * state).astype(jnp.bfloat16)

    def candidate(block):
        first = start(block)
        (total,) = convolve(block, reset_ref, motion_ref, lambda r, c: cand_ref[r, c], ((0, 1), (2,)))
        update = update_ref[pl.ds(first, tile), :]
        state = state_ref[pl.ds(first + WID, tile), :].astype(jnp.float32)
        hidden = ((1.0 - update) * state + update * jnp.tanh(total)).astype(jnp.bfloat16)
        for inner in range(4):
            at = inner * 2 * WID
            ordered = nn_dot(back_ref[...], hidden[at : at + 2 * WID, :]).astype(jnp.bfloat16)
            out_ref[pl.ds(first + at, 2 * WID), :] = ordered
            heads_ref[:, pl.ds(first + at, 2 * WID)] = nt_dot(head_ref[...], ordered)

    look_up(0)

    def first_loop(block, carry):
        encode(block - 1)
        look_up(block)
        return carry

    lax.fori_loop(1, blocks, first_loop, 0)
    encode(blocks - 1)
    for copy in copies:
        copy.wait()
    gates(0)
    gates(1)

    def second_loop(block, carry):
        candidate(block - 2)
        gates(block)
        return carry

    lax.fori_loop(2, blocks, second_loop, 0)
    candidate(blocks - 2)
    candidate(blocks - 1)


def edge_update(bands, source, state, inject, w_place, w_gates, w_cand, w_head):
    pixels, channels = source.shape
    width = w_head.shape[0]
    ways = len(bands)
    vmem = pl.BlockSpec(memory_space=pltpu.VMEM)
    hbm = pl.BlockSpec(memory_space=pl.ANY)
    bf, f32 = jnp.bfloat16, jnp.float32
    tables = [jnp.asarray(x, bf) for x in (PERM.T, MASK, *POOLS)]
    return pl.pallas_call(
        lambda *refs: edge_kernel(ways, *refs),
        out_shape=[
            jax.ShapeDtypeStruct((pixels, width), bf),
            jax.ShapeDtypeStruct((w_head.shape[1], pixels), f32),
        ],
        in_specs=[vmem] * (ways + 5 + len(tables)) + [hbm] * 2,
        out_specs=[vmem, vmem],
        scratch_shapes=[pltpu.VMEM((PAD_ROWS[l] * PITCH[l], channels), bf) for l in range(LEVELS)]
        + [pltpu.VMEM((pixels, TOTAL), bf)]
        + [pltpu.VMEM(((HGT + 2) * WID, width), bf)] * 3
        + [
            pltpu.VMEM((pixels, width), f32),
            pltpu.VMEM(w_gates.shape, bf),
            pltpu.VMEM(w_cand.shape, bf),
            pltpu.SemaphoreType.DMA((2,)),
        ],
        compiler_params=pltpu.CompilerParams(vmem_limit_bytes=48 << 20),
        name="edge_update",
    )(*bands, source, state, inject, w_place, w_head.T, *tables, w_gates, w_cand)


def ring_place(frame, size):
    if size % 2:
        return frame
    return jnp.where(frame % 2 == 0, frame // 2, size - (frame + 1) // 2)


def pack_kernel(pose_ref, band_ref, out_ref, sem):
    share = out_ref.shape[0] - 16
    first = pl.multiple_of(lax.axis_index("edges") * share, share)
    copy = pltpu.make_async_copy(band_ref.at[0, pl.ds(first, share), :], out_ref.at[pl.ds(0, share), :], sem)
    copy.start()
    lane = lax.broadcasted_iota(jnp.int32, (SUB, LANES), 1)
    sublane = lax.broadcasted_iota(jnp.int32, (SUB, LANES), 0)
    column = jnp.broadcast_to(pose_ref[...], (POSE, LANES))
    column = jnp.where(lane[:POSE] == sublane[:POSE], column, 0.0)
    pose = jnp.broadcast_to(jnp.sum(column, axis=0, keepdims=True), (SUB, LANES))
    high = pose.astype(jnp.bfloat16).astype(jnp.float32)
    mid = (pose - high).astype(jnp.bfloat16).astype(jnp.float32)
    low = pose - high - mid
    tail = jnp.where(sublane == 0, high, jnp.where(sublane == 1, mid, jnp.where(sublane == 2, low, 0.0)))
    tail = jnp.concatenate([tail, jnp.zeros((SUB, LANES), jnp.float32)], axis=0)
    out_ref[share:, :] = tail.astype(jnp.bfloat16)
    copy.wait()


def pack(poses, fmap, share):
    return pl.pallas_call(
        pack_kernel,
        out_shape=jax.ShapeDtypeStruct((share + 16, fmap.shape[2]), jnp.bfloat16),
        in_specs=[pl.BlockSpec(memory_space=pltpu.VMEM), pl.BlockSpec(memory_space=pl.ANY)],
        out_specs=pl.BlockSpec(memory_space=pltpu.VMEM),
        scratch_shapes=[pltpu.SemaphoreType.DMA],
        name="pack",
    )(poses, fmap)


def pick_kernel(size, ways, *refs):
    asked, blocks, outs = refs[:ways], refs[ways : ways + size], refs[ways + size : 2 * ways + size]
    rel_ref, place_ref, lift_ref, spread_ref, table, tails, held, into, back, tail_sems = refs[2 * ways + size :]
    share = held.shape[1]
    group, edge_slot = lax.axis_index("frames"), lax.axis_index("edges")
    here = ring_place(group, size)
    far = [lax.rem(ring_place(a[0], size) - here + size, size) for a in asked]
    for s in list(range(1, ways)) + [0]:
        for d in range(size):

            @pl.when(far[s] == d)
            def _(s=s, d=d):
                pltpu.make_async_copy(blocks[d].at[pl.ds(0, share), :], held.at[s], into.at[s]).start()

    for d in range(size):
        pltpu.make_async_copy(blocks[d].at[pl.ds(share, 16), :], tails.at[d], tail_sems.at[d]).start()

    unknowns, width = lift_ref.shape[0], place_ref.shape[1]
    rows = POSE * SUB
    sublane = lax.broadcasted_iota(jnp.int32, (SUB, LANES), 0)
    lane = lax.broadcasted_iota(jnp.int32, (SUB, LANES), 1)
    wide_sub = lax.broadcasted_iota(jnp.int32, (SUB, width), 0)
    wide_lane = lax.broadcasted_iota(jnp.int32, (SUB, width), 1)
    place = [jnp.zeros((SUB, width), jnp.float32) for _ in range(POSE)]
    lift = [jnp.zeros((SUB, LANES), jnp.float32) for _ in range(unknowns // SUB)]
    for slot in range(ways):
        edge, target = peer(edge_slot, slot, ways), asked[slot][0]
        for c in range(POSE):
            at_target = (wide_lane == c * size + target).astype(jnp.float32)
            at_source = (wide_lane == c * size + group).astype(jnp.float32)
            place[c] = jnp.where(wide_sub == edge, at_target - at_source, place[c])
        for g in range(unknowns // SUB):
            c, n = divmod(g * SUB, size)
            frame = sublane + n
            hit = (frame == target).astype(jnp.float32) - (frame == group).astype(jnp.float32)
            lift[g] = jnp.where(lane == c * SUB + edge, hit, lift[g])
    for c in range(POSE):
        place_ref[c * SUB : (c + 1) * SUB, :] = place[c]
        spread_ref[c * SUB : (c + 1) * SUB, :] = place[c]
    spread_ref[rows : rows + SUB, :] = ((wide_lane == unknowns) & (wide_sub == 0)).astype(jnp.float32)
    spread_ref[rows + SUB :, :] = jnp.zeros((LANES - rows - SUB, width), jnp.float32)
    for g in range(unknowns // SUB):
        lift_ref[g * SUB : (g + 1) * SUB, :] = lift[g]

    for s in list(range(1, ways)) + [0]:
        pltpu.make_async_copy(blocks[0].at[pl.ds(0, share), :], held.at[s], into.at[s]).wait()
        pltpu.make_async_copy(held.at[s], outs[s], back.at[s]).start()
    for d in range(size):
        pltpu.make_async_copy(blocks[d].at[pl.ds(share, 16), :], tails.at[d], tail_sems.at[d]).wait()
    for d in range(size):
        terms = tails[d].astype(jnp.float32)
        table[d : d + 1, :] = terms[0:1, :] + terms[1:2, :] + terms[2:3, :]
    apart = jnp.zeros((SUB, LANES), jnp.float32)
    for slot in range(ways):
        apart = jnp.where(
            sublane == peer(edge_slot, slot, ways), table[pl.ds(far[slot], 1), :] - table[0:1, :], apart
        )
    for c in range(POSE):
        rel_ref[c * SUB : (c + 1) * SUB, :] = jnp.broadcast_to(apart[:, c : c + 1], (SUB, LANES))
    for s in range(ways):
        pltpu.make_async_copy(held.at[s], outs[s], back.at[s]).wait()


def pick(asked, blocks, width):
    ways, size = len(asked), len(blocks)
    share, channels = blocks[0].shape[0] - 16, blocks[0].shape[1]
    vmem = pl.BlockSpec(memory_space=pltpu.VMEM)
    hbm = pl.BlockSpec(memory_space=pl.ANY)
    f32 = lambda *shape: jax.ShapeDtypeStruct(shape, jnp.float32)
    rows, unknowns = POSE * SUB, POSE * size
    out = pl.pallas_call(
        lambda *refs: pick_kernel(size, ways, *refs),
        out_shape=[jax.ShapeDtypeStruct((share, channels), jnp.bfloat16)] * ways
        + [f32(rows, LANES), f32(rows, width), f32(unknowns, LANES), f32(LANES, width)],
        in_specs=[pl.BlockSpec(memory_space=pltpu.SMEM)] * ways + [hbm] * size,
        out_specs=[hbm] * ways + [vmem] * 4,
        scratch_shapes=[
            pltpu.VMEM((-(-size // SUB) * SUB, channels), jnp.float32),
            pltpu.VMEM((size, 16, channels), jnp.bfloat16),
            pltpu.VMEM((ways, share, channels), jnp.bfloat16),
            pltpu.SemaphoreType.DMA((ways,)),
            pltpu.SemaphoreType.DMA((ways,)),
            pltpu.SemaphoreType.DMA((size,)),
        ],
        compiler_params=pltpu.CompilerParams(vmem_limit_bytes=8 << 20),
        name="pick",
    )(*asked, *blocks)
    return out[:ways], out[ways:]


def gauss_newton_terms(heads, depth_ref, rel, lift_ref, spread_ref, gram_ref, damp_ref, total_ref):
    pixels = depth_ref.shape[1]
    rows = POSE * SUB
    sublane = lax.broadcasted_iota(jnp.int32, (SUB, LANES), 0)
    lane = lax.broadcasted_iota(jnp.int32, (SUB, LANES), 1)
    col_pos = (lane % WID).astype(jnp.float32)
    lane_row = lane // WID
    center_x = (WID - 1) / 2.0
    center_y = (HGT - 1) / 2.0
    ray_x = (col_pos - center_x) / focal
    move_x, move_y, move_z, turn_x, turn_y, turn_z = rel
    pairs_u = [(a, b) for a in (0, 2, 3, 4, 5) for b in (0, 2, 3, 4, 5) if a <= b]
    pairs_v = [(a, b) for a in (1, 2, 3, 4, 5) for b in (1, 2, 3, 4, 5) if a <= b]
    keys = sorted(set(pairs_u) | set(pairs_v))

    def chunk(index, carry):
        hess, grad = dict(zip(keys, carry[0])), list(carry[1])
        at = pl.ds(pl.multiple_of(index * LANES, LANES), LANES)
        depth = jnp.broadcast_to(depth_ref[:, at], (SUB, LANES))
        flow_u, flow_v, weight_u, weight_v = [heads[i, :, at] for i in range(4)]
        row_pos = (lane_row + index * (LANES // WID)).astype(jnp.float32)
        ray_y = (row_pos - center_y) / focal
        point_x = ray_x + turn_y - turn_z * ray_y + depth * move_x
        point_y = ray_y + turn_z * ray_x - turn_x + depth * move_y
        point_z = 1.0 + turn_x * ray_y - turn_y * ray_x + depth * move_z
        inverse_z = 1.0 / point_z
        slope = focal * inverse_z
        shift_u = slope * point_x
        shift_v = slope * point_y
        bend_u = -shift_u * inverse_z
        bend_v = -shift_v * inverse_z
        resid_u = col_pos + flow_u - (shift_u + center_x)
        resid_v = row_pos + flow_v - (shift_v + center_y)
        jac_u = [depth * slope, None, depth * bend_u, bend_u * ray_y, slope - bend_u * ray_x, -slope * ray_y]
        jac_v = [None, jac_u[0], depth * bend_v, bend_v * ray_y - slope, -bend_v * ray_x, slope * ray_x]
        depth_u = slope * move_x + bend_u * move_z
        depth_v = slope * move_y + bend_v * move_z
        scaled_u = [None if j is None else weight_u * j for j in jac_u]
        scaled_v = [None if j is None else weight_v * j for j in jac_v]
        for a, b in pairs_u:
            hess[a, b] = hess[a, b] + scaled_u[a] * jac_u[b]
        for a, b in pairs_v:
            hess[a, b] = hess[a, b] + scaled_v[a] * jac_v[b]
        for c in range(POSE):
            cross = None
            for scaled, resid, along in ((scaled_u, resid_u, depth_u), (scaled_v, resid_v, depth_v)):
                if scaled[c] is not None:
                    grad[c] = grad[c] + scaled[c] * resid
                    term = scaled[c] * along
                    cross = term if cross is None else cross + term
            gram_ref[c * SUB : (c + 1) * SUB, at] = cross
        pull_u = weight_u * depth_u
        pull_v = weight_v * depth_v
        curve = jnp.sum(pull_u * depth_u + pull_v * depth_v, axis=0, keepdims=True)
        slide = jnp.sum(pull_u * resid_u + pull_v * resid_v, axis=0, keepdims=True)
        gram_ref[rows : rows + SUB, at] = jnp.where(sublane == 0, slide, 0.0)
        damp_ref[:, at] = (1.0 + depth_damping) * curve + depth_floor
        return tuple(hess[k] for k in keys), tuple(grad)

    zero = jnp.zeros((SUB, LANES), jnp.float32)
    hess, grad = lax.fori_loop(
        0, pixels // LANES, chunk, (tuple(zero for _ in keys), tuple(zero for _ in range(POSE))), unroll=2
    )
    table = {k: jnp.sum(h, axis=1, keepdims=True) for k, h in zip(keys, hess)}
    slabs = []
    for c in range(POSE):
        slab = jnp.where(lane == rows, jnp.sum(grad[c], axis=1, keepdims=True), 0.0)
        for other in range(POSE):
            key = (min(c, other), max(c, other))
            if key in table:
                slab = jnp.where(lane == sublane + other * SUB, table[key], slab)
        slabs.append(slab)
    local = jnp.concatenate(slabs, axis=0)
    gram = gram_ref[...]
    scaled = gram[0:rows, :] / damp_ref[...]
    schur = nt_dot(scaled, gram, precision=highest)
    schur = jnp.concatenate([schur, jnp.zeros((rows, LANES - rows - SUB), jnp.float32)], axis=1)
    lifted = nn_dot(lift_ref[:, :rows], local - schur, precision=highest)
    total_ref[...] = nn_dot(lifted, spread_ref[...], precision=highest)


def solve_step(parts, unknowns):
    system = parts[0][...]
    for part in parts[1:]:
        system = system + part[...]
    width = system.shape[1]
    lane = lax.broadcasted_iota(jnp.int32, (SUB, width), 1)
    sublane = lax.broadcasted_iota(jnp.int32, (SUB, width), 0)
    groups = []
    for g in range(unknowns // SUB):
        block = system[g * SUB : (g + 1) * SUB, :]
        block = jnp.where(lane == sublane + g * SUB, block * (1.0 + pose_damping) + pose_floor, block)
        groups.append(block)
    for k in range(0, unknowns, PIVOTS):
        g, s = divmod(k, SUB)
        columns = [[jnp.broadcast_to(b[:, k + j : k + j + 1], b.shape) for b in groups] for j in range(PIVOTS)]
        tops = [groups[g][s + i : s + i + 1, :] for i in range(PIVOTS)]
        mult = [[columns[j][g][s + i : s + i + 1, :] for j in range(PIVOTS)] for i in range(PIVOTS)]
        for p in range(PIVOTS):
            inverse = 1.0 / mult[p][p]
            tops[p] = tops[p] * inverse
            for j in range(p + 1, PIVOTS):
                mult[p][j] = mult[p][j] * inverse
            for i in range(PIVOTS):
                if i != p:
                    tops[i] = tops[i] - mult[i][p] * tops[p]
                    for j in range(p + 1, PIVOTS):
                        mult[i][j] = mult[i][j] - mult[i][p] * mult[p][j]
        wide = [jnp.broadcast_to(t, groups[0].shape) for t in tops]
        for i in range(len(groups)):
            update = groups[i]
            for j in range(PIVOTS):
                update = update - columns[j][i] * wide[j]
            if i == g:
                for j in range(PIVOTS):
                    update = jnp.where(sublane == s + j, wide[j], update)
            groups[i] = update
    return jnp.concatenate([jnp.broadcast_to(b[:, unknowns : unknowns + 1], (SUB, LANES)) for b in groups], axis=0)


def split_rel(rel_ref):
    return [rel_ref[c * SUB : (c + 1) * SUB, :] for c in range(POSE)]


def first_kernel(ways, *refs):
    slots, refs = refs[:ways], refs[ways:]
    depth_ref, rel_ref, lift_ref, spread_ref, heads, gram_ref, damp_ref, total_ref = refs
    edge_slot = lax.axis_index("edges")
    if ways < SUB:
        heads[...] = jnp.zeros(heads.shape, jnp.float32)
    for slot in range(ways):
        edge = peer(edge_slot, slot, ways)
        for i in range(4):
            value = slots[slot][i : i + 1, :]
            if i >= 2:
                value = jax.nn.sigmoid(value)
            heads[i, pl.ds(edge, 1), :] = value
    gauss_newton_terms(heads, depth_ref, split_rel(rel_ref), lift_ref, spread_ref, gram_ref, damp_ref, total_ref)


def take_step(parts, place_ref, gram_ref, damp_ref, depth_ref, out_depth_ref):
    unknowns = parts[0].shape[0]
    step = solve_step(parts, unknowns)
    edge_step = nn_dot(place_ref[:, :unknowns], step, precision=highest)
    slices = [edge_step[c * SUB : (c + 1) * SUB, :] for c in range(POSE)]
    rows = POSE * SUB

    def chunk(index, carry):
        at = pl.ds(pl.multiple_of(index * LANES, LANES), LANES)
        total = slices[0] * gram_ref[0:SUB, at]
        for c in range(1, POSE):
            total = total + slices[c] * gram_ref[c * SUB : (c + 1) * SUB, at]
        along = jnp.sum(total, axis=0, keepdims=True)
        out_depth_ref[:, at] = depth_ref[:, at] + (gram_ref[rows : rows + 1, at] - along) / damp_ref[:, at]
        return carry

    lax.fori_loop(0, depth_ref.shape[1] // LANES, chunk, 0, unroll=4)
    return step, edge_step


def middle_kernel(count, *refs):
    parts, refs = refs[:count], refs[count:]
    (heads, gram_ref, damp_ref, depth_ref, rel_ref, place_ref, lift_ref, spread_ref,
     out_gram, out_damp, out_total, out_depth, out_step, out_rel) = refs
    step, edge_step = take_step(parts, place_ref, gram_ref, damp_ref, depth_ref, out_depth)
    out_step[...] = step
    out_rel[...] = rel_ref[...] + edge_step
    gauss_newton_terms(heads, out_depth, split_rel(out_rel), lift_ref, spread_ref, out_gram, out_damp, out_total)


def last_kernel(count, *refs):
    own_ref, parts, refs = refs[0], refs[1 : count + 1], refs[count + 1 :]
    before, refs = refs[: ITERS - 1], refs[ITERS - 1 :]
    gram_ref, damp_ref, depth_ref, place_ref, out_depth, out_pose, held = refs
    step, _ = take_step(parts, place_ref, gram_ref, damp_ref, depth_ref, out_depth)
    for other in before:
        step = step + other[...]
    held[...] = step
    frames, group = lax.axis_size("frames"), lax.axis_index("frames")
    for c in range(POSE):
        out_pose[c : c + 1, :] = own_ref[c : c + 1, :] + held[pl.ds(c * frames + group, 1), :][:, :1]


def call(kernel, shapes, inputs, name, smem=(), scratch=()):
    vmem = pl.BlockSpec(memory_space=pltpu.VMEM)
    f32 = lambda shape: jax.ShapeDtypeStruct(shape, jnp.float32)
    return pl.pallas_call(
        kernel,
        out_shape=[f32(s) for s in shapes],
        in_specs=[
            pl.BlockSpec(memory_space=pltpu.SMEM if i in smem else pltpu.VMEM) for i in range(len(inputs))
        ],
        out_specs=[vmem] * len(shapes),
        scratch_shapes=[pltpu.VMEM(s, jnp.float32) for s in scratch],
        compiler_params=pltpu.CompilerParams(vmem_limit_bytes=32 << 20),
        name=name,
    )(*inputs)


def sum_over(value, axis):
    size = lax.axis_size(axis)
    if size & (size - 1):
        parts = [value]
        for s in range(1, size):
            parts.append(lax.ppermute(value, axis, [(i, (i + s) % size) for i in range(size)]))
        return parts
    radices, left = [], size
    while left > 1:
        radix = 2 if left in (2, 8, 32) else 4
        radices.append(radix)
        left //= radix
    stride, parts = 1, [value]
    for radix in radices:
        value = sum(parts[1:], parts[0])
        parts = [value]
        for s in range(1, radix):
            parts.append(lax.ppermute(value, axis, [(i, i ^ (s * stride)) for i in range(size)]))
        stride *= radix
    return parts


def peer(index, slot, size):
    return index ^ slot if size & (size - 1) == 0 else (index + slot) % size


def exchange(values, axis):
    size = lax.axis_size(axis)
    out = [values[0]]
    for s in range(1, size):
        if size & (size - 1) == 0:
            pairs = [(i, i ^ s) for i in range(size)]
        else:
            pairs = [((i + s) % size, i) for i in range(size)]
        out.append(lax.ppermute(values[s], axis, pairs))
    return out


def ring_order(size):
    if size % 2:
        return list(range(size))
    return list(range(0, size, 2)) + list(range(size - 1, 0, -2))


def ring_gather(value, axis):
    size = lax.axis_size(axis)
    order = ring_order(size)
    ahead = [(order[(i + 1) % size], order[i]) for i in range(size)]
    behind = [(order[i], order[(i + 1) % size]) for i in range(size)]
    out = [None] * size
    out[0] = value
    up = down = value
    for s in range(1, size // 2 + 1):
        up = lax.ppermute(up, axis, ahead)
        out[s] = up
        if size - s > size // 2:
            down = lax.ppermute(down, axis, behind)
            out[size - s] = down
    return out


def per_device(fmap, context, poses, inv_depth, targets, w_corr, w_gates, w_cand, w_head):
    ways = lax.axis_size("edges")
    frames_total = lax.axis_size("frames")
    pixel_count = fmap.shape[1]
    share = pixel_count // ways
    bf = jnp.bfloat16
    blocks = ring_gather(pack(poses, fmap, share), "frames")
    asked = exchange([targets] * ways, "edges")
    unknowns = POSE * frames_total
    width = -(-(unknowns + 1) // LANES) * LANES
    rows = POSE * SUB
    outgoing, (rel, place, lift, spread) = pick(asked, blocks, width)
    bands = exchange(outgoing, "edges")

    w_place = jnp.dot(jnp.asarray(PLACE, bf), w_corr, preferred_element_type=jnp.float32).astype(bf)
    w_place = jnp.concatenate([w_place[:TOTAL], w_place[TOTAL:]], axis=1)
    source, state, inject = prepare(fmap[0], context[0])
    hidden, heads = edge_update(bands, source, state, inject, w_place, w_gates, w_cand, w_head)
    slots = exchange([heads] * ways, "edges")

    big, line = (rows + SUB, pixel_count), (1, pixel_count)
    heads_all, gram, damp, total = call(
        lambda *refs: first_kernel(ways, *refs),
        [(4, SUB, pixel_count), big, line, (unknowns, width)],
        (*slots, inv_depth, rel, lift, spread),
        "terms",
    )
    depth = inv_depth
    steps = []
    for index in range(ITERS - 1):
        parts = sum_over(total, "frames")
        count = len(parts)
        gram, damp, total, depth, step, rel = call(
            lambda *refs: middle_kernel(count, *refs),
            [big, line, (unknowns, width), line, (unknowns, LANES), (rows, LANES)],
            (*parts, heads_all, gram, damp, depth, rel, place, lift, spread),
            "step",
        )
        steps.append(step)
    parts = sum_over(total, "frames")
    count = len(parts)
    depth, new_poses = call(
        lambda *refs: last_kernel(count, *refs),
        [line, poses.shape],
        (poses, *parts, *steps, gram, damp, depth, place),
        "final",
        scratch=[(unknowns, LANES)],
    )
    return (new_poses, depth, hidden[None])


def solution(mesh):
    return jax.shard_map(
        per_device,
        mesh=mesh,
        in_specs=(
            P("frames", None, None),
            P("frames", None, None),
            P(None, "frames"),
            P("frames", None),
            P(("frames", "edges")),
            P(),
            P(),
            P(),
            P(),
        ),
        out_specs=(P(None, "frames"), P("frames", None), P(("frames", "edges"), None, None)),
        check_vma=False,
    )
```

```python
import math

import numpy as np
import jax
import jax.numpy as jnp
from jax import lax
from jax.experimental import pallas as pl
from jax.experimental.pallas import tpu as pltpu
from jax.sharding import PartitionSpec as P

HGT = 48
WID = 64
LEVELS = 4
RADIUS = 3
ITERS = 2
SPAN = 2 * RADIUS + 1
POSE = 6
LANES = 128
SUB = 8
PIVOTS = 8

focal = 50.0
pose_damping = 0.1
pose_floor = 1.0
depth_damping = 0.1
depth_floor = 1.0
highest = lax.Precision.HIGHEST


PITCH = (64, 32, 16, 16)
WINDOW = tuple(8 * p for p in PITCH)
START = (0, 512, 768, 896)
TOTAL = 1024
PAD_ROWS = (54, 31, 19, 13)


def column_order():
    slot = np.arange(WID)
    return 8 * (7 - slot % 8) + slot // 8


def lookup_tables():
    cols = column_order()
    perm = np.zeros((2 * WID, 2 * WID), np.float32)
    for half in range(2):
        perm[half * WID + np.arange(WID), half * WID + cols] = 1.0
    mask = np.zeros((LEVELS, 2 * WID, LANES), np.float32)
    place = np.zeros((2 * TOTAL, LEVELS * SPAN * SPAN), np.float32)
    for level in range(LEVELS):
        pitch, width = PITCH[level], WID >> level
        per_block = LANES // pitch
        for y in range(8):
            block, first = y // per_block, (y % per_block) * pitch
            for b in range(-RADIUS, RADIUS + 1):
                lane = (first + b) % LANES
                reach = (cols >> level) + b
                ok = ((reach >= 0) & (reach < width)).astype(np.float32)
                mask[level, :, lane] = np.concatenate([ok, ok])
                row = START[level] + block * LANES + lane
                for odd in range(2):
                    a = y - RADIUS - (odd if level == 0 else 0)
                    if -RADIUS <= a <= RADIUS:
                        source = level * SPAN * SPAN + (a + RADIUS) * SPAN + b + RADIUS
                        place[odd * TOTAL + row, source] = 1.0
    pools = []
    for level in range(1, LEVELS):
        step = 1 << level
        pool = np.zeros((PITCH[level], step * WID), np.float32)
        for col in range(WID):
            pool[col // step, np.arange(step) * WID + col] = 1.0 / (step * step)
        pools.append(pool)
    return perm, mask, place, pools


PERM, MASK, PLACE, POOLS = lookup_tables()


def nt_dot(a, b, **kw):
    return lax.dot_general(a, b, (((1,), (1,)), ((), ())), preferred_element_type=jnp.float32, **kw)


def nn_dot(a, b, **kw):
    return lax.dot_general(a, b, (((1,), (0,)), ((), ())), preferred_element_type=jnp.float32, **kw)


def prepare_kernel(src_ref, ctx_ref, perm_ref, out_src, out_state, out_inject):
    width = out_state.shape[1]
    perm = perm_ref[...]

    def pair_loop(index, carry):
        at = pl.ds(pl.multiple_of(index * 2 * WID, 2 * WID), 2 * WID)
        out_src[at, :] = nn_dot(perm, src_ref[at, :]).astype(jnp.bfloat16)
        context = nn_dot(perm, ctx_ref[at, :])
        out_state[at, :] = jnp.tanh(context[:, :width]).astype(jnp.bfloat16)
        out_inject[at, :] = jnp.maximum(context[:, width:], 0.0).astype(jnp.bfloat16)
        return carry

    lax.fori_loop(0, HGT // 2, pair_loop, 0, unroll=4)


def prepare(source, context):
    vmem = pl.BlockSpec(memory_space=pltpu.VMEM)
    pixels, channels = source.shape
    half = context.shape[1] // 2
    return pl.pallas_call(
        prepare_kernel,
        out_shape=[jax.ShapeDtypeStruct((pixels, n), jnp.bfloat16) for n in (channels, half, half)],
        in_specs=[vmem] * 3,
        out_specs=[vmem] * 3,
        compiler_params=pltpu.CompilerParams(vmem_limit_bytes=16 << 20),
        name="prepare",
    )(source, context, jnp.asarray(PERM, jnp.bfloat16))


def edge_kernel(ways, *refs):
    band_refs, refs = refs[: 2 * ways], refs[2 * ways :]
    (src_ref, state_in, inject_ref, w_ref, head_ref, back_ref, mask_ref, pool1_ref, pool2_ref, pool3_ref, gates_hbm,
     cand_hbm, out_ref, heads_ref, pad0, pad1, pad2, pad3, corr_ref, state_ref, motion_ref, reset_ref, update_ref,
     gates_ref, cand_ref, sems) = refs
    copies = [
        pltpu.make_async_copy(gates_hbm, gates_ref, sems.at[0]),
        pltpu.make_async_copy(cand_hbm, cand_ref, sems.at[1]),
    ]
    for copy in copies:
        copy.start()
    width = out_ref.shape[1]
    edge = lax.axis_index("edges")
    half_share = band_refs[0].shape[0]
    scale = 1.0 / math.sqrt(src_ref.shape[1])
    pads = (pad0, pad1, pad2, pad3)
    for level, pad in enumerate(pads):
        lead = RADIUS * PITCH[level]
        body = (HGT >> level) * PITCH[level]
        pad[0:lead] = jnp.zeros((lead, pad.shape[1]), pad.dtype)
        pad[lead + body :] = jnp.zeros((pad.shape[0] - lead - body, pad.shape[1]), pad.dtype)
    for ref in (state_ref, motion_ref, reset_ref):
        ref[0:WID, :] = jnp.zeros((WID, width), ref.dtype)
        ref[(HGT + 1) * WID :, :] = jnp.zeros((WID, width), ref.dtype)
    state_ref[WID : (HGT + 1) * WID, :] = state_in[...]
    for slot in range(ways):
        for half in range(2):
            at = pl.multiple_of((peer(edge, slot, ways) * 2 + half) * half_share + RADIUS * WID, WID)
            pad0[pl.ds(at, half_share), :] = band_refs[half * ways + slot][...]
    for level, pool_ref in ((1, pool1_ref), (2, pool2_ref), (3, pool3_ref)):
        rows = 1 << level
        pool = pool_ref[...]
        for row in range(HGT >> level):
            first = (RADIUS + row * rows) * WID
            pooled = nn_dot(pool, pad0[first : first + rows * WID, :])
            at = (RADIUS + row) * PITCH[level]
            pads[level][at : at + PITCH[level], :] = pooled.astype(jnp.bfloat16)

    tile = 8 * WID
    blocks = HGT // 8
    start = lambda block: block * tile if isinstance(block, int) else pl.multiple_of(block * tile, tile)

    def look_up(block):
        for inner in range(4):
            pair = block * 4 + inner
            first = start(block) + inner * 2 * WID
            source = src_ref[pl.ds(first, 2 * WID), :]
            for level in range(LEVELS):
                shift = max(level - 1, 0)
                base = (pair >> shift) * PITCH[level] * (2 if level == 0 else 1)
                base = base if isinstance(base, int) else pl.multiple_of(base, 16)
                volume = nt_dot(source, pads[level][pl.ds(base, WINDOW[level]), :]) * scale
                keep = mask_ref[level]
                for lanes in range(WINDOW[level] // LANES):
                    part = volume[:, lanes * LANES : (lanes + 1) * LANES]
                    rolled = []
                    for group in range(2 * SUB):
                        turn = (8 >> level) * 7 + ((group % SUB) >> level)
                        rolled.append(
                            pltpu.roll(
                                part[group * SUB : (group + 1) * SUB, :],
                                (LANES - turn) % LANES,
                                1,
                                stride=8 >> level,
                                stride_axis=0,
                            )
                        )
                    value = jnp.concatenate(rolled, axis=0).astype(jnp.bfloat16) * keep
                    at = START[level] + lanes * LANES
                    corr_ref[pl.ds(first, 2 * WID), at : at + LANES] = value

    def encode(block):
        first = start(block)
        both = nn_dot(corr_ref[pl.ds(first, tile), :], w_ref[...])
        both = both.reshape(4, 2, WID, 2 * width)
        encoded = jnp.concatenate([both[:, :1, :, :width], both[:, 1:, :, width:]], axis=1).reshape(tile, width)
        inject = inject_ref[pl.ds(first, tile), :].astype(jnp.float32)
        motion_ref[pl.ds(first + WID, tile), :] = (jnp.maximum(encoded, 0.0) + inject).astype(jnp.bfloat16)

    sub = lax.broadcasted_iota(jnp.int32, (8, SUB, width), 1)

    def convolve(block, left_ref, right_ref, weights, columns):
        first = start(block)
        inputs = []
        for row in range(3):
            at = pl.ds(first + row * WID, tile)
            inputs.append(jnp.concatenate([left_ref[at, :], right_ref[at, :]], axis=1))
        taps = []
        for cols in columns:
            total = None
            for row in range(3):
                mats = [weights(row, col) for col in cols]
                mat = mats[0] if len(mats) == 1 else jnp.concatenate(mats, axis=1)
                part = nn_dot(inputs[row], mat)
                total = part if total is None else total + part
            size = total.shape[1] // len(cols)
            taps += [total[:, i * size : (i + 1) * size] for i in range(len(cols))]
        out = []
        for half in range(taps[0].shape[1] // width):
            left, mid, right = [t[:, half * width : (half + 1) * width].reshape(8, WID, width) for t in taps]
            wrapped = jnp.where(sub == SUB - 1, 0.0, jnp.roll(left[:, WID - SUB :], -1, axis=1))
            before = jnp.concatenate([wrapped, left[:, : WID - SUB]], axis=1)
            wrapped = jnp.where(sub == 0, 0.0, jnp.roll(right[:, :SUB], 1, axis=1))
            after = jnp.concatenate([right[:, SUB:], wrapped], axis=1)
            out.append((mid + before + after).reshape(tile, width))
        return out

    def gates(block):
        first = start(block)
        update, reset = convolve(
            block, state_ref, motion_ref, lambda r, c: gates_ref[r, c], ((0,), (1,), (2,))
        )
        update_ref[pl.ds(first, tile), :] = jax.nn.sigmoid(update)
        state = state_ref[pl.ds(first + WID, tile), :].astype(jnp.float32)
        reset_ref[pl.ds(first + WID, tile), :] = (jax.nn.sigmoid(reset) * state).astype(jnp.bfloat16)

    def candidate(block):
        first = start(block)
        (total,) = convolve(block, reset_ref, motion_ref, lambda r, c: cand_ref[r, c], ((0, 1), (2,)))
        update = update_ref[pl.ds(first, tile), :]
        state = state_ref[pl.ds(first + WID, tile), :].astype(jnp.float32)
        hidden = ((1.0 - update) * state + update * jnp.tanh(total)).astype(jnp.bfloat16)
        for inner in range(4):
            at = inner * 2 * WID
            ordered = nn_dot(back_ref[...], hidden[at : at + 2 * WID, :]).astype(jnp.bfloat16)
            out_ref[pl.ds(first + at, 2 * WID), :] = ordered
            heads_ref[:, pl.ds(first + at, 2 * WID)] = nt_dot(head_ref[...], ordered)

    look_up(0)

    def first_loop(block, carry):
        encode(block - 1)
        look_up(block)
        return carry

    lax.fori_loop(1, blocks, first_loop, 0)
    encode(blocks - 1)
    for copy in copies:
        copy.wait()
    gates(0)
    gates(1)

    def second_loop(block, carry):
        candidate(block - 2)
        gates(block)
        return carry

    lax.fori_loop(2, blocks, second_loop, 0)
    candidate(blocks - 2)
    candidate(blocks - 1)


def edge_update(bands, source, state, inject, w_place, w_gates, w_cand, w_head):
    pixels, channels = source.shape
    width = w_head.shape[0]
    ways = len(bands) // 2
    vmem = pl.BlockSpec(memory_space=pltpu.VMEM)
    hbm = pl.BlockSpec(memory_space=pl.ANY)
    bf, f32 = jnp.bfloat16, jnp.float32
    tables = [jnp.asarray(x, bf) for x in (PERM.T, MASK, *POOLS)]
    return pl.pallas_call(
        lambda *refs: edge_kernel(ways, *refs),
        out_shape=[
            jax.ShapeDtypeStruct((pixels, width), bf),
            jax.ShapeDtypeStruct((w_head.shape[1], pixels), f32),
        ],
        in_specs=[vmem] * (2 * ways + 5 + len(tables)) + [hbm] * 2,
        out_specs=[vmem, vmem],
        scratch_shapes=[pltpu.VMEM((PAD_ROWS[l] * PITCH[l], channels), bf) for l in range(LEVELS)]
        + [pltpu.VMEM((pixels, TOTAL), bf)]
        + [pltpu.VMEM(((HGT + 2) * WID, width), bf)] * 3
        + [
            pltpu.VMEM((pixels, width), f32),
            pltpu.VMEM(w_gates.shape, bf),
            pltpu.VMEM(w_cand.shape, bf),
            pltpu.SemaphoreType.DMA((2,)),
        ],
        compiler_params=pltpu.CompilerParams(vmem_limit_bytes=48 << 20),
        name="edge_update",
    )(*bands, source, state, inject, w_place, w_head.T, *tables, w_gates, w_cand)


def ring_place(frame, size):
    if size % 2:
        return frame
    return jnp.where(frame % 2 == 0, frame // 2, size - (frame + 1) // 2)


def pack_kernel(pose_ref, band_ref, first_ref, second_ref, row_ref, sems):
    half = second_ref.shape[0]
    first = pl.multiple_of(lax.axis_index("edges") * 2 * half, 2 * half)
    copies = [
        pltpu.make_async_copy(
            band_ref.at[0, pl.ds(first + i * half, half), :], ref.at[pl.ds(0, half), :], sems.at[i]
        )
        for i, ref in enumerate((first_ref, second_ref))
    ]
    for copy in copies:
        copy.start()
    sublane = lax.broadcasted_iota(jnp.int32, (SUB, LANES), 0)
    row_ref[...] = jnp.zeros(row_ref.shape, jnp.float32)
    row_ref[0:1, 0:POSE] = pose_ref[...]
    pose = jnp.broadcast_to(row_ref[0:1, :], (SUB, LANES))
    high = pose.astype(jnp.bfloat16).astype(jnp.float32)
    mid = (pose - high).astype(jnp.bfloat16).astype(jnp.float32)
    low = pose - high - mid
    tail = jnp.where(sublane == 0, high, jnp.where(sublane == 1, mid, jnp.where(sublane == 2, low, 0.0)))
    tail = jnp.concatenate([tail, jnp.zeros((SUB, LANES), jnp.float32)], axis=0)
    first_ref[half:, :] = tail.astype(jnp.bfloat16)
    for copy in copies:
        copy.wait()


def pack(pose_row, fmap, share):
    vmem = pl.BlockSpec(memory_space=pltpu.VMEM)
    return pl.pallas_call(
        pack_kernel,
        out_shape=[
            jax.ShapeDtypeStruct((share // 2 + 16, fmap.shape[2]), jnp.bfloat16),
            jax.ShapeDtypeStruct((share // 2, fmap.shape[2]), jnp.bfloat16),
        ],
        in_specs=[vmem, pl.BlockSpec(memory_space=pl.ANY)],
        out_specs=[vmem, vmem],
        scratch_shapes=[pltpu.VMEM((SUB, LANES), jnp.float32), pltpu.SemaphoreType.DMA((2,))],
        name="pack",
    )(pose_row, fmap)


def ring_distances(asked, size):
    here = ring_place(lax.axis_index("frames"), size)
    return [lax.rem(ring_place(a[0], size) - here + size, size) for a in asked]


def pick_kernel(size, ways, *refs):
    asked, blocks, outs = refs[:ways], refs[ways : ways + size], refs[ways + size :]
    far = ring_distances(asked, size)
    for s in range(ways):
        for d in range(size):

            @pl.when(far[s] == d)
            def _(s=s, d=d):
                outs[s][...] = blocks[d][0 : outs[s].shape[0], :]


def pick(asked, blocks, rows):
    ways, size = len(asked), len(blocks)
    vmem = pl.BlockSpec(memory_space=pltpu.VMEM)
    return pl.pallas_call(
        lambda *refs: pick_kernel(size, ways, *refs),
        out_shape=[jax.ShapeDtypeStruct((rows, blocks[0].shape[1]), jnp.bfloat16)] * ways,
        in_specs=[pl.BlockSpec(memory_space=pltpu.SMEM)] * ways + [vmem] * size,
        out_specs=[vmem] * ways,
        compiler_params=pltpu.CompilerParams(vmem_limit_bytes=16 << 20),
        name="pick",
    )(*asked, *blocks)


def index_kernel(size, ways, *refs):
    asked, blocks = refs[:ways], refs[ways : ways + size]
    rel_ref, place_ref, lift_ref, spread_ref, table = refs[ways + size :]
    group, edge_slot = lax.axis_index("frames"), lax.axis_index("edges")
    far = ring_distances(asked, size)
    unknowns, width = lift_ref.shape[0], place_ref.shape[1]
    rows = POSE * SUB
    sublane = lax.broadcasted_iota(jnp.int32, (SUB, LANES), 0)
    lane = lax.broadcasted_iota(jnp.int32, (SUB, LANES), 1)
    wide_sub = lax.broadcasted_iota(jnp.int32, (SUB, width), 0)
    wide_lane = lax.broadcasted_iota(jnp.int32, (SUB, width), 1)
    place = [jnp.zeros((SUB, width), jnp.float32) for _ in range(POSE)]
    lift = [jnp.zeros((SUB, LANES), jnp.float32) for _ in range(unknowns // SUB)]
    for slot in range(ways):
        edge, target = peer(edge_slot, slot, ways), asked[slot][0]
        for c in range(POSE):
            at_target = (wide_lane == c * size + target).astype(jnp.float32)
            at_source = (wide_lane == c * size + group).astype(jnp.float32)
            place[c] = jnp.where(wide_sub == edge, at_target - at_source, place[c])
        for g in range(unknowns // SUB):
            c, n = divmod(g * SUB, size)
            frame = sublane + n
            hit = (frame == target).astype(jnp.float32) - (frame == group).astype(jnp.float32)
            lift[g] = jnp.where(lane == c * SUB + edge, hit, lift[g])
    for c in range(POSE):
        place_ref[c * SUB : (c + 1) * SUB, :] = place[c]
        spread_ref[c * SUB : (c + 1) * SUB, :] = place[c]
    spread_ref[rows : rows + SUB, :] = ((wide_lane == unknowns) & (wide_sub == 0)).astype(jnp.float32)
    spread_ref[rows + SUB :, :] = jnp.zeros((LANES - rows - SUB, width), jnp.float32)
    for g in range(unknowns // SUB):
        lift_ref[g * SUB : (g + 1) * SUB, :] = lift[g]
    for d in range(size):
        terms = blocks[d][blocks[d].shape[0] - 16 :, :].astype(jnp.float32)
        table[d : d + 1, :] = terms[0:1, :] + terms[1:2, :] + terms[2:3, :]
    apart = jnp.zeros((SUB, LANES), jnp.float32)
    for slot in range(ways):
        apart = jnp.where(
            sublane == peer(edge_slot, slot, ways), table[pl.ds(far[slot], 1), :] - table[0:1, :], apart
        )
    for c in range(POSE):
        rel_ref[c * SUB : (c + 1) * SUB, :] = jnp.broadcast_to(apart[:, c : c + 1], (SUB, LANES))


def index_tables(asked, blocks, width):
    ways, size = len(asked), len(blocks)
    rows, unknowns = POSE * SUB, POSE * size
    shapes = [(rows, LANES), (rows, width), (unknowns, LANES), (LANES, width)]
    return call(
        lambda *refs: index_kernel(size, ways, *refs),
        shapes,
        (*asked, *blocks),
        "index",
        smem=range(ways),
        scratch=[(-(-size // SUB) * SUB, LANES)],
    )


def gauss_newton_terms(heads, depth_ref, rel, lift_ref, spread_ref, gram_ref, damp_ref, total_ref):
    pixels = depth_ref.shape[1]
    rows = POSE * SUB
    sublane = lax.broadcasted_iota(jnp.int32, (SUB, LANES), 0)
    lane = lax.broadcasted_iota(jnp.int32, (SUB, LANES), 1)
    col_pos = (lane % WID).astype(jnp.float32)
    lane_row = lane // WID
    center_x = (WID - 1) / 2.0
    center_y = (HGT - 1) / 2.0
    ray_x = (col_pos - center_x) / focal
    move_x, move_y, move_z, turn_x, turn_y, turn_z = rel
    pairs_u = [(a, b) for a in (0, 2, 3, 4, 5) for b in (0, 2, 3, 4, 5) if a <= b]
    pairs_v = [(a, b) for a in (1, 2, 3, 4, 5) for b in (1, 2, 3, 4, 5) if a <= b]
    keys = sorted(set(pairs_u) | set(pairs_v))

    def chunk(index, carry):
        hess, grad = dict(zip(keys, carry[0])), list(carry[1])
        at = pl.ds(pl.multiple_of(index * LANES, LANES), LANES)
        depth = jnp.broadcast_to(depth_ref[:, at], (SUB, LANES))
        flow_u, flow_v, weight_u, weight_v = [heads[i, :, at] for i in range(4)]
        row_pos = (lane_row + index * (LANES // WID)).astype(jnp.float32)
        ray_y = (row_pos - center_y) / focal
        point_x = ray_x + turn_y - turn_z * ray_y + depth * move_x
        point_y = ray_y + turn_z * ray_x - turn_x + depth * move_y
        point_z = 1.0 + turn_x * ray_y - turn_y * ray_x + depth * move_z
        inverse_z = 1.0 / point_z
        slope = focal * inverse_z
        shift_u = slope * point_x
        shift_v = slope * point_y
        bend_u = -shift_u * inverse_z
        bend_v = -shift_v * inverse_z
        resid_u = col_pos + flow_u - (shift_u + center_x)
        resid_v = row_pos + flow_v - (shift_v + center_y)
        jac_u = [depth * slope, None, depth * bend_u, bend_u * ray_y, slope - bend_u * ray_x, -slope * ray_y]
        jac_v = [None, jac_u[0], depth * bend_v, bend_v * ray_y - slope, -bend_v * ray_x, slope * ray_x]
        depth_u = slope * move_x + bend_u * move_z
        depth_v = slope * move_y + bend_v * move_z
        scaled_u = [None if j is None else weight_u * j for j in jac_u]
        scaled_v = [None if j is None else weight_v * j for j in jac_v]
        for a, b in pairs_u:
            hess[a, b] = hess[a, b] + scaled_u[a] * jac_u[b]
        for a, b in pairs_v:
            hess[a, b] = hess[a, b] + scaled_v[a] * jac_v[b]
        for c in range(POSE):
            cross = None
            for scaled, resid, along in ((scaled_u, resid_u, depth_u), (scaled_v, resid_v, depth_v)):
                if scaled[c] is not None:
                    grad[c] = grad[c] + scaled[c] * resid
                    term = scaled[c] * along
                    cross = term if cross is None else cross + term
            gram_ref[c * SUB : (c + 1) * SUB, at] = cross
        pull_u = weight_u * depth_u
        pull_v = weight_v * depth_v
        curve = jnp.sum(pull_u * depth_u + pull_v * depth_v, axis=0, keepdims=True)
        slide = jnp.sum(pull_u * resid_u + pull_v * resid_v, axis=0, keepdims=True)
        gram_ref[rows : rows + SUB, at] = jnp.where(sublane == 0, slide, 0.0)
        damp_ref[:, at] = (1.0 + depth_damping) * curve + depth_floor
        return tuple(hess[k] for k in keys), tuple(grad)

    zero = jnp.zeros((SUB, LANES), jnp.float32)
    hess, grad = lax.fori_loop(
        0, pixels // LANES, chunk, (tuple(zero for _ in keys), tuple(zero for _ in range(POSE))), unroll=2
    )
    table = {k: jnp.sum(h, axis=1, keepdims=True) for k, h in zip(keys, hess)}
    slabs = []
    for c in range(POSE):
        slab = jnp.where(lane == rows, jnp.sum(grad[c], axis=1, keepdims=True), 0.0)
        for other in range(POSE):
            key = (min(c, other), max(c, other))
            if key in table:
                slab = jnp.where(lane == sublane + other * SUB, table[key], slab)
        slabs.append(slab)
    local = jnp.concatenate(slabs, axis=0)
    gram = gram_ref[...]
    scaled = gram[0:rows, :] / damp_ref[...]
    schur = nt_dot(scaled, gram, precision=highest)
    schur = jnp.concatenate([schur, jnp.zeros((rows, LANES - rows - SUB), jnp.float32)], axis=1)
    lifted = nn_dot(lift_ref[:, :rows], local - schur, precision=highest)
    total_ref[...] = nn_dot(lifted, spread_ref[...], precision=highest)


def solve_step(parts, unknowns):
    system = parts[0][...]
    for part in parts[1:]:
        system = system + part[...]
    width = system.shape[1]
    lane = lax.broadcasted_iota(jnp.int32, (SUB, width), 1)
    sublane = lax.broadcasted_iota(jnp.int32, (SUB, width), 0)
    groups = []
    for g in range(unknowns // SUB):
        block = system[g * SUB : (g + 1) * SUB, :]
        block = jnp.where(lane == sublane + g * SUB, block * (1.0 + pose_damping) + pose_floor, block)
        groups.append(block)
    for k in range(0, unknowns, PIVOTS):
        g, s = divmod(k, SUB)
        columns = [[jnp.broadcast_to(b[:, k + j : k + j + 1], b.shape) for b in groups] for j in range(PIVOTS)]
        tops = [groups[g][s + i : s + i + 1, :] for i in range(PIVOTS)]
        mult = [[columns[j][g][s + i : s + i + 1, :] for j in range(PIVOTS)] for i in range(PIVOTS)]
        for p in range(PIVOTS):
            inverse = 1.0 / mult[p][p]
            tops[p] = tops[p] * inverse
            for j in range(p + 1, PIVOTS):
                mult[p][j] = mult[p][j] * inverse
            for i in range(PIVOTS):
                if i != p:
                    tops[i] = tops[i] - mult[i][p] * tops[p]
                    for j in range(p + 1, PIVOTS):
                        mult[i][j] = mult[i][j] - mult[i][p] * mult[p][j]
        wide = [jnp.broadcast_to(t, groups[0].shape) for t in tops]
        for i in range(len(groups)):
            update = groups[i]
            for j in range(PIVOTS):
                update = update - columns[j][i] * wide[j]
            if i == g:
                for j in range(PIVOTS):
                    update = jnp.where(sublane == s + j, wide[j], update)
            groups[i] = update
    return jnp.concatenate([jnp.broadcast_to(b[:, unknowns : unknowns + 1], (SUB, LANES)) for b in groups], axis=0)


def split_rel(rel_ref):
    return [rel_ref[c * SUB : (c + 1) * SUB, :] for c in range(POSE)]


def first_kernel(ways, *refs):
    slots, refs = refs[:ways], refs[ways:]
    depth_ref, rel_ref, lift_ref, spread_ref, heads, gram_ref, damp_ref, total_ref = refs
    edge_slot = lax.axis_index("edges")
    if ways < SUB:
        heads[...] = jnp.zeros(heads.shape, jnp.float32)
    for slot in range(ways):
        edge = peer(edge_slot, slot, ways)
        for i in range(4):
            value = slots[slot][i : i + 1, :]
            if i >= 2:
                value = jax.nn.sigmoid(value)
            heads[i, pl.ds(edge, 1), :] = value
    gauss_newton_terms(heads, depth_ref, split_rel(rel_ref), lift_ref, spread_ref, gram_ref, damp_ref, total_ref)


def take_step(parts, place_ref, gram_ref, damp_ref, depth_ref, out_depth_ref):
    unknowns = parts[0].shape[0]
    step = solve_step(parts, unknowns)
    edge_step = nn_dot(place_ref[:, :unknowns], step, precision=highest)
    slices = [edge_step[c * SUB : (c + 1) * SUB, :] for c in range(POSE)]
    rows = POSE * SUB

    def chunk(index, carry):
        at = pl.ds(pl.multiple_of(index * LANES, LANES), LANES)
        total = slices[0] * gram_ref[0:SUB, at]
        for c in range(1, POSE):
            total = total + slices[c] * gram_ref[c * SUB : (c + 1) * SUB, at]
        along = jnp.sum(total, axis=0, keepdims=True)
        out_depth_ref[:, at] = depth_ref[:, at] + (gram_ref[rows : rows + 1, at] - along) / damp_ref[:, at]
        return carry

    lax.fori_loop(0, depth_ref.shape[1] // LANES, chunk, 0, unroll=4)
    return step, edge_step


def middle_kernel(count, *refs):
    parts, refs = refs[:count], refs[count:]
    (heads, gram_ref, damp_ref, depth_ref, rel_ref, place_ref, lift_ref, spread_ref,
     out_gram, out_damp, out_total, out_depth, out_step, out_rel) = refs
    step, edge_step = take_step(parts, place_ref, gram_ref, damp_ref, depth_ref, out_depth)
    out_step[...] = step
    out_rel[...] = rel_ref[...] + edge_step
    gauss_newton_terms(heads, out_depth, split_rel(out_rel), lift_ref, spread_ref, out_gram, out_damp, out_total)


def last_kernel(count, *refs):
    own_ref, parts, refs = refs[0], refs[1 : count + 1], refs[count + 1 :]
    before, refs = refs[: ITERS - 1], refs[ITERS - 1 :]
    gram_ref, damp_ref, depth_ref, place_ref, out_depth, out_pose, held = refs
    step, _ = take_step(parts, place_ref, gram_ref, damp_ref, depth_ref, out_depth)
    for other in before:
        step = step + other[...]
    held[...] = step
    frames, group = lax.axis_size("frames"), lax.axis_index("frames")
    lane = lax.broadcasted_iota(jnp.int32, (1, LANES), 1)
    moved = jnp.zeros((1, LANES), jnp.float32)
    for c in range(POSE):
        moved = jnp.where(lane == c, held[pl.ds(c * frames + group, 1), :], moved)
    out_pose[...] = own_ref[...] + moved[:, :POSE]


def call(kernel, shapes, inputs, name, smem=(), scratch=()):
    vmem = pl.BlockSpec(memory_space=pltpu.VMEM)
    f32 = lambda shape: jax.ShapeDtypeStruct(shape, jnp.float32)
    return pl.pallas_call(
        kernel,
        out_shape=[f32(s) for s in shapes],
        in_specs=[
            pl.BlockSpec(memory_space=pltpu.SMEM if i in smem else pltpu.VMEM) for i in range(len(inputs))
        ],
        out_specs=[vmem] * len(shapes),
        scratch_shapes=[pltpu.VMEM(s, jnp.float32) for s in scratch],
        compiler_params=pltpu.CompilerParams(vmem_limit_bytes=32 << 20),
        name=name,
    )(*inputs)


def sum_over(value, axis):
    size = lax.axis_size(axis)
    if size & (size - 1):
        parts = [value]
        for s in range(1, size):
            parts.append(lax.ppermute(value, axis, [(i, (i + s) % size) for i in range(size)]))
        return parts
    radices, left = [], size
    while left > 1:
        radix = 4 if left % 4 == 0 else 2
        radices.append(radix)
        left //= radix
    stride, parts = 1, [value]
    for radix in radices:
        value = sum(parts[1:], parts[0])
        parts = [value]
        for s in range(1, radix):
            parts.append(lax.ppermute(value, axis, [(i, i ^ (s * stride)) for i in range(size)]))
        stride *= radix
    return parts


def peer(index, slot, size):
    return index ^ slot if size & (size - 1) == 0 else (index + slot) % size


def exchange(values, axis):
    size = lax.axis_size(axis)
    out = [values[0]]
    for s in range(1, size):
        if size & (size - 1) == 0:
            pairs = [(i, i ^ s) for i in range(size)]
        else:
            pairs = [((i + s) % size, i) for i in range(size)]
        out.append(lax.ppermute(values[s], axis, pairs))
    return out


def ring_order(size):
    if size % 2:
        return list(range(size))
    return list(range(0, size, 2)) + list(range(size - 1, 0, -2))


def ring_gather(values, axis):
    size = lax.axis_size(axis)
    order = ring_order(size)
    ahead = [(order[(i + 1) % size], order[i]) for i in range(size)]
    behind = [(order[i], order[(i + 1) % size]) for i in range(size)]
    out = [[value] + [None] * (size - 1) for value in values]
    up, down = list(values), list(values)
    for s in range(1, size // 2 + 1):
        for i in range(len(values)):
            up[i] = out[i][s] = lax.ppermute(up[i], axis, ahead)
            if size - s > size // 2:
                down[i] = out[i][size - s] = lax.ppermute(down[i], axis, behind)
    return out


def per_device(fmap, context, poses, inv_depth, targets, w_corr, w_gates, w_cand, w_head):
    ways = lax.axis_size("edges")
    frames_total = lax.axis_size("frames")
    pixel_count = fmap.shape[1]
    share = pixel_count // ways
    bf = jnp.bfloat16
    first, second = ring_gather(pack(poses.T, fmap, share), "frames")
    asked = exchange([targets] * ways, "edges")
    unknowns = POSE * frames_total
    width = -(-(unknowns + 1) // LANES) * LANES
    rows = POSE * SUB
    bands = exchange(pick(asked, first, share // 2), "edges")
    bands += exchange(pick(asked, second, share // 2), "edges")
    rel, place, lift, spread = index_tables(asked, first, width)

    w_place = jnp.dot(jnp.asarray(PLACE, bf), w_corr, preferred_element_type=jnp.float32).astype(bf)
    w_place = jnp.concatenate([w_place[:TOTAL], w_place[TOTAL:]], axis=1)
    source, state, inject = prepare(fmap[0], context[0])
    hidden, heads = edge_update(bands, source, state, inject, w_place, w_gates, w_cand, w_head)
    slots = exchange([heads] * ways, "edges")

    big, line = (rows + SUB, pixel_count), (1, pixel_count)
    heads_all, gram, damp, total = call(
        lambda *refs: first_kernel(ways, *refs),
        [(4, SUB, pixel_count), big, line, (unknowns, width)],
        (*slots, inv_depth, rel, lift, spread),
        "terms",
    )
    depth = inv_depth
    steps = []
    for index in range(ITERS - 1):
        parts = sum_over(total, "frames")
        count = len(parts)
        gram, damp, total, depth, step, rel = call(
            lambda *refs: middle_kernel(count, *refs),
            [big, line, (unknowns, width), line, (unknowns, LANES), (rows, LANES)],
            (*parts, heads_all, gram, damp, depth, rel, place, lift, spread),
            "step",
        )
        steps.append(step)
    parts = sum_over(total, "frames")
    count = len(parts)
    depth, new_poses = call(
        lambda *refs: last_kernel(count, *refs),
        [line, (1, POSE)],
        (poses.T, *parts, *steps, gram, damp, depth, place),
        "final",
        scratch=[(unknowns, LANES)],
    )
    return (new_poses.T, depth, hidden[None])


def solution(mesh):
    return jax.shard_map(
        per_device,
        mesh=mesh,
        in_specs=(
            P("frames", None, None),
            P("frames", None, None),
            P(None, "frames"),
            P("frames", None),
            P(("frames", "edges")),
            P(),
            P(),
            P(),
            P(),
        ),
        out_specs=(P(None, "frames"), P("frames", None), P(("frames", "edges"), None, None)),
        check_vma=False,
    )
```

```python
import math

import numpy as np
import jax
import jax.numpy as jnp
from jax import lax
from jax.experimental import pallas as pl
from jax.experimental.pallas import tpu as pltpu
from jax.sharding import PartitionSpec as P

HGT = 48
WID = 64
LEVELS = 4
RADIUS = 3
ITERS = 2
SPAN = 2 * RADIUS + 1
POSE = 6
LANES = 128
SUB = 8
PIVOTS = 8

focal = 50.0
pose_damping = 0.1
pose_floor = 1.0
depth_damping = 0.1
depth_floor = 1.0
highest = lax.Precision.HIGHEST


PITCH = (64, 32, 16, 16)
WINDOW = tuple(8 * p for p in PITCH)
START = (0, 512, 768, 896)
TOTAL = 1024
PAD_ROWS = (54, 31, 19, 13)


def column_order():
    slot = np.arange(WID)
    return 8 * (7 - slot % 8) + slot // 8


def lookup_tables():
    cols = column_order()
    perm = np.zeros((2 * WID, 2 * WID), np.float32)
    for half in range(2):
        perm[half * WID + np.arange(WID), half * WID + cols] = 1.0
    mask = np.zeros((LEVELS, 2 * WID, LANES), np.float32)
    place = np.zeros((2 * TOTAL, LEVELS * SPAN * SPAN), np.float32)
    for level in range(LEVELS):
        pitch, width = PITCH[level], WID >> level
        per_block = LANES // pitch
        for y in range(8):
            block, first = y // per_block, (y % per_block) * pitch
            for b in range(-RADIUS, RADIUS + 1):
                lane = (first + b) % LANES
                reach = (cols >> level) + b
                ok = ((reach >= 0) & (reach < width)).astype(np.float32)
                mask[level, :, lane] = np.concatenate([ok, ok])
                row = START[level] + block * LANES + lane
                for odd in range(2):
                    a = y - RADIUS - (odd if level == 0 else 0)
                    if -RADIUS <= a <= RADIUS:
                        source = level * SPAN * SPAN + (a + RADIUS) * SPAN + b + RADIUS
                        place[odd * TOTAL + row, source] = 1.0
    pools = []
    for level in range(1, LEVELS):
        step = 1 << level
        pool = np.zeros((PITCH[level], step * WID), np.float32)
        for col in range(WID):
            pool[col // step, np.arange(step) * WID + col] = 1.0 / (step * step)
        pools.append(pool)
    return perm, mask, place, pools


PERM, MASK, PLACE, POOLS = lookup_tables()


def nt_dot(a, b, **kw):
    return lax.dot_general(a, b, (((1,), (1,)), ((), ())), preferred_element_type=jnp.float32, **kw)


def nn_dot(a, b, **kw):
    return lax.dot_general(a, b, (((1,), (0,)), ((), ())), preferred_element_type=jnp.float32, **kw)


def prepare_kernel(src_ref, ctx_ref, perm_ref, out_src, out_state, out_inject):
    width = out_state.shape[1]
    perm = perm_ref[...]

    def pair_loop(index, carry):
        at = pl.ds(pl.multiple_of(index * 2 * WID, 2 * WID), 2 * WID)
        out_src[at, :] = nn_dot(perm, src_ref[at, :]).astype(jnp.bfloat16)
        context = nn_dot(perm, ctx_ref[at, :])
        out_state[at, :] = jnp.tanh(context[:, :width]).astype(jnp.bfloat16)
        out_inject[at, :] = jnp.maximum(context[:, width:], 0.0).astype(jnp.bfloat16)
        return carry

    lax.fori_loop(0, HGT // 2, pair_loop, 0, unroll=4)


def prepare(source, context):
    vmem = pl.BlockSpec(memory_space=pltpu.VMEM)
    pixels, channels = source.shape
    half = context.shape[1] // 2
    return pl.pallas_call(
        prepare_kernel,
        out_shape=[jax.ShapeDtypeStruct((pixels, n), jnp.bfloat16) for n in (channels, half, half)],
        in_specs=[vmem] * 3,
        out_specs=[vmem] * 3,
        compiler_params=pltpu.CompilerParams(vmem_limit_bytes=16 << 20),
        name="prepare",
    )(source, context, jnp.asarray(PERM, jnp.bfloat16))


def edge_kernel(ways, *refs):
    band_refs, refs = refs[: 2 * ways], refs[2 * ways :]
    (src_ref, state_in, inject_ref, w_ref, head_ref, back_ref, mask_ref, pool1_ref, pool2_ref, pool3_ref, gates_hbm,
     cand_hbm, out_ref, heads_ref, pad0, pad1, pad2, pad3, corr_ref, state_ref, motion_ref, reset_ref, update_ref,
     gates_ref, cand_ref, sems) = refs
    copies = [
        pltpu.make_async_copy(gates_hbm, gates_ref, sems.at[0]),
        pltpu.make_async_copy(cand_hbm, cand_ref, sems.at[1]),
    ]
    for copy in copies:
        copy.start()
    width = out_ref.shape[1]
    edge = lax.axis_index("edges")
    half_share = band_refs[0].shape[0]
    scale = 1.0 / math.sqrt(src_ref.shape[1])
    pads = (pad0, pad1, pad2, pad3)
    for level, pad in enumerate(pads):
        lead = RADIUS * PITCH[level]
        body = (HGT >> level) * PITCH[level]
        pad[0:lead] = jnp.zeros((lead, pad.shape[1]), pad.dtype)
        pad[lead + body :] = jnp.zeros((pad.shape[0] - lead - body, pad.shape[1]), pad.dtype)
    for ref in (state_ref, motion_ref, reset_ref):
        ref[0:WID, :] = jnp.zeros((WID, width), ref.dtype)
        ref[(HGT + 1) * WID :, :] = jnp.zeros((WID, width), ref.dtype)
    state_ref[WID : (HGT + 1) * WID, :] = state_in[...]
    for slot in range(ways):
        for half in range(2):
            at = pl.multiple_of((peer(edge, slot, ways) * 2 + half) * half_share + RADIUS * WID, WID)
            pad0[pl.ds(at, half_share), :] = band_refs[half * ways + slot][...]
    for level, pool_ref in ((1, pool1_ref), (2, pool2_ref), (3, pool3_ref)):
        rows = 1 << level
        pool = pool_ref[...]
        for row in range(HGT >> level):
            first = (RADIUS + row * rows) * WID
            pooled = nn_dot(pool, pad0[first : first + rows * WID, :])
            at = (RADIUS + row) * PITCH[level]
            pads[level][at : at + PITCH[level], :] = pooled.astype(jnp.bfloat16)

    tile = 8 * WID
    blocks = HGT // 8
    start = lambda block: block * tile if isinstance(block, int) else pl.multiple_of(block * tile, tile)

    def look_up(block):
        for inner in range(4):
            pair = block * 4 + inner
            first = start(block) + inner * 2 * WID
            source = src_ref[pl.ds(first, 2 * WID), :]
            for level in range(LEVELS):
                shift = max(level - 1, 0)
                base = (pair >> shift) * PITCH[level] * (2 if level == 0 else 1)
                base = base if isinstance(base, int) else pl.multiple_of(base, 16)
                volume = nt_dot(source, pads[level][pl.ds(base, WINDOW[level]), :]) * scale
                keep = mask_ref[level]
                for lanes in range(WINDOW[level] // LANES):
                    part = volume[:, lanes * LANES : (lanes + 1) * LANES]
                    rolled = []
                    for group in range(2 * SUB):
                        turn = (8 >> level) * 7 + ((group % SUB) >> level)
                        rolled.append(
                            pltpu.roll(
                                part[group * SUB : (group + 1) * SUB, :],
                                (LANES - turn) % LANES,
                                1,
                                stride=8 >> level,
                                stride_axis=0,
                            )
                        )
                    value = jnp.concatenate(rolled, axis=0).astype(jnp.bfloat16) * keep
                    at = START[level] + lanes * LANES
                    corr_ref[pl.ds(first, 2 * WID), at : at + LANES] = value

    def encode(block):
        first = start(block)
        both = nn_dot(corr_ref[pl.ds(first, tile), :], w_ref[...])
        both = both.reshape(4, 2, WID, 2 * width)
        encoded = jnp.concatenate([both[:, :1, :, :width], both[:, 1:, :, width:]], axis=1).reshape(tile, width)
        inject = inject_ref[pl.ds(first, tile), :].astype(jnp.float32)
        motion_ref[pl.ds(first + WID, tile), :] = (jnp.maximum(encoded, 0.0) + inject).astype(jnp.bfloat16)

    sub = lax.broadcasted_iota(jnp.int32, (8, SUB, width), 1)

    def convolve(block, left_ref, right_ref, weights, columns):
        first = start(block)
        inputs = []
        for row in range(3):
            at = pl.ds(first + row * WID, tile)
            inputs.append(jnp.concatenate([left_ref[at, :], right_ref[at, :]], axis=1))
        taps = []
        for cols in columns:
            total = None
            for row in range(3):
                mats = [weights(row, col) for col in cols]
                mat = mats[0] if len(mats) == 1 else jnp.concatenate(mats, axis=1)
                part = nn_dot(inputs[row], mat)
                total = part if total is None else total + part
            size = total.shape[1] // len(cols)
            taps += [total[:, i * size : (i + 1) * size] for i in range(len(cols))]
        out = []
        for half in range(taps[0].shape[1] // width):
            left, mid, right = [t[:, half * width : (half + 1) * width].reshape(8, WID, width) for t in taps]
            wrapped = jnp.where(sub == SUB - 1, 0.0, jnp.roll(left[:, WID - SUB :], -1, axis=1))
            before = jnp.concatenate([wrapped, left[:, : WID - SUB]], axis=1)
            wrapped = jnp.where(sub == 0, 0.0, jnp.roll(right[:, :SUB], 1, axis=1))
            after = jnp.concatenate([right[:, SUB:], wrapped], axis=1)
            out.append((mid + before + after).reshape(tile, width))
        return out

    def gates(block):
        first = start(block)
        update, reset = convolve(
            block, state_ref, motion_ref, lambda r, c: gates_ref[r, c], ((0,), (1,), (2,))
        )
        update_ref[pl.ds(first, tile), :] = jax.nn.sigmoid(update)
        state = state_ref[pl.ds(first + WID, tile), :].astype(jnp.float32)
        reset_ref[pl.ds(first + WID, tile), :] = (jax.nn.sigmoid(reset) * state).astype(jnp.bfloat16)

    def candidate(block):
        first = start(block)
        (total,) = convolve(block, reset_ref, motion_ref, lambda r, c: cand_ref[r, c], ((0, 1), (2,)))
        update = update_ref[pl.ds(first, tile), :]
        state = state_ref[pl.ds(first + WID, tile), :].astype(jnp.float32)
        hidden = ((1.0 - update) * state + update * jnp.tanh(total)).astype(jnp.bfloat16)
        for inner in range(4):
            at = inner * 2 * WID
            ordered = nn_dot(back_ref[...], hidden[at : at + 2 * WID, :]).astype(jnp.bfloat16)
            out_ref[pl.ds(first + at, 2 * WID), :] = ordered
            heads_ref[:, pl.ds(first + at, 2 * WID)] = nt_dot(head_ref[...], ordered)

    look_up(0)

    def first_loop(block, carry):
        encode(block - 1)
        look_up(block)
        return carry

    lax.fori_loop(1, blocks, first_loop, 0)
    encode(blocks - 1)
    for copy in copies:
        copy.wait()
    def gates_loop(block, carry):
        gates(block)
        return carry

    def candidate_loop(block, carry):
        candidate(block)
        return carry

    lax.fori_loop(0, blocks, gates_loop, 0, unroll=3)
    lax.fori_loop(0, blocks, candidate_loop, 0, unroll=3)


def edge_update(bands, source, state, inject, w_place, w_gates, w_cand, w_head):
    pixels, channels = source.shape
    width = w_head.shape[0]
    ways = len(bands) // 2
    vmem = pl.BlockSpec(memory_space=pltpu.VMEM)
    hbm = pl.BlockSpec(memory_space=pl.ANY)
    bf, f32 = jnp.bfloat16, jnp.float32
    tables = [jnp.asarray(x, bf) for x in (PERM.T, MASK, *POOLS)]
    return pl.pallas_call(
        lambda *refs: edge_kernel(ways, *refs),
        out_shape=[
            jax.ShapeDtypeStruct((pixels, width), bf),
            jax.ShapeDtypeStruct((w_head.shape[1], pixels), f32),
        ],
        in_specs=[vmem] * (2 * ways + 5 + len(tables)) + [hbm] * 2,
        out_specs=[vmem, vmem],
        scratch_shapes=[pltpu.VMEM((PAD_ROWS[l] * PITCH[l], channels), bf) for l in range(LEVELS)]
        + [pltpu.VMEM((pixels, TOTAL), bf)]
        + [pltpu.VMEM(((HGT + 2) * WID, width), bf)] * 3
        + [
            pltpu.VMEM((pixels, width), f32),
            pltpu.VMEM(w_gates.shape, bf),
            pltpu.VMEM(w_cand.shape, bf),
            pltpu.SemaphoreType.DMA((2,)),
        ],
        compiler_params=pltpu.CompilerParams(vmem_limit_bytes=48 << 20),
        name="edge_update",
    )(*bands, source, state, inject, w_place, w_head.T, *tables, w_gates, w_cand)


def ring_place(frame, size):
    if size % 2:
        return frame
    return jnp.where(frame % 2 == 0, frame // 2, size - (frame + 1) // 2)


def pack_kernel(pose_ref, band_ref, first_ref, second_ref, row_ref, sems):
    half = second_ref.shape[0]
    first = pl.multiple_of(lax.axis_index("edges") * 2 * half, 2 * half)
    copies = [
        pltpu.make_async_copy(
            band_ref.at[0, pl.ds(first + i * half, half), :], ref.at[pl.ds(0, half), :], sems.at[i]
        )
        for i, ref in enumerate((first_ref, second_ref))
    ]
    for copy in copies:
        copy.start()
    sublane = lax.broadcasted_iota(jnp.int32, (SUB, LANES), 0)
    row_ref[...] = jnp.zeros(row_ref.shape, jnp.float32)
    row_ref[0:1, 0:POSE] = pose_ref[...]
    pose = jnp.broadcast_to(row_ref[0:1, :], (SUB, LANES))
    high = pose.astype(jnp.bfloat16).astype(jnp.float32)
    mid = (pose - high).astype(jnp.bfloat16).astype(jnp.float32)
    low = pose - high - mid
    tail = jnp.where(sublane == 0, high, jnp.where(sublane == 1, mid, jnp.where(sublane == 2, low, 0.0)))
    tail = jnp.concatenate([tail, jnp.zeros((SUB, LANES), jnp.float32)], axis=0)
    first_ref[half:, :] = tail.astype(jnp.bfloat16)
    for copy in copies:
        copy.wait()


def pack(pose_row, fmap, share):
    vmem = pl.BlockSpec(memory_space=pltpu.VMEM)
    return pl.pallas_call(
        pack_kernel,
        out_shape=[
            jax.ShapeDtypeStruct((share // 2 + 16, fmap.shape[2]), jnp.bfloat16),
            jax.ShapeDtypeStruct((share // 2, fmap.shape[2]), jnp.bfloat16),
        ],
        in_specs=[vmem, pl.BlockSpec(memory_space=pl.ANY)],
        out_specs=[vmem, vmem],
        scratch_shapes=[pltpu.VMEM((SUB, LANES), jnp.float32), pltpu.SemaphoreType.DMA((2,))],
        name="pack",
    )(pose_row, fmap)


def ring_distances(asked, size):
    here = ring_place(lax.axis_index("frames"), size)
    return [lax.rem(ring_place(asked[s], size) - here + size, size) for s in range(asked.shape[0])]


def pick_kernel(size, ways, *refs):
    asked, blocks, outs = refs[0], refs[1 : 1 + size], refs[1 + size :]
    far = ring_distances(asked, size)
    for s in range(ways):
        for d in range(size):

            @pl.when(far[s] == d)
            def _(s=s, d=d):
                outs[s][...] = blocks[d][0 : outs[s].shape[0], :]


def pick(asked, blocks, rows):
    ways, size = asked.shape[0], len(blocks)
    vmem = pl.BlockSpec(memory_space=pltpu.VMEM)
    return pl.pallas_call(
        lambda *refs: pick_kernel(size, ways, *refs),
        out_shape=[jax.ShapeDtypeStruct((rows, blocks[0].shape[1]), jnp.bfloat16)] * ways,
        in_specs=[pl.BlockSpec(memory_space=pltpu.SMEM)] + [vmem] * size,
        out_specs=[vmem] * ways,
        compiler_params=pltpu.CompilerParams(vmem_limit_bytes=16 << 20),
        name="pick",
    )(asked, *blocks)


def index_kernel(size, ways, *refs):
    asked, blocks = refs[0], refs[1 : 1 + size]
    rel_ref, place_ref, lift_ref, spread_ref, table = refs[1 + size :]
    group, edge_slot = lax.axis_index("frames"), lax.axis_index("edges")
    far = ring_distances(asked, size)
    unknowns, width = lift_ref.shape[0], place_ref.shape[1]
    rows = POSE * SUB
    sublane = lax.broadcasted_iota(jnp.int32, (SUB, LANES), 0)
    lane = lax.broadcasted_iota(jnp.int32, (SUB, LANES), 1)
    wide_sub = lax.broadcasted_iota(jnp.int32, (SUB, width), 0)
    wide_lane = lax.broadcasted_iota(jnp.int32, (SUB, width), 1)
    place = [jnp.zeros((SUB, width), jnp.float32) for _ in range(POSE)]
    lift = [jnp.zeros((SUB, LANES), jnp.float32) for _ in range(unknowns // SUB)]
    for slot in range(ways):
        edge, target = peer(edge_slot, slot, ways), asked[slot]
        for c in range(POSE):
            at_target = (wide_lane == c * size + target).astype(jnp.float32)
            at_source = (wide_lane == c * size + group).astype(jnp.float32)
            place[c] = jnp.where(wide_sub == edge, at_target - at_source, place[c])
        for g in range(unknowns // SUB):
            c, n = divmod(g * SUB, size)
            frame = sublane + n
            hit = (frame == target).astype(jnp.float32) - (frame == group).astype(jnp.float32)
            lift[g] = jnp.where(lane == c * SUB + edge, hit, lift[g])
    for c in range(POSE):
        place_ref[c * SUB : (c + 1) * SUB, :] = place[c]
        spread_ref[c * SUB : (c + 1) * SUB, :] = place[c]
    spread_ref[rows : rows + SUB, :] = ((wide_lane == unknowns) & (wide_sub == 0)).astype(jnp.float32)
    spread_ref[rows + SUB :, :] = jnp.zeros((LANES - rows - SUB, width), jnp.float32)
    for g in range(unknowns // SUB):
        lift_ref[g * SUB : (g + 1) * SUB, :] = lift[g]
    for d in range(size):
        terms = blocks[d][blocks[d].shape[0] - 16 :, :].astype(jnp.float32)
        table[d : d + 1, :] = terms[0:1, :] + terms[1:2, :] + terms[2:3, :]
    apart = jnp.zeros((SUB, LANES), jnp.float32)
    for slot in range(ways):
        apart = jnp.where(
            sublane == peer(edge_slot, slot, ways), table[pl.ds(far[slot], 1), :] - table[0:1, :], apart
        )
    for c in range(POSE):
        rel_ref[c * SUB : (c + 1) * SUB, :] = jnp.broadcast_to(apart[:, c : c + 1], (SUB, LANES))


def index_tables(asked, blocks, width):
    ways, size = asked.shape[0], len(blocks)
    rows, unknowns = POSE * SUB, POSE * size
    shapes = [(rows, LANES), (rows, width), (unknowns, LANES), (LANES, width)]
    return call(
        lambda *refs: index_kernel(size, ways, *refs),
        shapes,
        (asked, *blocks),
        "index",
        smem=(0,),
        scratch=[(-(-size // SUB) * SUB, LANES)],
    )


def gauss_newton_terms(heads, depth_ref, rel, lift_ref, spread_ref, gram_ref, damp_ref, total_ref):
    pixels = depth_ref.shape[1]
    rows = POSE * SUB
    sublane = lax.broadcasted_iota(jnp.int32, (SUB, LANES), 0)
    lane = lax.broadcasted_iota(jnp.int32, (SUB, LANES), 1)
    col_pos = (lane % WID).astype(jnp.float32)
    lane_row = lane // WID
    center_x = (WID - 1) / 2.0
    center_y = (HGT - 1) / 2.0
    ray_x = (col_pos - center_x) / focal
    move_x, move_y, move_z, turn_x, turn_y, turn_z = rel
    pairs_u = [(a, b) for a in (0, 2, 3, 4, 5) for b in (0, 2, 3, 4, 5) if a <= b]
    pairs_v = [(a, b) for a in (1, 2, 3, 4, 5) for b in (1, 2, 3, 4, 5) if a <= b]
    keys = sorted(set(pairs_u) | set(pairs_v))

    def chunk(index, carry):
        hess, grad = dict(zip(keys, carry[0])), list(carry[1])
        at = pl.ds(pl.multiple_of(index * LANES, LANES), LANES)
        depth = jnp.broadcast_to(depth_ref[:, at], (SUB, LANES))
        flow_u, flow_v, weight_u, weight_v = [heads[i, :, at] for i in range(4)]
        row_pos = (lane_row + index * (LANES // WID)).astype(jnp.float32)
        ray_y = (row_pos - center_y) / focal
        point_x = ray_x + turn_y - turn_z * ray_y + depth * move_x
        point_y = ray_y + turn_z * ray_x - turn_x + depth * move_y
        point_z = 1.0 + turn_x * ray_y - turn_y * ray_x + depth * move_z
        inverse_z = 1.0 / point_z
        slope = focal * inverse_z
        shift_u = slope * point_x
        shift_v = slope * point_y
        bend_u = -shift_u * inverse_z
        bend_v = -shift_v * inverse_z
        resid_u = col_pos + flow_u - (shift_u + center_x)
        resid_v = row_pos + flow_v - (shift_v + center_y)
        jac_u = [depth * slope, None, depth * bend_u, bend_u * ray_y, slope - bend_u * ray_x, -slope * ray_y]
        jac_v = [None, jac_u[0], depth * bend_v, bend_v * ray_y - slope, -bend_v * ray_x, slope * ray_x]
        depth_u = slope * move_x + bend_u * move_z
        depth_v = slope * move_y + bend_v * move_z
        scaled_u = [None if j is None else weight_u * j for j in jac_u]
        scaled_v = [None if j is None else weight_v * j for j in jac_v]
        for a, b in pairs_u:
            hess[a, b] = hess[a, b] + scaled_u[a] * jac_u[b]
        for a, b in pairs_v:
            hess[a, b] = hess[a, b] + scaled_v[a] * jac_v[b]
        for c in range(POSE):
            cross = None
            for scaled, resid, along in ((scaled_u, resid_u, depth_u), (scaled_v, resid_v, depth_v)):
                if scaled[c] is not None:
                    grad[c] = grad[c] + scaled[c] * resid
                    term = scaled[c] * along
                    cross = term if cross is None else cross + term
            gram_ref[c * SUB : (c + 1) * SUB, at] = cross
        pull_u = weight_u * depth_u
        pull_v = weight_v * depth_v
        curve = jnp.sum(pull_u * depth_u + pull_v * depth_v, axis=0, keepdims=True)
        slide = jnp.sum(pull_u * resid_u + pull_v * resid_v, axis=0, keepdims=True)
        gram_ref[rows : rows + SUB, at] = jnp.where(sublane == 0, slide, 0.0)
        damp_ref[:, at] = (1.0 + depth_damping) * curve + depth_floor
        return tuple(hess[k] for k in keys), tuple(grad)

    zero = jnp.zeros((SUB, LANES), jnp.float32)
    hess, grad = lax.fori_loop(
        0, pixels // LANES, chunk, (tuple(zero for _ in keys), tuple(zero for _ in range(POSE))), unroll=2
    )
    table = {k: jnp.sum(h, axis=1, keepdims=True) for k, h in zip(keys, hess)}
    slabs = []
    for c in range(POSE):
        slab = jnp.where(lane == rows, jnp.sum(grad[c], axis=1, keepdims=True), 0.0)
        for other in range(POSE):
            key = (min(c, other), max(c, other))
            if key in table:
                slab = jnp.where(lane == sublane + other * SUB, table[key], slab)
        slabs.append(slab)
    local = jnp.concatenate(slabs, axis=0)
    gram = gram_ref[...]
    scaled = gram[0:rows, :] / damp_ref[...]
    schur = nt_dot(scaled, gram, precision=highest)
    schur = jnp.concatenate([schur, jnp.zeros((rows, LANES - rows - SUB), jnp.float32)], axis=1)
    lifted = nn_dot(lift_ref[:, :rows], local - schur, precision=highest)
    total_ref[...] = nn_dot(lifted, spread_ref[...], precision=highest)


def solve_step(parts, unknowns):
    system = parts[0][...]
    for part in parts[1:]:
        system = system + part[...]
    width = system.shape[1]
    lane = lax.broadcasted_iota(jnp.int32, (SUB, width), 1)
    sublane = lax.broadcasted_iota(jnp.int32, (SUB, width), 0)
    groups = []
    for g in range(unknowns // SUB):
        block = system[g * SUB : (g + 1) * SUB, :]
        block = jnp.where(lane == sublane + g * SUB, block * (1.0 + pose_damping) + pose_floor, block)
        groups.append(block)
    for k in range(0, unknowns, PIVOTS):
        g, s = divmod(k, SUB)
        columns = [[jnp.broadcast_to(b[:, k + j : k + j + 1], b.shape) for b in groups] for j in range(PIVOTS)]
        tops = [groups[g][s + i : s + i + 1, :] for i in range(PIVOTS)]
        mult = [[columns[j][g][s + i : s + i + 1, :] for j in range(PIVOTS)] for i in range(PIVOTS)]
        for p in range(PIVOTS):
            inverse = 1.0 / mult[p][p]
            tops[p] = tops[p] * inverse
            for j in range(p + 1, PIVOTS):
                mult[p][j] = mult[p][j] * inverse
            for i in range(PIVOTS):
                if i != p:
                    tops[i] = tops[i] - mult[i][p] * tops[p]
                    for j in range(p + 1, PIVOTS):
                        mult[i][j] = mult[i][j] - mult[i][p] * mult[p][j]
        wide = [jnp.broadcast_to(t, groups[0].shape) for t in tops]
        for i in range(len(groups)):
            update = groups[i]
            for j in range(PIVOTS):
                update = update - columns[j][i] * wide[j]
            if i == g:
                for j in range(PIVOTS):
                    update = jnp.where(sublane == s + j, wide[j], update)
            groups[i] = update
    return jnp.concatenate([jnp.broadcast_to(b[:, unknowns : unknowns + 1], (SUB, LANES)) for b in groups], axis=0)


def split_rel(rel_ref):
    return [rel_ref[c * SUB : (c + 1) * SUB, :] for c in range(POSE)]


def first_kernel(ways, *refs):
    slots, refs = refs[:ways], refs[ways:]
    depth_ref, rel_ref, lift_ref, spread_ref, heads, gram_ref, damp_ref, total_ref = refs
    edge_slot = lax.axis_index("edges")
    if ways < SUB:
        heads[...] = jnp.zeros(heads.shape, jnp.float32)
    for slot in range(ways):
        edge = peer(edge_slot, slot, ways)
        for i in range(4):
            value = slots[slot][i : i + 1, :]
            if i >= 2:
                value = jax.nn.sigmoid(value)
            heads[i, pl.ds(edge, 1), :] = value
    gauss_newton_terms(heads, depth_ref, split_rel(rel_ref), lift_ref, spread_ref, gram_ref, damp_ref, total_ref)


def take_step(parts, place_ref, gram_ref, damp_ref, depth_ref, out_depth_ref):
    unknowns = parts[0].shape[0]
    step = solve_step(parts, unknowns)
    edge_step = nn_dot(place_ref[:, :unknowns], step, precision=highest)
    slices = [edge_step[c * SUB : (c + 1) * SUB, :] for c in range(POSE)]
    rows = POSE * SUB

    def chunk(index, carry):
        at = pl.ds(pl.multiple_of(index * LANES, LANES), LANES)
        total = slices[0] * gram_ref[0:SUB, at]
        for c in range(1, POSE):
            total = total + slices[c] * gram_ref[c * SUB : (c + 1) * SUB, at]
        along = jnp.sum(total, axis=0, keepdims=True)
        out_depth_ref[:, at] = depth_ref[:, at] + (gram_ref[rows : rows + 1, at] - along) / damp_ref[:, at]
        return carry

    lax.fori_loop(0, depth_ref.shape[1] // LANES, chunk, 0, unroll=4)
    return step, edge_step


def middle_kernel(count, *refs):
    parts, refs = refs[:count], refs[count:]
    (heads, gram_ref, damp_ref, depth_ref, rel_ref, place_ref, lift_ref, spread_ref,
     out_gram, out_damp, out_total, out_depth, out_step, out_rel) = refs
    step, edge_step = take_step(parts, place_ref, gram_ref, damp_ref, depth_ref, out_depth)
    out_step[...] = step
    out_rel[...] = rel_ref[...] + edge_step
    gauss_newton_terms(heads, out_depth, split_rel(out_rel), lift_ref, spread_ref, out_gram, out_damp, out_total)


def last_kernel(count, *refs):
    own_ref, parts, refs = refs[0], refs[1 : count + 1], refs[count + 1 :]
    before, refs = refs[: ITERS - 1], refs[ITERS - 1 :]
    gram_ref, damp_ref, depth_ref, place_ref, out_depth, out_pose, held = refs
    step, _ = take_step(parts, place_ref, gram_ref, damp_ref, depth_ref, out_depth)
    for other in before:
        step = step + other[...]
    held[...] = step
    frames, group = lax.axis_size("frames"), lax.axis_index("frames")
    lane = lax.broadcasted_iota(jnp.int32, (1, LANES), 1)
    moved = jnp.zeros((1, LANES), jnp.float32)
    for c in range(POSE):
        moved = jnp.where(lane == c, held[pl.ds(c * frames + group, 1), :], moved)
    out_pose[...] = own_ref[...] + moved[:, :POSE]


def call(kernel, shapes, inputs, name, smem=(), scratch=()):
    vmem = pl.BlockSpec(memory_space=pltpu.VMEM)
    f32 = lambda shape: jax.ShapeDtypeStruct(shape, jnp.float32)
    return pl.pallas_call(
        kernel,
        out_shape=[f32(s) for s in shapes],
        in_specs=[
            pl.BlockSpec(memory_space=pltpu.SMEM if i in smem else pltpu.VMEM) for i in range(len(inputs))
        ],
        out_specs=[vmem] * len(shapes),
        scratch_shapes=[pltpu.VMEM(s, jnp.float32) for s in scratch],
        compiler_params=pltpu.CompilerParams(vmem_limit_bytes=32 << 20),
        name=name,
    )(*inputs)


def sum_over(value, axis):
    size = lax.axis_size(axis)
    if size & (size - 1):
        parts = [value]
        for s in range(1, size):
            parts.append(lax.ppermute(value, axis, [(i, (i + s) % size) for i in range(size)]))
        return parts
    radices, left = [], size
    while left > 1:
        radix = 4 if left % 4 == 0 else 2
        radices.append(radix)
        left //= radix
    stride, parts = 1, [value]
    for radix in radices:
        value = sum(parts[1:], parts[0])
        parts = [value]
        for s in range(1, radix):
            parts.append(lax.ppermute(value, axis, [(i, i ^ (s * stride)) for i in range(size)]))
        stride *= radix
    return parts


def peer(index, slot, size):
    return index ^ slot if size & (size - 1) == 0 else (index + slot) % size


def exchange(values, axis):
    size = lax.axis_size(axis)
    out = [values[0]]
    for s in range(1, size):
        if size & (size - 1) == 0:
            pairs = [(i, i ^ s) for i in range(size)]
        else:
            pairs = [((i + s) % size, i) for i in range(size)]
        out.append(lax.ppermute(values[s], axis, pairs))
    return out


def ring_order(size):
    if size % 2:
        return list(range(size))
    return list(range(0, size, 2)) + list(range(size - 1, 0, -2))


def ring_gather(values, axis):
    size = lax.axis_size(axis)
    order = ring_order(size)
    ahead = [(order[(i + 1) % size], order[i]) for i in range(size)]
    behind = [(order[i], order[(i + 1) % size]) for i in range(size)]
    out = [[value] + [None] * (size - 1) for value in values]
    up, down = list(values), list(values)
    for s in range(1, size // 2 + 1):
        for i in range(len(values)):
            if 2 * s < size or i % 2 == 0:
                up[i] = out[i][s] = lax.ppermute(up[i], axis, ahead)
            if size - s > size // 2 or (2 * s == size and i % 2):
                down[i] = out[i][size - s] = lax.ppermute(down[i], axis, behind)
    return out


def per_device(fmap, context, poses, inv_depth, targets, w_corr, w_gates, w_cand, w_head):
    ways = lax.axis_size("edges")
    frames_total = lax.axis_size("frames")
    pixel_count = fmap.shape[1]
    share = pixel_count // ways
    bf = jnp.bfloat16
    first, second = ring_gather(pack(poses.T, fmap, share), "frames")
    late_targets, _ = lax.optimization_barrier((targets, first[min(2, frames_total // 2)]))
    asked = jnp.concatenate(exchange([late_targets] * ways, "edges"))
    unknowns = POSE * frames_total
    width = -(-(unknowns + 1) // LANES) * LANES
    rows = POSE * SUB
    early, late = pick(asked, second, share // 2), pick(asked, first, share // 2)
    bands = exchange(late, "edges") + exchange(early, "edges")
    rel, place, lift, spread = index_tables(asked, first, width)

    own_source, own_context, own_corr, _ = lax.optimization_barrier((fmap[0], context[0], w_corr, early[0]))
    w_place = jnp.dot(jnp.asarray(PLACE, bf), own_corr, preferred_element_type=jnp.float32).astype(bf)
    w_place = jnp.concatenate([w_place[:TOTAL], w_place[TOTAL:]], axis=1)
    source, state, inject = prepare(own_source, own_context)
    hidden, heads = edge_update(bands, source, state, inject, w_place, w_gates, w_cand, w_head)
    slots = exchange([heads] * ways, "edges")

    big, line = (rows + SUB, pixel_count), (1, pixel_count)
    heads_all, gram, damp, total = call(
        lambda *refs: first_kernel(ways, *refs),
        [(4, SUB, pixel_count), big, line, (unknowns, width)],
        (*slots, inv_depth, rel, lift, spread),
        "terms",
    )
    depth = inv_depth
    steps = []
    for index in range(ITERS - 1):
        parts = sum_over(total, "frames")
        count = len(parts)
        gram, damp, total, depth, step, rel = call(
            lambda *refs: middle_kernel(count, *refs),
            [big, line, (unknowns, width), line, (unknowns, LANES), (rows, LANES)],
            (*parts, heads_all, gram, damp, depth, rel, place, lift, spread),
            "step",
        )
        steps.append(step)
    parts = sum_over(total, "frames")
    count = len(parts)
    depth, new_poses = call(
        lambda *refs: last_kernel(count, *refs),
        [line, (1, POSE)],
        (poses.T, *parts, *steps, gram, damp, depth, place),
        "final",
        scratch=[(unknowns, LANES)],
    )
    return (new_poses.T, depth, hidden[None])


def solution(mesh):
    return jax.shard_map(
        per_device,
        mesh=mesh,
        in_specs=(
            P("frames", None, None),
            P("frames", None, None),
            P(None, "frames"),
            P("frames", None),
            P(("frames", "edges")),
            P(),
            P(),
            P(),
            P(),
        ),
        out_specs=(P(None, "frames"), P("frames", None), P(("frames", "edges"), None, None)),
        check_vma=False,
    )
```

```python
import math

import numpy as np
import jax
import jax.numpy as jnp
from jax import lax
from jax.experimental import pallas as pl
from jax.experimental.pallas import tpu as pltpu
from jax.sharding import PartitionSpec as P

HGT = 48
WID = 64
LEVELS = 4
RADIUS = 3
ITERS = 2
SPAN = 2 * RADIUS + 1
POSE = 6
LANES = 128
SUB = 8
PIVOTS = 8

focal = 50.0
pose_damping = 0.1
pose_floor = 1.0
depth_damping = 0.1
depth_floor = 1.0
highest = lax.Precision.HIGHEST


PITCH = (64, 32, 16, 16)
WINDOW = tuple(8 * p for p in PITCH)
START = (0, 512, 768, 896)
TOTAL = 1024
PAD_ROWS = (54, 31, 19, 13)


def column_order():
    slot = np.arange(WID)
    return 8 * (7 - slot % 8) + slot // 8


def lookup_tables():
    cols = column_order()
    perm = np.zeros((2 * WID, 2 * WID), np.float32)
    for half in range(2):
        perm[half * WID + np.arange(WID), half * WID + cols] = 1.0
    mask = np.zeros((LEVELS, 2 * WID, LANES), np.float32)
    place = np.zeros((2 * TOTAL, LEVELS * SPAN * SPAN), np.float32)
    for level in range(LEVELS):
        pitch, width = PITCH[level], WID >> level
        per_block = LANES // pitch
        for y in range(8):
            block, first = y // per_block, (y % per_block) * pitch
            for b in range(-RADIUS, RADIUS + 1):
                lane = (first + b) % LANES
                reach = (cols >> level) + b
                ok = ((reach >= 0) & (reach < width)).astype(np.float32)
                mask[level, :, lane] = np.concatenate([ok, ok])
                row = START[level] + block * LANES + lane
                for odd in range(2):
                    a = y - RADIUS - (odd if level == 0 else 0)
                    if -RADIUS <= a <= RADIUS:
                        source = level * SPAN * SPAN + (a + RADIUS) * SPAN + b + RADIUS
                        place[odd * TOTAL + row, source] = 1.0
    pools = []
    for level in range(1, LEVELS):
        step = 1 << level
        pool = np.zeros((PITCH[level], step * WID), np.float32)
        for col in range(WID):
            pool[col // step, np.arange(step) * WID + col] = 1.0 / (step * step)
        pools.append(pool)
    return perm, mask, place, pools


PERM, MASK, PLACE, POOLS = lookup_tables()


def nt_dot(a, b, **kw):
    return lax.dot_general(a, b, (((1,), (1,)), ((), ())), preferred_element_type=jnp.float32, **kw)


def nn_dot(a, b, **kw):
    return lax.dot_general(a, b, (((1,), (0,)), ((), ())), preferred_element_type=jnp.float32, **kw)


def prepare_kernel(src_ref, ctx_ref, perm_ref, out_src, out_state, out_inject):
    width = out_state.shape[1]
    perm = perm_ref[...]

    def pair_loop(index, carry):
        at = pl.ds(pl.multiple_of(index * 2 * WID, 2 * WID), 2 * WID)
        out_src[at, :] = nn_dot(perm, src_ref[at, :]).astype(jnp.bfloat16)
        context = nn_dot(perm, ctx_ref[at, :])
        out_state[at, :] = jnp.tanh(context[:, :width]).astype(jnp.bfloat16)
        out_inject[at, :] = jnp.maximum(context[:, width:], 0.0).astype(jnp.bfloat16)
        return carry

    lax.fori_loop(0, HGT // 2, pair_loop, 0, unroll=4)


def prepare(source, context):
    vmem = pl.BlockSpec(memory_space=pltpu.VMEM)
    pixels, channels = source.shape
    half = context.shape[1] // 2
    return pl.pallas_call(
        prepare_kernel,
        out_shape=[jax.ShapeDtypeStruct((pixels, n), jnp.bfloat16) for n in (channels, half, half)],
        in_specs=[vmem] * 3,
        out_specs=[vmem] * 3,
        compiler_params=pltpu.CompilerParams(vmem_limit_bytes=16 << 20),
        name="prepare",
    )(source, context, jnp.asarray(PERM, jnp.bfloat16))


def edge_kernel(ways, *refs):
    band_refs, refs = refs[: 2 * ways], refs[2 * ways :]
    (src_ref, state_in, inject_ref, w_ref, head_ref, back_ref, mask_ref, pool1_ref, pool2_ref, pool3_ref, gates_hbm,
     cand_hbm, out_ref, heads_ref, pad0, pad1, pad2, pad3, corr_ref, state_ref, motion_ref, reset_ref, update_ref,
     gates_ref, cand_ref, sems) = refs
    copies = [
        pltpu.make_async_copy(gates_hbm, gates_ref, sems.at[0]),
        pltpu.make_async_copy(cand_hbm, cand_ref, sems.at[1]),
    ]
    for copy in copies:
        copy.start()
    width = out_ref.shape[1]
    edge = lax.axis_index("edges")
    half_share = band_refs[0].shape[0]
    scale = 1.0 / math.sqrt(src_ref.shape[1])
    pads = (pad0, pad1, pad2, pad3)
    for level, pad in enumerate(pads):
        lead = RADIUS * PITCH[level]
        body = (HGT >> level) * PITCH[level]
        pad[0:lead] = jnp.zeros((lead, pad.shape[1]), pad.dtype)
        pad[lead + body :] = jnp.zeros((pad.shape[0] - lead - body, pad.shape[1]), pad.dtype)
    for ref in (state_ref, motion_ref, reset_ref):
        ref[0:WID, :] = jnp.zeros((WID, width), ref.dtype)
        ref[(HGT + 1) * WID :, :] = jnp.zeros((WID, width), ref.dtype)
    state_ref[WID : (HGT + 1) * WID, :] = state_in[...]
    for slot in range(ways):
        for half in range(2):
            at = pl.multiple_of((peer(edge, slot, ways) * 2 + half) * half_share + RADIUS * WID, WID)
            pad0[pl.ds(at, half_share), :] = band_refs[half * ways + slot][...]
    for level, pool_ref in ((1, pool1_ref), (2, pool2_ref), (3, pool3_ref)):
        rows = 1 << level
        pool = pool_ref[...]
        for row in range(HGT >> level):
            first = (RADIUS + row * rows) * WID
            pooled = nn_dot(pool, pad0[first : first + rows * WID, :])
            at = (RADIUS + row) * PITCH[level]
            pads[level][at : at + PITCH[level], :] = pooled.astype(jnp.bfloat16)

    tile = 8 * WID
    blocks = HGT // 8
    start = lambda block: block * tile if isinstance(block, int) else pl.multiple_of(block * tile, tile)

    def look_up(block):
        for inner in range(4):
            pair = block * 4 + inner
            first = start(block) + inner * 2 * WID
            source = src_ref[pl.ds(first, 2 * WID), :]
            for level in range(LEVELS):
                shift = max(level - 1, 0)
                base = (pair >> shift) * PITCH[level] * (2 if level == 0 else 1)
                base = base if isinstance(base, int) else pl.multiple_of(base, 16)
                volume = nt_dot(source, pads[level][pl.ds(base, WINDOW[level]), :]) * scale
                keep = mask_ref[level]
                for lanes in range(WINDOW[level] // LANES):
                    part = volume[:, lanes * LANES : (lanes + 1) * LANES]
                    rolled = []
                    for group in range(2 * SUB):
                        turn = (8 >> level) * 7 + ((group % SUB) >> level)
                        rolled.append(
                            pltpu.roll(
                                part[group * SUB : (group + 1) * SUB, :],
                                (LANES - turn) % LANES,
                                1,
                                stride=8 >> level,
                                stride_axis=0,
                            )
                        )
                    value = jnp.concatenate(rolled, axis=0).astype(jnp.bfloat16) * keep
                    at = START[level] + lanes * LANES
                    corr_ref[pl.ds(first, 2 * WID), at : at + LANES] = value

    def encode(block):
        first = start(block)
        both = nn_dot(corr_ref[pl.ds(first, tile), :], w_ref[...])
        both = both.reshape(4, 2, WID, 2 * width)
        encoded = jnp.concatenate([both[:, :1, :, :width], both[:, 1:, :, width:]], axis=1).reshape(tile, width)
        inject = inject_ref[pl.ds(first, tile), :].astype(jnp.float32)
        motion_ref[pl.ds(first + WID, tile), :] = (jnp.maximum(encoded, 0.0) + inject).astype(jnp.bfloat16)

    sub = lax.broadcasted_iota(jnp.int32, (8, SUB, width), 1)

    def convolve(block, left_ref, right_ref, weights, columns):
        first = start(block)
        inputs = []
        for row in range(3):
            at = pl.ds(first + row * WID, tile)
            inputs.append(jnp.concatenate([left_ref[at, :], right_ref[at, :]], axis=1))
        taps = []
        for cols in columns:
            total = None
            for row in range(3):
                mats = [weights(row, col) for col in cols]
                mat = mats[0] if len(mats) == 1 else jnp.concatenate(mats, axis=1)
                part = nn_dot(inputs[row], mat)
                total = part if total is None else total + part
            size = total.shape[1] // len(cols)
            taps += [total[:, i * size : (i + 1) * size] for i in range(len(cols))]
        out = []
        for half in range(taps[0].shape[1] // width):
            left, mid, right = [t[:, half * width : (half + 1) * width].reshape(8, WID, width) for t in taps]
            wrapped = jnp.where(sub == SUB - 1, 0.0, jnp.roll(left[:, WID - SUB :], -1, axis=1))
            before = jnp.concatenate([wrapped, left[:, : WID - SUB]], axis=1)
            wrapped = jnp.where(sub == 0, 0.0, jnp.roll(right[:, :SUB], 1, axis=1))
            after = jnp.concatenate([right[:, SUB:], wrapped], axis=1)
            out.append((mid + before + after).reshape(tile, width))
        return out

    def gates(block):
        first = start(block)
        update, reset = convolve(
            block, state_ref, motion_ref, lambda r, c: gates_ref[r, c], ((0,), (1,), (2,))
        )
        update_ref[pl.ds(first, tile), :] = jax.nn.sigmoid(update)
        state = state_ref[pl.ds(first + WID, tile), :].astype(jnp.float32)
        reset_ref[pl.ds(first + WID, tile), :] = (jax.nn.sigmoid(reset) * state).astype(jnp.bfloat16)

    def candidate(block):
        first = start(block)
        (total,) = convolve(block, reset_ref, motion_ref, lambda r, c: cand_ref[r, c], ((0, 1), (2,)))
        update = update_ref[pl.ds(first, tile), :]
        state = state_ref[pl.ds(first + WID, tile), :].astype(jnp.float32)
        hidden = ((1.0 - update) * state + update * jnp.tanh(total)).astype(jnp.bfloat16)
        for inner in range(4):
            at = inner * 2 * WID
            ordered = nn_dot(back_ref[...], hidden[at : at + 2 * WID, :]).astype(jnp.bfloat16)
            out_ref[pl.ds(first + at, 2 * WID), :] = ordered
            heads_ref[:, pl.ds(first + at, 2 * WID)] = nt_dot(head_ref[...], ordered)

    look_up(0)

    def first_loop(block, carry):
        encode(block - 1)
        look_up(block)
        return carry

    lax.fori_loop(1, blocks, first_loop, 0)
    encode(blocks - 1)
    for copy in copies:
        copy.wait()
    def gates_loop(block, carry):
        gates(block)
        return carry

    def candidate_loop(block, carry):
        candidate(block)
        return carry

    lax.fori_loop(0, blocks, gates_loop, 0, unroll=3)
    lax.fori_loop(0, blocks, candidate_loop, 0, unroll=3)


def edge_update(bands, source, state, inject, w_place, w_gates, w_cand, w_head):
    pixels, channels = source.shape
    width = w_head.shape[0]
    ways = len(bands) // 2
    vmem = pl.BlockSpec(memory_space=pltpu.VMEM)
    hbm = pl.BlockSpec(memory_space=pl.ANY)
    bf, f32 = jnp.bfloat16, jnp.float32
    tables = [jnp.asarray(x, bf) for x in (PERM.T, MASK, *POOLS)]
    return pl.pallas_call(
        lambda *refs: edge_kernel(ways, *refs),
        out_shape=[
            jax.ShapeDtypeStruct((pixels, width), bf),
            jax.ShapeDtypeStruct((w_head.shape[1], pixels), f32),
        ],
        in_specs=[vmem] * (2 * ways + 5 + len(tables)) + [hbm] * 2,
        out_specs=[vmem, vmem],
        scratch_shapes=[pltpu.VMEM((PAD_ROWS[l] * PITCH[l], channels), bf) for l in range(LEVELS)]
        + [pltpu.VMEM((pixels, TOTAL), bf)]
        + [pltpu.VMEM(((HGT + 2) * WID, width), bf)] * 3
        + [
            pltpu.VMEM((pixels, width), f32),
            pltpu.VMEM(w_gates.shape, bf),
            pltpu.VMEM(w_cand.shape, bf),
            pltpu.SemaphoreType.DMA((2,)),
        ],
        compiler_params=pltpu.CompilerParams(vmem_limit_bytes=48 << 20),
        name="edge_update",
    )(*bands, source, state, inject, w_place, w_head.T, *tables, w_gates, w_cand)


def ring_place(frame, size):
    if size % 2:
        return frame
    return jnp.where(frame % 2 == 0, frame // 2, size - (frame + 1) // 2)


def ring_place_of(frame, size):
    if size % 2:
        return frame
    half = frame >> 1
    return jnp.where((frame & 1) == 0, half, size - 1 - half)


def pack_kernel(target_ref, pose_ref, band_ref, first_ref, second_ref, asked_ref, row_ref, sems):
    half = second_ref.shape[0]
    first = pl.multiple_of(lax.axis_index("edges") * 2 * half, 2 * half)
    copies = [
        pltpu.make_async_copy(
            band_ref.at[0, pl.ds(first + i * half, half), :], ref.at[pl.ds(0, half), :], sems.at[i]
        )
        for i, ref in enumerate((first_ref, second_ref))
    ]
    for copy in copies:
        copy.start()
    sublane = lax.broadcasted_iota(jnp.int32, (SUB, LANES), 0)
    row_ref[...] = jnp.zeros(row_ref.shape, jnp.float32)
    row_ref[0:1, 0:POSE] = pose_ref[...]
    pose = jnp.broadcast_to(row_ref[0:1, :], (SUB, LANES))
    high = pose.astype(jnp.bfloat16).astype(jnp.float32)
    mid = (pose - high).astype(jnp.bfloat16).astype(jnp.float32)
    low = pose - high - mid
    tail = jnp.where(sublane == 0, high, jnp.where(sublane == 1, mid, jnp.where(sublane == 2, low, 0.0)))
    tail = jnp.concatenate([tail, jnp.zeros((SUB, LANES), jnp.float32)], axis=0)
    first_ref[half:, :] = tail.astype(jnp.bfloat16)
    asked_ref[...] = jnp.full(asked_ref.shape, target_ref[0], jnp.int32)
    for copy in copies:
        copy.wait()


def pack(targets, pose_row, fmap, share):
    vmem = pl.BlockSpec(memory_space=pltpu.VMEM)
    return pl.pallas_call(
        pack_kernel,
        out_shape=[
            jax.ShapeDtypeStruct((share // 2 + 16, fmap.shape[2]), jnp.bfloat16),
            jax.ShapeDtypeStruct((share // 2, fmap.shape[2]), jnp.bfloat16),
            jax.ShapeDtypeStruct((SUB, LANES), jnp.int32),
        ],
        in_specs=[pl.BlockSpec(memory_space=pltpu.SMEM), vmem, pl.BlockSpec(memory_space=pl.ANY)],
        out_specs=[vmem] * 3,
        scratch_shapes=[pltpu.VMEM((SUB, LANES), jnp.float32), pltpu.SemaphoreType.DMA((2,))],
        name="pack",
    )(targets, pose_row, fmap)


def ring_distances(asked, size):
    here = ring_place(lax.axis_index("frames"), size)
    apart = [ring_place_of(a[...], size) - here for a in asked]
    return [jnp.where(d < 0, d + size, d) for d in apart]


def pick_kernel(size, ways, *refs):
    asked, blocks, outs = refs[:ways], refs[ways : ways + size], refs[ways + size :]
    far = ring_distances(asked, size)
    rows = outs[0].shape[0]
    tile = 2 * SUB
    chosen = []
    for s in range(ways):
        ones = [jnp.where(far[s] == d, 1.0, 0.0) for d in range(size)]
        chosen.append([jnp.concatenate([w, w], axis=0).astype(jnp.bfloat16) for w in ones])

    def step(index, carry):
        at = pl.ds(pl.multiple_of(index * tile, tile), tile)
        values = [block[at, :] for block in blocks]
        for s in range(ways):
            total = values[0] * chosen[s][0]
            for d in range(1, size):
                total = total + values[d] * chosen[s][d]
            outs[s][at, :] = total
        return carry

    lax.fori_loop(0, rows // tile, step, 0, unroll=2)


def pick(asked, blocks, rows):
    ways, size = len(asked), len(blocks)
    vmem = pl.BlockSpec(memory_space=pltpu.VMEM)
    return pl.pallas_call(
        lambda *refs: pick_kernel(size, ways, *refs),
        out_shape=[jax.ShapeDtypeStruct((rows, blocks[0].shape[1]), jnp.bfloat16)] * ways,
        in_specs=[vmem] * (ways + size),
        out_specs=[vmem] * ways,
        compiler_params=pltpu.CompilerParams(vmem_limit_bytes=16 << 20),
        name="pick",
    )(*asked, *blocks)


def index_kernel(size, ways, *refs):
    asked, blocks = refs[:ways], refs[ways : ways + size]
    rel_ref, place_ref, lift_ref, spread_ref, table = refs[ways + size :]
    group, edge_slot = lax.axis_index("frames"), lax.axis_index("edges")
    far = ring_distances(asked, size)
    unknowns, width = lift_ref.shape[0], place_ref.shape[1]
    rows = POSE * SUB
    sublane = lax.broadcasted_iota(jnp.int32, (SUB, LANES), 0)
    lane = lax.broadcasted_iota(jnp.int32, (SUB, LANES), 1)
    wide_sub = lax.broadcasted_iota(jnp.int32, (SUB, width), 0)
    wide_lane = lax.broadcasted_iota(jnp.int32, (SUB, width), 1)
    place = [jnp.zeros((SUB, width), jnp.float32) for _ in range(POSE)]
    lift = [jnp.zeros((SUB, LANES), jnp.float32) for _ in range(unknowns // SUB)]
    for slot in range(ways):
        edge, target = peer(edge_slot, slot, ways), asked[slot][...]
        wide = jnp.concatenate([target] * (width // LANES), axis=1)
        for c in range(POSE):
            at_target = (wide_lane == c * size + wide).astype(jnp.float32)
            at_source = (wide_lane == c * size + group).astype(jnp.float32)
            place[c] = jnp.where(wide_sub == edge, at_target - at_source, place[c])
        for g in range(unknowns // SUB):
            c, n = divmod(g * SUB, size)
            frame = sublane + n
            hit = (frame == target).astype(jnp.float32) - (frame == group).astype(jnp.float32)
            lift[g] = jnp.where(lane == c * SUB + edge, hit, lift[g])
    for c in range(POSE):
        place_ref[c * SUB : (c + 1) * SUB, :] = place[c]
        spread_ref[c * SUB : (c + 1) * SUB, :] = place[c]
    spread_ref[rows : rows + SUB, :] = ((wide_lane == unknowns) & (wide_sub == 0)).astype(jnp.float32)
    spread_ref[rows + SUB :, :] = jnp.zeros((LANES - rows - SUB, width), jnp.float32)
    for g in range(unknowns // SUB):
        lift_ref[g * SUB : (g + 1) * SUB, :] = lift[g]
    for d in range(size):
        terms = blocks[d][blocks[d].shape[0] - 16 :, :].astype(jnp.float32)
        table[d : d + 1, :] = terms[0:1, :] + terms[1:2, :] + terms[2:3, :]
    apart = jnp.zeros((SUB, LANES), jnp.float32)
    for slot in range(ways):
        pose = jnp.zeros((SUB, LANES), jnp.float32)
        for d in range(size):
            pose = jnp.where(far[slot] == d, table[d : d + 1, :], pose)
        apart = jnp.where(sublane == peer(edge_slot, slot, ways), pose - table[0:1, :], apart)
    for c in range(POSE):
        rel_ref[c * SUB : (c + 1) * SUB, :] = jnp.broadcast_to(apart[:, c : c + 1], (SUB, LANES))


def index_tables(asked, blocks, width):
    ways, size = len(asked), len(blocks)
    rows, unknowns = POSE * SUB, POSE * size
    shapes = [(rows, LANES), (rows, width), (unknowns, LANES), (LANES, width)]
    return call(
        lambda *refs: index_kernel(size, ways, *refs),
        shapes,
        (*asked, *blocks),
        "index",
        scratch=[(-(-size // SUB) * SUB, LANES)],
    )


def gauss_newton_terms(heads, depth_ref, rel, lift_ref, spread_ref, gram_ref, damp_ref, total_ref):
    pixels = depth_ref.shape[1]
    rows = POSE * SUB
    sublane = lax.broadcasted_iota(jnp.int32, (SUB, LANES), 0)
    lane = lax.broadcasted_iota(jnp.int32, (SUB, LANES), 1)
    col_pos = (lane % WID).astype(jnp.float32)
    lane_row = lane // WID
    center_x = (WID - 1) / 2.0
    center_y = (HGT - 1) / 2.0
    ray_x = (col_pos - center_x) / focal
    move_x, move_y, move_z, turn_x, turn_y, turn_z = rel
    pairs_u = [(a, b) for a in (0, 2, 3, 4, 5) for b in (0, 2, 3, 4, 5) if a <= b]
    pairs_v = [(a, b) for a in (1, 2, 3, 4, 5) for b in (1, 2, 3, 4, 5) if a <= b]
    keys = sorted(set(pairs_u) | set(pairs_v))

    def chunk(index, carry):
        hess, grad = dict(zip(keys, carry[0])), list(carry[1])
        at = pl.ds(pl.multiple_of(index * LANES, LANES), LANES)
        depth = jnp.broadcast_to(depth_ref[:, at], (SUB, LANES))
        flow_u, flow_v, weight_u, weight_v = [heads[i, :, at] for i in range(4)]
        row_pos = (lane_row + index * (LANES // WID)).astype(jnp.float32)
        ray_y = (row_pos - center_y) / focal
        point_x = ray_x + turn_y - turn_z * ray_y + depth * move_x
        point_y = ray_y + turn_z * ray_x - turn_x + depth * move_y
        point_z = 1.0 + turn_x * ray_y - turn_y * ray_x + depth * move_z
        inverse_z = 1.0 / point_z
        slope = focal * inverse_z
        shift_u = slope * point_x
        shift_v = slope * point_y
        bend_u = -shift_u * inverse_z
        bend_v = -shift_v * inverse_z
        resid_u = col_pos + flow_u - (shift_u + center_x)
        resid_v = row_pos + flow_v - (shift_v + center_y)
        jac_u = [depth * slope, None, depth * bend_u, bend_u * ray_y, slope - bend_u * ray_x, -slope * ray_y]
        jac_v = [None, jac_u[0], depth * bend_v, bend_v * ray_y - slope, -bend_v * ray_x, slope * ray_x]
        depth_u = slope * move_x + bend_u * move_z
        depth_v = slope * move_y + bend_v * move_z
        scaled_u = [None if j is None else weight_u * j for j in jac_u]
        scaled_v = [None if j is None else weight_v * j for j in jac_v]
        for a, b in pairs_u:
            hess[a, b] = hess[a, b] + scaled_u[a] * jac_u[b]
        for a, b in pairs_v:
            hess[a, b] = hess[a, b] + scaled_v[a] * jac_v[b]
        for c in range(POSE):
            cross = None
            for scaled, resid, along in ((scaled_u, resid_u, depth_u), (scaled_v, resid_v, depth_v)):
                if scaled[c] is not None:
                    grad[c] = grad[c] + scaled[c] * resid
                    term = scaled[c] * along
                    cross = term if cross is None else cross + term
            gram_ref[c * SUB : (c + 1) * SUB, at] = cross
        pull_u = weight_u * depth_u
        pull_v = weight_v * depth_v
        curve = jnp.sum(pull_u * depth_u + pull_v * depth_v, axis=0, keepdims=True)
        slide = jnp.sum(pull_u * resid_u + pull_v * resid_v, axis=0, keepdims=True)
        gram_ref[rows : rows + SUB, at] = jnp.where(sublane == 0, slide, 0.0)
        damp_ref[:, at] = (1.0 + depth_damping) * curve + depth_floor
        return tuple(hess[k] for k in keys), tuple(grad)

    zero = jnp.zeros((SUB, LANES), jnp.float32)
    hess, grad = lax.fori_loop(
        0, pixels // LANES, chunk, (tuple(zero for _ in keys), tuple(zero for _ in range(POSE))), unroll=2
    )
    table = {k: jnp.sum(h, axis=1, keepdims=True) for k, h in zip(keys, hess)}
    slabs = []
    for c in range(POSE):
        slab = jnp.where(lane == rows, jnp.sum(grad[c], axis=1, keepdims=True), 0.0)
        for other in range(POSE):
            key = (min(c, other), max(c, other))
            if key in table:
                slab = jnp.where(lane == sublane + other * SUB, table[key], slab)
        slabs.append(slab)
    local = jnp.concatenate(slabs, axis=0)
    gram = gram_ref[...]
    scaled = gram[0:rows, :] / damp_ref[...]
    schur = nt_dot(scaled, gram, precision=highest)
    schur = jnp.concatenate([schur, jnp.zeros((rows, LANES - rows - SUB), jnp.float32)], axis=1)
    lifted = nn_dot(lift_ref[:, :rows], local - schur, precision=highest)
    total_ref[...] = nn_dot(lifted, spread_ref[...], precision=highest)


def solve_step(parts, unknowns):
    system = parts[0][...]
    for part in parts[1:]:
        system = system + part[...]
    width = system.shape[1]
    lane = lax.broadcasted_iota(jnp.int32, (SUB, width), 1)
    sublane = lax.broadcasted_iota(jnp.int32, (SUB, width), 0)
    groups = []
    for g in range(unknowns // SUB):
        block = system[g * SUB : (g + 1) * SUB, :]
        block = jnp.where(lane == sublane + g * SUB, block * (1.0 + pose_damping) + pose_floor, block)
        groups.append(block)
    for k in range(0, unknowns, PIVOTS):
        g, s = divmod(k, SUB)
        columns = [[jnp.broadcast_to(b[:, k + j : k + j + 1], b.shape) for b in groups] for j in range(PIVOTS)]
        tops = [groups[g][s + i : s + i + 1, :] for i in range(PIVOTS)]
        mult = [[columns[j][g][s + i : s + i + 1, :] for j in range(PIVOTS)] for i in range(PIVOTS)]
        for p in range(PIVOTS):
            inverse = 1.0 / mult[p][p]
            tops[p] = tops[p] * inverse
            for j in range(p + 1, PIVOTS):
                mult[p][j] = mult[p][j] * inverse
            for i in range(PIVOTS):
                if i != p:
                    tops[i] = tops[i] - mult[i][p] * tops[p]
                    for j in range(p + 1, PIVOTS):
                        mult[i][j] = mult[i][j] - mult[i][p] * mult[p][j]
        wide = [jnp.broadcast_to(t, groups[0].shape) for t in tops]
        for i in range(len(groups)):
            update = groups[i]
            for j in range(PIVOTS):
                update = update - columns[j][i] * wide[j]
            if i == g:
                for j in range(PIVOTS):
                    update = jnp.where(sublane == s + j, wide[j], update)
            groups[i] = update
    return jnp.concatenate([jnp.broadcast_to(b[:, unknowns : unknowns + 1], (SUB, LANES)) for b in groups], axis=0)


def split_rel(rel_ref):
    return [rel_ref[c * SUB : (c + 1) * SUB, :] for c in range(POSE)]


def first_kernel(ways, *refs):
    slots, refs = refs[:ways], refs[ways:]
    depth_ref, rel_ref, lift_ref, spread_ref, heads, gram_ref, damp_ref, total_ref = refs
    edge_slot = lax.axis_index("edges")
    if ways < SUB:
        heads[...] = jnp.zeros(heads.shape, jnp.float32)
    for slot in range(ways):
        edge = peer(edge_slot, slot, ways)
        for i in range(4):
            value = slots[slot][i : i + 1, :]
            if i >= 2:
                value = jax.nn.sigmoid(value)
            heads[i, pl.ds(edge, 1), :] = value
    gauss_newton_terms(heads, depth_ref, split_rel(rel_ref), lift_ref, spread_ref, gram_ref, damp_ref, total_ref)


def take_step(parts, place_ref, gram_ref, damp_ref, depth_ref, out_depth_ref):
    unknowns = parts[0].shape[0]
    step = solve_step(parts, unknowns)
    edge_step = nn_dot(place_ref[:, :unknowns], step, precision=highest)
    slices = [edge_step[c * SUB : (c + 1) * SUB, :] for c in range(POSE)]
    rows = POSE * SUB

    def chunk(index, carry):
        at = pl.ds(pl.multiple_of(index * LANES, LANES), LANES)
        total = slices[0] * gram_ref[0:SUB, at]
        for c in range(1, POSE):
            total = total + slices[c] * gram_ref[c * SUB : (c + 1) * SUB, at]
        along = jnp.sum(total, axis=0, keepdims=True)
        out_depth_ref[:, at] = depth_ref[:, at] + (gram_ref[rows : rows + 1, at] - along) / damp_ref[:, at]
        return carry

    lax.fori_loop(0, depth_ref.shape[1] // LANES, chunk, 0, unroll=4)
    return step, edge_step


def middle_kernel(count, *refs):
    parts, refs = refs[:count], refs[count:]
    (heads, gram_ref, damp_ref, depth_ref, rel_ref, place_ref, lift_ref, spread_ref,
     out_gram, out_damp, out_total, out_depth, out_step, out_rel) = refs
    step, edge_step = take_step(parts, place_ref, gram_ref, damp_ref, depth_ref, out_depth)
    out_step[...] = step
    out_rel[...] = rel_ref[...] + edge_step
    gauss_newton_terms(heads, out_depth, split_rel(out_rel), lift_ref, spread_ref, out_gram, out_damp, out_total)


def last_kernel(count, *refs):
    own_ref, parts, refs = refs[0], refs[1 : count + 1], refs[count + 1 :]
    before, refs = refs[: ITERS - 1], refs[ITERS - 1 :]
    gram_ref, damp_ref, depth_ref, place_ref, out_depth, out_pose, held = refs
    step, _ = take_step(parts, place_ref, gram_ref, damp_ref, depth_ref, out_depth)
    for other in before:
        step = step + other[...]
    held[...] = step
    frames, group = lax.axis_size("frames"), lax.axis_index("frames")
    lane = lax.broadcasted_iota(jnp.int32, (1, LANES), 1)
    moved = jnp.zeros((1, LANES), jnp.float32)
    for c in range(POSE):
        moved = jnp.where(lane == c, held[pl.ds(c * frames + group, 1), :], moved)
    out_pose[...] = own_ref[...] + moved[:, :POSE]


def call(kernel, shapes, inputs, name, smem=(), scratch=()):
    vmem = pl.BlockSpec(memory_space=pltpu.VMEM)
    f32 = lambda shape: jax.ShapeDtypeStruct(shape, jnp.float32)
    return pl.pallas_call(
        kernel,
        out_shape=[f32(s) for s in shapes],
        in_specs=[
            pl.BlockSpec(memory_space=pltpu.SMEM if i in smem else pltpu.VMEM) for i in range(len(inputs))
        ],
        out_specs=[vmem] * len(shapes),
        scratch_shapes=[pltpu.VMEM(s, jnp.float32) for s in scratch],
        compiler_params=pltpu.CompilerParams(vmem_limit_bytes=32 << 20),
        name=name,
    )(*inputs)


def sum_over(value, axis):
    size = lax.axis_size(axis)
    if size & (size - 1):
        parts = [value]
        for s in range(1, size):
            parts.append(lax.ppermute(value, axis, [(i, (i + s) % size) for i in range(size)]))
        return parts
    radices, left = [], size
    while left > 1:
        radix = 4 if left % 4 == 0 else 2
        radices.append(radix)
        left //= radix
    stride, parts = 1, [value]
    for radix in radices:
        value = sum(parts[1:], parts[0])
        parts = [value]
        for s in range(1, radix):
            parts.append(lax.ppermute(value, axis, [(i, i ^ (s * stride)) for i in range(size)]))
        stride *= radix
    return parts


def peer(index, slot, size):
    return index ^ slot if size & (size - 1) == 0 else (index + slot) % size


def exchange(values, axis):
    size = lax.axis_size(axis)
    out = [values[0]]
    for s in range(1, size):
        if size & (size - 1) == 0:
            pairs = [(i, i ^ s) for i in range(size)]
        else:
            pairs = [((i + s) % size, i) for i in range(size)]
        out.append(lax.ppermute(values[s], axis, pairs))
    return out


def ring_order(size):
    if size % 2:
        return list(range(size))
    return list(range(0, size, 2)) + list(range(size - 1, 0, -2))


def ring_gather(values, axis):
    size = lax.axis_size(axis)
    order = ring_order(size)
    ahead = [(order[(i + 1) % size], order[i]) for i in range(size)]
    behind = [(order[i], order[(i + 1) % size]) for i in range(size)]
    out = [[value] + [None] * (size - 1) for value in values]
    up, down = list(values), list(values)
    for s in range(1, size // 2 + 1):
        for i in range(len(values)):
            if 2 * s < size or i % 2 == 0:
                up[i] = out[i][s] = lax.ppermute(up[i], axis, ahead)
            if size - s > size // 2 or (2 * s == size and i % 2):
                down[i] = out[i][size - s] = lax.ppermute(down[i], axis, behind)
    return out


def per_device(fmap, context, poses, inv_depth, targets, w_corr, w_gates, w_cand, w_head):
    ways = lax.axis_size("edges")
    frames_total = lax.axis_size("frames")
    pixel_count = fmap.shape[1]
    share = pixel_count // ways
    bf = jnp.bfloat16
    first_band, second_band, target = pack(targets, poses.T, fmap, share)
    first, second = ring_gather((first_band, second_band), "frames")
    late_target, _ = lax.optimization_barrier((target, first[min(2, frames_total // 2)]))
    asked = exchange([late_target] * ways, "edges")
    unknowns = POSE * frames_total
    width = -(-(unknowns + 1) // LANES) * LANES
    rows = POSE * SUB
    early, late = pick(asked, second, share // 2), pick(asked, first, share // 2)
    bands = exchange(late, "edges") + exchange(early, "edges")
    rel, place, lift, spread = index_tables(asked, first, width)

    own_source, own_context, own_corr, _ = lax.optimization_barrier((fmap[0], context[0], w_corr, late[0]))
    w_place = jnp.dot(jnp.asarray(PLACE, bf), own_corr, preferred_element_type=jnp.float32).astype(bf)
    w_place = jnp.concatenate([w_place[:TOTAL], w_place[TOTAL:]], axis=1)
    source, state, inject = prepare(own_source, own_context)
    hidden, heads = edge_update(bands, source, state, inject, w_place, w_gates, w_cand, w_head)
    slots = exchange([heads] * ways, "edges")

    big, line = (rows + SUB, pixel_count), (1, pixel_count)
    heads_all, gram, damp, total = call(
        lambda *refs: first_kernel(ways, *refs),
        [(4, SUB, pixel_count), big, line, (unknowns, width)],
        (*slots, inv_depth, rel, lift, spread),
        "terms",
    )
    depth = inv_depth
    steps = []
    for index in range(ITERS - 1):
        parts = sum_over(total, "frames")
        count = len(parts)
        gram, damp, total, depth, step, rel = call(
            lambda *refs: middle_kernel(count, *refs),
            [big, line, (unknowns, width), line, (unknowns, LANES), (rows, LANES)],
            (*parts, heads_all, gram, damp, depth, rel, place, lift, spread),
            "step",
        )
        steps.append(step)
    parts = sum_over(total, "frames")
    count = len(parts)
    depth, new_poses = call(
        lambda *refs: last_kernel(count, *refs),
        [line, (1, POSE)],
        (poses.T, *parts, *steps, gram, damp, depth, place),
        "final",
        scratch=[(unknowns, LANES)],
    )
    return (new_poses.T, depth, hidden[None])


def solution(mesh):
    return jax.shard_map(
        per_device,
        mesh=mesh,
        in_specs=(
            P("frames", None, None),
            P("frames", None, None),
            P(None, "frames"),
            P("frames", None),
            P(("frames", "edges")),
            P(),
            P(),
            P(),
            P(),
        ),
        out_specs=(P(None, "frames"), P("frames", None), P(("frames", "edges"), None, None)),
        check_vma=False,
    )
```

```python
import math

import numpy as np
import jax
import jax.numpy as jnp
from jax import lax
from jax.experimental import pallas as pl
from jax.experimental.pallas import tpu as pltpu
from jax.sharding import PartitionSpec as P

HGT = 48
WID = 64
LEVELS = 4
RADIUS = 3
ITERS = 2
SPAN = 2 * RADIUS + 1
POSE = 6
LANES = 128
SUB = 8
PIVOTS = 8

focal = 50.0
pose_damping = 0.1
pose_floor = 1.0
depth_damping = 0.1
depth_floor = 1.0
highest = lax.Precision.HIGHEST


PITCH = (64, 32, 16, 16)
WINDOW = tuple(8 * p for p in PITCH)
START = (0, 512, 768, 896)
TOTAL = 1024
PAD_ROWS = (54, 31, 19, 13)


def column_order():
    slot = np.arange(WID)
    return 8 * (7 - slot % 8) + slot // 8


def lookup_tables():
    cols = column_order()
    perm = np.zeros((2 * WID, 2 * WID), np.float32)
    for half in range(2):
        perm[half * WID + np.arange(WID), half * WID + cols] = 1.0
    mask = np.zeros((LEVELS, 2 * WID, LANES), np.float32)
    place = np.zeros((2 * TOTAL, LEVELS * SPAN * SPAN), np.float32)
    for level in range(LEVELS):
        pitch, width = PITCH[level], WID >> level
        per_block = LANES // pitch
        for y in range(8):
            block, first = y // per_block, (y % per_block) * pitch
            for b in range(-RADIUS, RADIUS + 1):
                lane = (first + b) % LANES
                reach = (cols >> level) + b
                ok = ((reach >= 0) & (reach < width)).astype(np.float32)
                mask[level, :, lane] = np.concatenate([ok, ok])
                row = START[level] + block * LANES + lane
                for odd in range(2):
                    a = y - RADIUS - (odd if level == 0 else 0)
                    if -RADIUS <= a <= RADIUS:
                        source = level * SPAN * SPAN + (a + RADIUS) * SPAN + b + RADIUS
                        place[odd * TOTAL + row, source] = 1.0
    pools = []
    for level in range(1, LEVELS):
        step = 1 << level
        pool = np.zeros((PITCH[level], step * WID), np.float32)
        for col in range(WID):
            pool[col // step, np.arange(step) * WID + col] = 1.0 / (step * step)
        pools.append(pool)
    return perm, mask, place, pools


PERM, MASK, PLACE, POOLS = lookup_tables()


def nt_dot(a, b, **kw):
    return lax.dot_general(a, b, (((1,), (1,)), ((), ())), preferred_element_type=jnp.float32, **kw)


def nn_dot(a, b, **kw):
    return lax.dot_general(a, b, (((1,), (0,)), ((), ())), preferred_element_type=jnp.float32, **kw)


def prepare_kernel(src_ref, ctx_ref, perm_ref, out_src, out_state, out_inject):
    width = out_state.shape[1]
    perm = perm_ref[...]

    def pair_loop(index, carry):
        at = pl.ds(pl.multiple_of(index * 2 * WID, 2 * WID), 2 * WID)
        out_src[at, :] = nn_dot(perm, src_ref[at, :]).astype(jnp.bfloat16)
        context = nn_dot(perm, ctx_ref[at, :])
        out_state[at, :] = jnp.tanh(context[:, :width]).astype(jnp.bfloat16)
        out_inject[at, :] = jnp.maximum(context[:, width:], 0.0).astype(jnp.bfloat16)
        return carry

    lax.fori_loop(0, HGT // 2, pair_loop, 0, unroll=4)


def prepare(source, context):
    vmem = pl.BlockSpec(memory_space=pltpu.VMEM)
    pixels, channels = source.shape
    half = context.shape[1] // 2
    return pl.pallas_call(
        prepare_kernel,
        out_shape=[jax.ShapeDtypeStruct((pixels, n), jnp.bfloat16) for n in (channels, half, half)],
        in_specs=[vmem] * 3,
        out_specs=[vmem] * 3,
        compiler_params=pltpu.CompilerParams(vmem_limit_bytes=16 << 20),
        name="prepare",
    )(source, context, jnp.asarray(PERM, jnp.bfloat16))


def edge_kernel(ways, *refs):
    band_refs, refs = refs[: 2 * ways], refs[2 * ways :]
    (src_ref, state_in, inject_ref, w_ref, head_ref, back_ref, mask_ref, pool1_ref, pool2_ref, pool3_ref, gates_hbm,
     cand_hbm, out_ref, heads_ref, pad0, pad1, pad2, pad3, corr_ref, state_ref, motion_ref, reset_ref, update_ref,
     gates_ref, cand_ref, sems) = refs
    copies = [
        pltpu.make_async_copy(gates_hbm, gates_ref, sems.at[0]),
        pltpu.make_async_copy(cand_hbm, cand_ref, sems.at[1]),
    ]
    for copy in copies:
        copy.start()
    width = out_ref.shape[1]
    edge = lax.axis_index("edges")
    half_share = band_refs[0].shape[0]
    scale = 1.0 / math.sqrt(src_ref.shape[1])
    pads = (pad0, pad1, pad2, pad3)
    for level, pad in enumerate(pads):
        lead = RADIUS * PITCH[level]
        body = (HGT >> level) * PITCH[level]
        pad[0:lead] = jnp.zeros((lead, pad.shape[1]), pad.dtype)
        pad[lead + body :] = jnp.zeros((pad.shape[0] - lead - body, pad.shape[1]), pad.dtype)
    for ref in (state_ref, motion_ref, reset_ref):
        ref[0:WID, :] = jnp.zeros((WID, width), ref.dtype)
        ref[(HGT + 1) * WID :, :] = jnp.zeros((WID, width), ref.dtype)
    state_ref[WID : (HGT + 1) * WID, :] = state_in[...]
    for slot in range(ways):
        for half in range(2):
            at = pl.multiple_of((peer(edge, slot, ways) * 2 + half) * half_share + RADIUS * WID, WID)
            pad0[pl.ds(at, half_share), :] = band_refs[half * ways + slot][...]
    for level, pool_ref in ((1, pool1_ref), (2, pool2_ref), (3, pool3_ref)):
        rows = 1 << level
        pool = pool_ref[...]
        for row in range(HGT >> level):
            first = (RADIUS + row * rows) * WID
            pooled = nn_dot(pool, pad0[first : first + rows * WID, :])
            at = (RADIUS + row) * PITCH[level]
            pads[level][at : at + PITCH[level], :] = pooled.astype(jnp.bfloat16)

    tile = 8 * WID
    blocks = HGT // 8
    start = lambda block: block * tile if isinstance(block, int) else pl.multiple_of(block * tile, tile)

    def look_up(block):
        for inner in range(4):
            pair = block * 4 + inner
            first = start(block) + inner * 2 * WID
            source = src_ref[pl.ds(first, 2 * WID), :]
            for level in range(LEVELS):
                shift = max(level - 1, 0)
                base = (pair >> shift) * PITCH[level] * (2 if level == 0 else 1)
                base = base if isinstance(base, int) else pl.multiple_of(base, 16)
                volume = nt_dot(source, pads[level][pl.ds(base, WINDOW[level]), :]) * scale
                keep = mask_ref[level]
                for lanes in range(WINDOW[level] // LANES):
                    part = volume[:, lanes * LANES : (lanes + 1) * LANES]
                    rolled = []
                    for group in range(2 * SUB):
                        turn = (8 >> level) * 7 + ((group % SUB) >> level)
                        rolled.append(
                            pltpu.roll(
                                part[group * SUB : (group + 1) * SUB, :],
                                (LANES - turn) % LANES,
                                1,
                                stride=8 >> level,
                                stride_axis=0,
                            )
                        )
                    value = jnp.concatenate(rolled, axis=0).astype(jnp.bfloat16) * keep
                    at = START[level] + lanes * LANES
                    corr_ref[pl.ds(first, 2 * WID), at : at + LANES] = value

    def encode(block):
        first = start(block)
        both = nn_dot(corr_ref[pl.ds(first, tile), :], w_ref[...])
        both = both.reshape(4, 2, WID, 2 * width)
        encoded = jnp.concatenate([both[:, :1, :, :width], both[:, 1:, :, width:]], axis=1).reshape(tile, width)
        inject = inject_ref[pl.ds(first, tile), :].astype(jnp.float32)
        motion_ref[pl.ds(first + WID, tile), :] = (jnp.maximum(encoded, 0.0) + inject).astype(jnp.bfloat16)

    sub = lax.broadcasted_iota(jnp.int32, (8, SUB, width), 1)

    def convolve(block, left_ref, right_ref, weights, columns):
        first = start(block)
        inputs = []
        for row in range(3):
            at = pl.ds(first + row * WID, tile)
            inputs.append(jnp.concatenate([left_ref[at, :], right_ref[at, :]], axis=1))
        taps = []
        for cols in columns:
            total = None
            for row in range(3):
                mats = [weights(row, col) for col in cols]
                mat = mats[0] if len(mats) == 1 else jnp.concatenate(mats, axis=1)
                part = nn_dot(inputs[row], mat)
                total = part if total is None else total + part
            size = total.shape[1] // len(cols)
            taps += [total[:, i * size : (i + 1) * size] for i in range(len(cols))]
        out = []
        for half in range(taps[0].shape[1] // width):
            left, mid, right = [t[:, half * width : (half + 1) * width].reshape(8, WID, width) for t in taps]
            wrapped = jnp.where(sub == SUB - 1, 0.0, jnp.roll(left[:, WID - SUB :], -1, axis=1))
            before = jnp.concatenate([wrapped, left[:, : WID - SUB]], axis=1)
            wrapped = jnp.where(sub == 0, 0.0, jnp.roll(right[:, :SUB], 1, axis=1))
            after = jnp.concatenate([right[:, SUB:], wrapped], axis=1)
            out.append((mid + before + after).reshape(tile, width))
        return out

    def gates(block):
        first = start(block)
        update, reset = convolve(
            block, state_ref, motion_ref, lambda r, c: gates_ref[r, c], ((0,), (1,), (2,))
        )
        update_ref[pl.ds(first, tile), :] = jax.nn.sigmoid(update)
        state = state_ref[pl.ds(first + WID, tile), :].astype(jnp.float32)
        reset_ref[pl.ds(first + WID, tile), :] = (jax.nn.sigmoid(reset) * state).astype(jnp.bfloat16)

    def candidate(block):
        first = start(block)
        (total,) = convolve(block, reset_ref, motion_ref, lambda r, c: cand_ref[r, c], ((0, 1), (2,)))
        update = update_ref[pl.ds(first, tile), :]
        state = state_ref[pl.ds(first + WID, tile), :].astype(jnp.float32)
        hidden = ((1.0 - update) * state + update * jnp.tanh(total)).astype(jnp.bfloat16)
        for inner in range(4):
            at = inner * 2 * WID
            ordered = nn_dot(back_ref[...], hidden[at : at + 2 * WID, :]).astype(jnp.bfloat16)
            out_ref[pl.ds(first + at, 2 * WID), :] = ordered
            heads_ref[:, pl.ds(first + at, 2 * WID)] = nt_dot(head_ref[...], ordered)

    look_up(0)

    def first_loop(block, carry):
        encode(block - 1)
        look_up(block)
        return carry

    lax.fori_loop(1, blocks, first_loop, 0)
    encode(blocks - 1)
    for copy in copies:
        copy.wait()
    def gates_loop(block, carry):
        gates(block)
        return carry

    def candidate_loop(block, carry):
        candidate(block)
        return carry

    lax.fori_loop(0, blocks, gates_loop, 0, unroll=3)
    lax.fori_loop(0, blocks, candidate_loop, 0, unroll=3)


def edge_update(bands, source, state, inject, w_place, w_gates, w_cand, w_head):
    pixels, channels = source.shape
    width = w_head.shape[0]
    ways = len(bands) // 2
    vmem = pl.BlockSpec(memory_space=pltpu.VMEM)
    hbm = pl.BlockSpec(memory_space=pl.ANY)
    bf, f32 = jnp.bfloat16, jnp.float32
    tables = [jnp.asarray(x, bf) for x in (PERM.T, MASK, *POOLS)]
    return pl.pallas_call(
        lambda *refs: edge_kernel(ways, *refs),
        out_shape=[
            jax.ShapeDtypeStruct((pixels, width), bf),
            jax.ShapeDtypeStruct((w_head.shape[1], pixels), f32),
        ],
        in_specs=[vmem] * (2 * ways + 5 + len(tables)) + [hbm] * 2,
        out_specs=[vmem, vmem],
        scratch_shapes=[pltpu.VMEM((PAD_ROWS[l] * PITCH[l], channels), bf) for l in range(LEVELS)]
        + [pltpu.VMEM((pixels, TOTAL), bf)]
        + [pltpu.VMEM(((HGT + 2) * WID, width), bf)] * 3
        + [
            pltpu.VMEM((pixels, width), f32),
            pltpu.VMEM(w_gates.shape, bf),
            pltpu.VMEM(w_cand.shape, bf),
            pltpu.SemaphoreType.DMA((2,)),
        ],
        compiler_params=pltpu.CompilerParams(vmem_limit_bytes=48 << 20),
        name="edge_update",
    )(*bands, source, state, inject, w_place, w_head.T, *tables, w_gates, w_cand)


def ring_place(frame, size):
    if size % 2:
        return frame
    return jnp.where(frame % 2 == 0, frame // 2, size - (frame + 1) // 2)


def ring_place_of(frame, size):
    if size % 2:
        return frame
    half = frame >> 1
    return jnp.where((frame & 1) == 0, half, size - 1 - half)


def pack_kernel(target_ref, pose_ref, band_ref, first_ref, second_ref, asked_ref, row_ref, sems):
    half = second_ref.shape[0]
    first = pl.multiple_of(lax.axis_index("edges") * 2 * half, 2 * half)
    copies = [
        pltpu.make_async_copy(
            band_ref.at[0, pl.ds(first + i * half, half), :], ref.at[pl.ds(0, half), :], sems.at[i]
        )
        for i, ref in enumerate((first_ref, second_ref))
    ]
    for copy in copies:
        copy.start()
    sublane = lax.broadcasted_iota(jnp.int32, (SUB, LANES), 0)
    row_ref[...] = jnp.zeros(row_ref.shape, jnp.float32)
    row_ref[0:1, 0:POSE] = pose_ref[...]
    pose = jnp.broadcast_to(row_ref[0:1, :], (SUB, LANES))
    high = pose.astype(jnp.bfloat16).astype(jnp.float32)
    mid = (pose - high).astype(jnp.bfloat16).astype(jnp.float32)
    low = pose - high - mid
    tail = jnp.where(sublane == 0, high, jnp.where(sublane == 1, mid, jnp.where(sublane == 2, low, 0.0)))
    tail = jnp.concatenate([tail, jnp.zeros((SUB, LANES), jnp.float32)], axis=0)
    first_ref[half:, :] = tail.astype(jnp.bfloat16)
    asked_ref[...] = jnp.full(asked_ref.shape, target_ref[0], jnp.int32)
    for copy in copies:
        copy.wait()


def pack(targets, pose_row, fmap, share):
    vmem = pl.BlockSpec(memory_space=pltpu.VMEM)
    return pl.pallas_call(
        pack_kernel,
        out_shape=[
            jax.ShapeDtypeStruct((share // 2 + 16, fmap.shape[2]), jnp.bfloat16),
            jax.ShapeDtypeStruct((share // 2, fmap.shape[2]), jnp.bfloat16),
            jax.ShapeDtypeStruct((SUB, LANES), jnp.int32),
        ],
        in_specs=[pl.BlockSpec(memory_space=pltpu.SMEM), vmem, pl.BlockSpec(memory_space=pl.ANY)],
        out_specs=[vmem] * 3,
        scratch_shapes=[pltpu.VMEM((SUB, LANES), jnp.float32), pltpu.SemaphoreType.DMA((2,))],
        name="pack",
    )(targets, pose_row, fmap)


def ring_distances(asked, size):
    here = ring_place(lax.axis_index("frames"), size)
    apart = [ring_place_of(a, size) - here for a in asked]
    return [jnp.where(d < 0, d + size, d) for d in apart]


def asked_tiles(refs):
    return [jnp.full((SUB, LANES), refs[0][0], jnp.int32)] + [ref[...] for ref in refs[1:]]


def pick_kernel(size, ways, *refs):
    asked, blocks, outs = refs[:ways], (None,) + refs[ways : ways + size - 1], refs[ways + size - 1 :]
    far = ring_distances(asked_tiles(asked), size)
    rows = outs[0].shape[0]
    tile = 2 * SUB
    chosen = []
    for s in range(ways):
        ones = [jnp.where(far[s] == d, 1.0, 0.0) for d in range(size)]
        chosen.append([jnp.concatenate([w, w], axis=0).astype(jnp.bfloat16) for w in ones])

    def step(index, carry):
        at = pl.ds(pl.multiple_of(index * tile, tile), tile)
        values = [None] + [block[at, :] for block in blocks[1:]]
        for s in range(ways):
            total = values[1] * chosen[s][1]
            for d in range(2, size):
                total = total + values[d] * chosen[s][d]
            outs[s][at, :] = total
        return carry

    lax.fori_loop(0, rows // tile, step, 0, unroll=2)


def pick(asked, blocks, rows):
    ways, size = len(asked), len(blocks)
    vmem = pl.BlockSpec(memory_space=pltpu.VMEM)
    return pl.pallas_call(
        lambda *refs: pick_kernel(size, ways, *refs),
        out_shape=[jax.ShapeDtypeStruct((rows, blocks[0].shape[1]), jnp.bfloat16)] * ways,
        in_specs=[pl.BlockSpec(memory_space=pltpu.SMEM)] + [vmem] * (ways + size - 2),
        out_specs=[vmem] * ways,
        compiler_params=pltpu.CompilerParams(vmem_limit_bytes=16 << 20),
        name="pick",
    )(*asked, *blocks[1:])


def index_kernel(size, ways, *refs):
    asked, blocks = refs[:ways], refs[ways : ways + size]
    rel_ref, place_ref, lift_ref, spread_ref, table = refs[ways + size :]
    group, edge_slot = lax.axis_index("frames"), lax.axis_index("edges")
    asked = asked_tiles(asked)
    far = ring_distances(asked, size)
    unknowns, width = lift_ref.shape[0], place_ref.shape[1]
    rows = POSE * SUB
    sublane = lax.broadcasted_iota(jnp.int32, (SUB, LANES), 0)
    lane = lax.broadcasted_iota(jnp.int32, (SUB, LANES), 1)
    wide_sub = lax.broadcasted_iota(jnp.int32, (SUB, width), 0)
    wide_lane = lax.broadcasted_iota(jnp.int32, (SUB, width), 1)
    place = [jnp.zeros((SUB, width), jnp.float32) for _ in range(POSE)]
    lift = [jnp.zeros((SUB, LANES), jnp.float32) for _ in range(unknowns // SUB)]
    for slot in range(ways):
        edge, target = peer(edge_slot, slot, ways), asked[slot]
        wide = jnp.concatenate([target] * (width // LANES), axis=1)
        for c in range(POSE):
            at_target = (wide_lane == c * size + wide).astype(jnp.float32)
            at_source = (wide_lane == c * size + group).astype(jnp.float32)
            place[c] = jnp.where(wide_sub == edge, at_target - at_source, place[c])
        for g in range(unknowns // SUB):
            c, n = divmod(g * SUB, size)
            frame = sublane + n
            hit = (frame == target).astype(jnp.float32) - (frame == group).astype(jnp.float32)
            lift[g] = jnp.where(lane == c * SUB + edge, hit, lift[g])
    for c in range(POSE):
        place_ref[c * SUB : (c + 1) * SUB, :] = place[c]
        spread_ref[c * SUB : (c + 1) * SUB, :] = place[c]
    spread_ref[rows : rows + SUB, :] = ((wide_lane == unknowns) & (wide_sub == 0)).astype(jnp.float32)
    spread_ref[rows + SUB :, :] = jnp.zeros((LANES - rows - SUB, width), jnp.float32)
    for g in range(unknowns // SUB):
        lift_ref[g * SUB : (g + 1) * SUB, :] = lift[g]
    for d in range(size):
        terms = blocks[d][blocks[d].shape[0] - 16 :, :].astype(jnp.float32)
        table[d : d + 1, :] = terms[0:1, :] + terms[1:2, :] + terms[2:3, :]
    apart = jnp.zeros((SUB, LANES), jnp.float32)
    for slot in range(ways):
        pose = jnp.zeros((SUB, LANES), jnp.float32)
        for d in range(size):
            pose = jnp.where(far[slot] == d, table[d : d + 1, :], pose)
        apart = jnp.where(sublane == peer(edge_slot, slot, ways), pose - table[0:1, :], apart)
    for c in range(POSE):
        rel_ref[c * SUB : (c + 1) * SUB, :] = jnp.broadcast_to(apart[:, c : c + 1], (SUB, LANES))


def index_tables(asked, blocks, width):
    ways, size = len(asked), len(blocks)
    rows, unknowns = POSE * SUB, POSE * size
    shapes = [(rows, LANES), (rows, width), (unknowns, LANES), (LANES, width)]
    return call(
        lambda *refs: index_kernel(size, ways, *refs),
        shapes,
        (*asked, *blocks),
        "index",
        smem=(0,),
        scratch=[(-(-size // SUB) * SUB, LANES)],
    )


def gauss_newton_terms(heads, depth_ref, rel, lift_ref, spread_ref, gram_ref, damp_ref, total_ref):
    pixels = depth_ref.shape[1]
    rows = POSE * SUB
    sublane = lax.broadcasted_iota(jnp.int32, (SUB, LANES), 0)
    lane = lax.broadcasted_iota(jnp.int32, (SUB, LANES), 1)
    col_pos = (lane % WID).astype(jnp.float32)
    lane_row = lane // WID
    center_x = (WID - 1) / 2.0
    center_y = (HGT - 1) / 2.0
    ray_x = (col_pos - center_x) / focal
    move_x, move_y, move_z, turn_x, turn_y, turn_z = rel
    pairs_u = [(a, b) for a in (0, 2, 3, 4, 5) for b in (0, 2, 3, 4, 5) if a <= b]
    pairs_v = [(a, b) for a in (1, 2, 3, 4, 5) for b in (1, 2, 3, 4, 5) if a <= b]
    keys = sorted(set(pairs_u) | set(pairs_v))

    def chunk(index, carry):
        hess, grad = dict(zip(keys, carry[0])), list(carry[1])
        at = pl.ds(pl.multiple_of(index * LANES, LANES), LANES)
        depth = jnp.broadcast_to(depth_ref[:, at], (SUB, LANES))
        flow_u, flow_v, weight_u, weight_v = [heads[i, :, at] for i in range(4)]
        row_pos = (lane_row + index * (LANES // WID)).astype(jnp.float32)
        ray_y = (row_pos - center_y) / focal
        point_x = ray_x + turn_y - turn_z * ray_y + depth * move_x
        point_y = ray_y + turn_z * ray_x - turn_x + depth * move_y
        point_z = 1.0 + turn_x * ray_y - turn_y * ray_x + depth * move_z
        inverse_z = 1.0 / point_z
        slope = focal * inverse_z
        shift_u = slope * point_x
        shift_v = slope * point_y
        bend_u = -shift_u * inverse_z
        bend_v = -shift_v * inverse_z
        resid_u = col_pos + flow_u - (shift_u + center_x)
        resid_v = row_pos + flow_v - (shift_v + center_y)
        jac_u = [depth * slope, None, depth * bend_u, bend_u * ray_y, slope - bend_u * ray_x, -slope * ray_y]
        jac_v = [None, jac_u[0], depth * bend_v, bend_v * ray_y - slope, -bend_v * ray_x, slope * ray_x]
        depth_u = slope * move_x + bend_u * move_z
        depth_v = slope * move_y + bend_v * move_z
        scaled_u = [None if j is None else weight_u * j for j in jac_u]
        scaled_v = [None if j is None else weight_v * j for j in jac_v]
        for a, b in pairs_u:
            hess[a, b] = hess[a, b] + scaled_u[a] * jac_u[b]
        for a, b in pairs_v:
            hess[a, b] = hess[a, b] + scaled_v[a] * jac_v[b]
        for c in range(POSE):
            cross = None
            for scaled, resid, along in ((scaled_u, resid_u, depth_u), (scaled_v, resid_v, depth_v)):
                if scaled[c] is not None:
                    grad[c] = grad[c] + scaled[c] * resid
                    term = scaled[c] * along
                    cross = term if cross is None else cross + term
            gram_ref[c * SUB : (c + 1) * SUB, at] = cross
        pull_u = weight_u * depth_u
        pull_v = weight_v * depth_v
        curve = jnp.sum(pull_u * depth_u + pull_v * depth_v, axis=0, keepdims=True)
        slide = jnp.sum(pull_u * resid_u + pull_v * resid_v, axis=0, keepdims=True)
        gram_ref[rows : rows + SUB, at] = jnp.where(sublane == 0, slide, 0.0)
        damp_ref[:, at] = (1.0 + depth_damping) * curve + depth_floor
        return tuple(hess[k] for k in keys), tuple(grad)

    zero = jnp.zeros((SUB, LANES), jnp.float32)
    hess, grad = lax.fori_loop(
        0, pixels // LANES, chunk, (tuple(zero for _ in keys), tuple(zero for _ in range(POSE))), unroll=2
    )
    table = {k: jnp.sum(h, axis=1, keepdims=True) for k, h in zip(keys, hess)}
    slabs = []
    for c in range(POSE):
        slab = jnp.where(lane == rows, jnp.sum(grad[c], axis=1, keepdims=True), 0.0)
        for other in range(POSE):
            key = (min(c, other), max(c, other))
            if key in table:
                slab = jnp.where(lane == sublane + other * SUB, table[key], slab)
        slabs.append(slab)
    local = jnp.concatenate(slabs, axis=0)
    gram = gram_ref[...]
    scaled = gram[0:rows, :] / damp_ref[...]
    schur = nt_dot(scaled, gram, precision=highest)
    schur = jnp.concatenate([schur, jnp.zeros((rows, LANES - rows - SUB), jnp.float32)], axis=1)
    lifted = nn_dot(lift_ref[:, :rows], local - schur, precision=highest)
    total_ref[...] = nn_dot(lifted, spread_ref[...], precision=highest)


def solve_step(parts, unknowns):
    system = parts[0][...]
    for part in parts[1:]:
        system = system + part[...]
    width = system.shape[1]
    lane = lax.broadcasted_iota(jnp.int32, (SUB, width), 1)
    sublane = lax.broadcasted_iota(jnp.int32, (SUB, width), 0)
    groups = []
    for g in range(unknowns // SUB):
        block = system[g * SUB : (g + 1) * SUB, :]
        block = jnp.where(lane == sublane + g * SUB, block * (1.0 + pose_damping) + pose_floor, block)
        groups.append(block)
    for k in range(0, unknowns, PIVOTS):
        g, s = divmod(k, SUB)
        columns = [[jnp.broadcast_to(b[:, k + j : k + j + 1], b.shape) for b in groups] for j in range(PIVOTS)]
        tops = [groups[g][s + i : s + i + 1, :] for i in range(PIVOTS)]
        mult = [[columns[j][g][s + i : s + i + 1, :] for j in range(PIVOTS)] for i in range(PIVOTS)]
        for p in range(PIVOTS):
            inverse = 1.0 / mult[p][p]
            tops[p] = tops[p] * inverse
            for j in range(p + 1, PIVOTS):
                mult[p][j] = mult[p][j] * inverse
            for i in range(PIVOTS):
                if i != p:
                    tops[i] = tops[i] - mult[i][p] * tops[p]
                    for j in range(p + 1, PIVOTS):
                        mult[i][j] = mult[i][j] - mult[i][p] * mult[p][j]
        wide = [jnp.broadcast_to(t, groups[0].shape) for t in tops]
        for i in range(len(groups)):
            update = groups[i]
            for j in range(PIVOTS):
                update = update - columns[j][i] * wide[j]
            if i == g:
                for j in range(PIVOTS):
                    update = jnp.where(sublane == s + j, wide[j], update)
            groups[i] = update
    return jnp.concatenate([jnp.broadcast_to(b[:, unknowns : unknowns + 1], (SUB, LANES)) for b in groups], axis=0)


def split_rel(rel_ref):
    return [rel_ref[c * SUB : (c + 1) * SUB, :] for c in range(POSE)]


def first_kernel(ways, *refs):
    slots, refs = refs[:ways], refs[ways:]
    depth_ref, rel_ref, lift_ref, spread_ref, heads, gram_ref, damp_ref, total_ref = refs
    edge_slot = lax.axis_index("edges")
    if ways < SUB:
        heads[...] = jnp.zeros(heads.shape, jnp.float32)
    for slot in range(ways):
        edge = peer(edge_slot, slot, ways)
        for i in range(4):
            value = slots[slot][i : i + 1, :]
            if i >= 2:
                value = jax.nn.sigmoid(value)
            heads[i, pl.ds(edge, 1), :] = value
    gauss_newton_terms(heads, depth_ref, split_rel(rel_ref), lift_ref, spread_ref, gram_ref, damp_ref, total_ref)


def take_step(parts, place_ref, gram_ref, damp_ref, depth_ref, out_depth_ref):
    unknowns = parts[0].shape[0]
    step = solve_step(parts, unknowns)
    edge_step = nn_dot(place_ref[:, :unknowns], step, precision=highest)
    slices = [edge_step[c * SUB : (c + 1) * SUB, :] for c in range(POSE)]
    rows = POSE * SUB

    def chunk(index, carry):
        at = pl.ds(pl.multiple_of(index * LANES, LANES), LANES)
        total = slices[0] * gram_ref[0:SUB, at]
        for c in range(1, POSE):
            total = total + slices[c] * gram_ref[c * SUB : (c + 1) * SUB, at]
        along = jnp.sum(total, axis=0, keepdims=True)
        out_depth_ref[:, at] = depth_ref[:, at] + (gram_ref[rows : rows + 1, at] - along) / damp_ref[:, at]
        return carry

    lax.fori_loop(0, depth_ref.shape[1] // LANES, chunk, 0, unroll=4)
    return step, edge_step


def middle_kernel(count, *refs):
    parts, refs = refs[:count], refs[count:]
    (heads, gram_ref, damp_ref, depth_ref, rel_ref, place_ref, lift_ref, spread_ref,
     out_gram, out_damp, out_total, out_depth, out_step, out_rel) = refs
    step, edge_step = take_step(parts, place_ref, gram_ref, damp_ref, depth_ref, out_depth)
    out_step[...] = step
    out_rel[...] = rel_ref[...] + edge_step
    gauss_newton_terms(heads, out_depth, split_rel(out_rel), lift_ref, spread_ref, out_gram, out_damp, out_total)


def last_kernel(count, *refs):
    own_ref, parts, refs = refs[0], refs[1 : count + 1], refs[count + 1 :]
    before, refs = refs[: ITERS - 1], refs[ITERS - 1 :]
    gram_ref, damp_ref, depth_ref, place_ref, out_depth, out_pose, held = refs
    step, _ = take_step(parts, place_ref, gram_ref, damp_ref, depth_ref, out_depth)
    for other in before:
        step = step + other[...]
    held[...] = step
    frames, group = lax.axis_size("frames"), lax.axis_index("frames")
    lane = lax.broadcasted_iota(jnp.int32, (1, LANES), 1)
    moved = jnp.zeros((1, LANES), jnp.float32)
    for c in range(POSE):
        moved = jnp.where(lane == c, held[pl.ds(c * frames + group, 1), :], moved)
    out_pose[...] = own_ref[...] + moved[:, :POSE]


def call(kernel, shapes, inputs, name, smem=(), scratch=()):
    vmem = pl.BlockSpec(memory_space=pltpu.VMEM)
    f32 = lambda shape: jax.ShapeDtypeStruct(shape, jnp.float32)
    return pl.pallas_call(
        kernel,
        out_shape=[f32(s) for s in shapes],
        in_specs=[
            pl.BlockSpec(memory_space=pltpu.SMEM if i in smem else pltpu.VMEM) for i in range(len(inputs))
        ],
        out_specs=[vmem] * len(shapes),
        scratch_shapes=[pltpu.VMEM(s, jnp.float32) for s in scratch],
        compiler_params=pltpu.CompilerParams(vmem_limit_bytes=32 << 20),
        name=name,
    )(*inputs)


def sum_over(value, axis):
    size = lax.axis_size(axis)
    if size & (size - 1):
        parts = [value]
        for s in range(1, size):
            parts.append(lax.ppermute(value, axis, [(i, (i + s) % size) for i in range(size)]))
        return parts
    radices, left = [], size
    while left > 1:
        radix = 4 if left % 4 == 0 else 2
        radices.append(radix)
        left //= radix
    stride, parts = 1, [value]
    for radix in radices:
        value = sum(parts[1:], parts[0])
        parts = [value]
        for s in range(1, radix):
            parts.append(lax.ppermute(value, axis, [(i, i ^ (s * stride)) for i in range(size)]))
        stride *= radix
    return parts


def peer(index, slot, size):
    return index ^ slot if size & (size - 1) == 0 else (index + slot) % size


def exchange(values, axis):
    size = lax.axis_size(axis)
    out = [values[0]]
    for s in range(1, size):
        if size & (size - 1) == 0:
            pairs = [(i, i ^ s) for i in range(size)]
        else:
            pairs = [((i + s) % size, i) for i in range(size)]
        out.append(lax.ppermute(values[s], axis, pairs))
    return out


def ring_order(size):
    if size % 2:
        return list(range(size))
    return list(range(0, size, 2)) + list(range(size - 1, 0, -2))


def ring_gather(values, axis):
    size = lax.axis_size(axis)
    order = ring_order(size)
    ahead = [(order[(i + 1) % size], order[i]) for i in range(size)]
    behind = [(order[i], order[(i + 1) % size]) for i in range(size)]
    out = [[value] + [None] * (size - 1) for value in values]
    up, down = list(values), list(values)
    for s in range(1, size // 2 + 1):
        for i in range(len(values)):
            if 2 * s < size or i % 2 == 0:
                up[i] = out[i][s] = lax.ppermute(up[i], axis, ahead)
            if size - s > size // 2 or (2 * s == size and i % 2):
                down[i] = out[i][size - s] = lax.ppermute(down[i], axis, behind)
    return out


def per_device(fmap, context, poses, inv_depth, targets, w_corr, w_gates, w_cand, w_head):
    ways = lax.axis_size("edges")
    frames_total = lax.axis_size("frames")
    pixel_count = fmap.shape[1]
    share = pixel_count // ways
    bf = jnp.bfloat16
    first_band, second_band, target = pack(targets, poses.T, fmap, share)
    first, second = ring_gather((first_band, second_band), "frames")
    late_target, _ = lax.optimization_barrier((target, first[min(2, frames_total // 2)]))
    asked = [targets] + exchange([late_target] * ways, "edges")[1:]
    unknowns = POSE * frames_total
    width = -(-(unknowns + 1) // LANES) * LANES
    rows = POSE * SUB
    early, late = pick(asked, second, share // 2), pick(asked, first, share // 2)
    bands = exchange(late, "edges") + exchange(early, "edges")
    rel, place, lift, spread = index_tables(asked, first, width)

    own_source, own_context, own_corr, _ = lax.optimization_barrier((fmap[0], context[0], w_corr, late[0]))
    w_place = jnp.dot(jnp.asarray(PLACE, bf), own_corr, preferred_element_type=jnp.float32).astype(bf)
    w_place = jnp.concatenate([w_place[:TOTAL], w_place[TOTAL:]], axis=1)
    source, state, inject = prepare(own_source, own_context)
    hidden, heads = edge_update(bands, source, state, inject, w_place, w_gates, w_cand, w_head)
    slots = exchange([heads] * ways, "edges")

    big, line = (rows + SUB, pixel_count), (1, pixel_count)
    heads_all, gram, damp, total = call(
        lambda *refs: first_kernel(ways, *refs),
        [(4, SUB, pixel_count), big, line, (unknowns, width)],
        (*slots, inv_depth, rel, lift, spread),
        "terms",
    )
    depth = inv_depth
    steps = []
    for index in range(ITERS - 1):
        parts = sum_over(total, "frames")
        count = len(parts)
        gram, damp, total, depth, step, rel = call(
            lambda *refs: middle_kernel(count, *refs),
            [big, line, (unknowns, width), line, (unknowns, LANES), (rows, LANES)],
            (*parts, heads_all, gram, damp, depth, rel, place, lift, spread),
            "step",
        )
        steps.append(step)
    parts = sum_over(total, "frames")
    count = len(parts)
    depth, new_poses = call(
        lambda *refs: last_kernel(count, *refs),
        [line, (1, POSE)],
        (poses.T, *parts, *steps, gram, damp, depth, place),
        "final",
        scratch=[(unknowns, LANES)],
    )
    return (new_poses.T, depth, hidden[None])


def solution(mesh):
    return jax.shard_map(
        per_device,
        mesh=mesh,
        in_specs=(
            P("frames", None, None),
            P("frames", None, None),
            P(None, "frames"),
            P("frames", None),
            P(("frames", "edges")),
            P(),
            P(),
            P(),
            P(),
        ),
        out_specs=(P(None, "frames"), P("frames", None), P(("frames", "edges"), None, None)),
        check_vma=False,
    )
```

```python
import math

import numpy as np
import jax
import jax.numpy as jnp
from jax import lax
from jax.experimental import pallas as pl
from jax.experimental.pallas import tpu as pltpu
from jax.sharding import PartitionSpec as P

HGT = 48
WID = 64
LEVELS = 4
RADIUS = 3
ITERS = 2
SPAN = 2 * RADIUS + 1
POSE = 6
LANES = 128
SUB = 8
PIVOTS = 8

focal = 50.0
pose_damping = 0.1
pose_floor = 1.0
depth_damping = 0.1
depth_floor = 1.0
highest = lax.Precision.HIGHEST


PITCH = (64, 32, 16, 16)
WINDOW = tuple(8 * p for p in PITCH)
START = (0, 512, 768, 896)
TOTAL = 1024
PAD_ROWS = (54, 31, 19, 13)


def column_order():
    slot = np.arange(WID)
    return 8 * (7 - slot % 8) + slot // 8


def lookup_tables():
    cols = column_order()
    perm = np.zeros((2 * WID, 2 * WID), np.float32)
    for half in range(2):
        perm[half * WID + np.arange(WID), half * WID + cols] = 1.0
    mask = np.zeros((LEVELS, 2 * WID, LANES), np.float32)
    place = np.zeros((2 * TOTAL, LEVELS * SPAN * SPAN), np.float32)
    for level in range(LEVELS):
        pitch, width = PITCH[level], WID >> level
        per_block = LANES // pitch
        for y in range(8):
            block, first = y // per_block, (y % per_block) * pitch
            for b in range(-RADIUS, RADIUS + 1):
                lane = (first + b) % LANES
                reach = (cols >> level) + b
                ok = ((reach >= 0) & (reach < width)).astype(np.float32)
                mask[level, :, lane] = np.concatenate([ok, ok])
                row = START[level] + block * LANES + lane
                for odd in range(2):
                    a = y - RADIUS - (odd if level == 0 else 0)
                    if -RADIUS <= a <= RADIUS:
                        source = level * SPAN * SPAN + (a + RADIUS) * SPAN + b + RADIUS
                        place[odd * TOTAL + row, source] = 1.0
    pools = []
    for level in range(1, LEVELS):
        step = 1 << level
        pool = np.zeros((PITCH[level], step * WID), np.float32)
        for col in range(WID):
            pool[col // step, np.arange(step) * WID + col] = 1.0 / (step * step)
        pools.append(pool)
    return perm, mask, place, pools


PERM, MASK, PLACE, POOLS = lookup_tables()


def nt_dot(a, b, **kw):
    return lax.dot_general(a, b, (((1,), (1,)), ((), ())), preferred_element_type=jnp.float32, **kw)


def nn_dot(a, b, **kw):
    return lax.dot_general(a, b, (((1,), (0,)), ((), ())), preferred_element_type=jnp.float32, **kw)


def prepare_kernel(src_ref, ctx_ref, perm_ref, out_src, out_state, out_inject):
    width = out_state.shape[1]
    perm = perm_ref[...]

    def pair_loop(index, carry):
        at = pl.ds(pl.multiple_of(index * 2 * WID, 2 * WID), 2 * WID)
        out_src[at, :] = nn_dot(perm, src_ref[at, :]).astype(jnp.bfloat16)
        context = nn_dot(perm, ctx_ref[at, :])
        out_state[at, :] = jnp.tanh(context[:, :width]).astype(jnp.bfloat16)
        out_inject[at, :] = jnp.maximum(context[:, width:], 0.0).astype(jnp.bfloat16)
        return carry

    lax.fori_loop(0, HGT // 2, pair_loop, 0, unroll=4)


def prepare(source, context):
    vmem = pl.BlockSpec(memory_space=pltpu.VMEM)
    pixels, channels = source.shape
    half = context.shape[1] // 2
    return pl.pallas_call(
        prepare_kernel,
        out_shape=[jax.ShapeDtypeStruct((pixels, n), jnp.bfloat16) for n in (channels, half, half)],
        in_specs=[vmem] * 3,
        out_specs=[vmem] * 3,
        compiler_params=pltpu.CompilerParams(vmem_limit_bytes=16 << 20),
        name="prepare",
    )(source, context, jnp.asarray(PERM, jnp.bfloat16))


def edge_kernel(ways, *refs):
    band_refs, refs = refs[: 2 * ways], refs[2 * ways :]
    (src_ref, state_in, inject_ref, w_ref, head_ref, back_ref, mask_ref, pool1_ref, pool2_ref, pool3_ref, gates_hbm,
     cand_hbm, out_ref, heads_ref, pad0, pad1, pad2, pad3, corr_ref, state_ref, motion_ref, reset_ref, update_ref,
     gates_ref, cand_ref, sems) = refs
    copies = [
        pltpu.make_async_copy(gates_hbm, gates_ref, sems.at[0]),
        pltpu.make_async_copy(cand_hbm, cand_ref, sems.at[1]),
    ]
    for copy in copies:
        copy.start()
    width = out_ref.shape[1]
    edge = lax.axis_index("edges")
    half_share = band_refs[0].shape[0]
    scale = 1.0 / math.sqrt(src_ref.shape[1])
    pads = (pad0, pad1, pad2, pad3)
    for level, pad in enumerate(pads):
        lead = RADIUS * PITCH[level]
        body = (HGT >> level) * PITCH[level]
        pad[0:lead] = jnp.zeros((lead, pad.shape[1]), pad.dtype)
        pad[lead + body :] = jnp.zeros((pad.shape[0] - lead - body, pad.shape[1]), pad.dtype)
    for ref in (state_ref, motion_ref, reset_ref):
        ref[0:WID, :] = jnp.zeros((WID, width), ref.dtype)
        ref[(HGT + 1) * WID :, :] = jnp.zeros((WID, width), ref.dtype)
    state_ref[WID : (HGT + 1) * WID, :] = state_in[...]
    for slot in range(ways):
        for half in range(2):
            at = pl.multiple_of((peer(edge, slot, ways) * 2 + half) * half_share + RADIUS * WID, WID)
            pad0[pl.ds(at, half_share), :] = band_refs[half * ways + slot][...]
    for level, pool_ref in ((1, pool1_ref), (2, pool2_ref), (3, pool3_ref)):
        rows = 1 << level
        pool = pool_ref[...]
        for row in range(HGT >> level):
            first = (RADIUS + row * rows) * WID
            pooled = nn_dot(pool, pad0[first : first + rows * WID, :])
            at = (RADIUS + row) * PITCH[level]
            pads[level][at : at + PITCH[level], :] = pooled.astype(jnp.bfloat16)

    tile = 8 * WID
    blocks = HGT // 8
    start = lambda block: block * tile if isinstance(block, int) else pl.multiple_of(block * tile, tile)

    def look_up(block):
        for inner in range(4):
            pair = block * 4 + inner
            first = start(block) + inner * 2 * WID
            source = src_ref[pl.ds(first, 2 * WID), :]
            for level in range(LEVELS):
                shift = max(level - 1, 0)
                base = (pair >> shift) * PITCH[level] * (2 if level == 0 else 1)
                base = base if isinstance(base, int) else pl.multiple_of(base, 16)
                volume = nt_dot(source, pads[level][pl.ds(base, WINDOW[level]), :]) * scale
                keep = mask_ref[level]
                for lanes in range(WINDOW[level] // LANES):
                    part = volume[:, lanes * LANES : (lanes + 1) * LANES]
                    rolled = []
                    for group in range(2 * SUB):
                        turn = (8 >> level) * 7 + ((group % SUB) >> level)
                        rolled.append(
                            pltpu.roll(
                                part[group * SUB : (group + 1) * SUB, :],
                                (LANES - turn) % LANES,
                                1,
                                stride=8 >> level,
                                stride_axis=0,
                            )
                        )
                    value = jnp.concatenate(rolled, axis=0).astype(jnp.bfloat16) * keep
                    at = START[level] + lanes * LANES
                    corr_ref[pl.ds(first, 2 * WID), at : at + LANES] = value

    def encode(block):
        first = start(block)
        both = nn_dot(corr_ref[pl.ds(first, tile), :], w_ref[...])
        both = both.reshape(4, 2, WID, 2 * width)
        encoded = jnp.concatenate([both[:, :1, :, :width], both[:, 1:, :, width:]], axis=1).reshape(tile, width)
        inject = inject_ref[pl.ds(first, tile), :].astype(jnp.float32)
        motion_ref[pl.ds(first + WID, tile), :] = (jnp.maximum(encoded, 0.0) + inject).astype(jnp.bfloat16)

    sub = lax.broadcasted_iota(jnp.int32, (8, SUB, width), 1)

    def convolve(block, left_ref, right_ref, weights, columns):
        first = start(block)
        inputs = []
        for row in range(3):
            at = pl.ds(first + row * WID, tile)
            inputs.append(jnp.concatenate([left_ref[at, :], right_ref[at, :]], axis=1))
        taps = []
        for cols in columns:
            total = None
            for row in range(3):
                mats = [weights(row, col) for col in cols]
                mat = mats[0] if len(mats) == 1 else jnp.concatenate(mats, axis=1)
                part = nn_dot(inputs[row], mat)
                total = part if total is None else total + part
            size = total.shape[1] // len(cols)
            taps += [total[:, i * size : (i + 1) * size] for i in range(len(cols))]
        out = []
        for half in range(taps[0].shape[1] // width):
            left, mid, right = [t[:, half * width : (half + 1) * width].reshape(8, WID, width) for t in taps]
            wrapped = jnp.where(sub == SUB - 1, 0.0, jnp.roll(left[:, WID - SUB :], -1, axis=1))
            before = jnp.concatenate([wrapped, left[:, : WID - SUB]], axis=1)
            wrapped = jnp.where(sub == 0, 0.0, jnp.roll(right[:, :SUB], 1, axis=1))
            after = jnp.concatenate([right[:, SUB:], wrapped], axis=1)
            out.append((mid + before + after).reshape(tile, width))
        return out

    def gates(block):
        first = start(block)
        update, reset = convolve(
            block, state_ref, motion_ref, lambda r, c: gates_ref[r, c], ((0,), (1,), (2,))
        )
        update_ref[pl.ds(first, tile), :] = jax.nn.sigmoid(update)
        state = state_ref[pl.ds(first + WID, tile), :].astype(jnp.float32)
        reset_ref[pl.ds(first + WID, tile), :] = (jax.nn.sigmoid(reset) * state).astype(jnp.bfloat16)

    def candidate(block):
        first = start(block)
        (total,) = convolve(block, reset_ref, motion_ref, lambda r, c: cand_ref[r, c], ((0, 1), (2,)))
        update = update_ref[pl.ds(first, tile), :]
        state = state_ref[pl.ds(first + WID, tile), :].astype(jnp.float32)
        hidden = ((1.0 - update) * state + update * jnp.tanh(total)).astype(jnp.bfloat16)
        for inner in range(4):
            at = inner * 2 * WID
            ordered = nn_dot(back_ref[...], hidden[at : at + 2 * WID, :]).astype(jnp.bfloat16)
            out_ref[pl.ds(first + at, 2 * WID), :] = ordered
            heads_ref[:, pl.ds(first + at, 2 * WID)] = nt_dot(head_ref[...], ordered)

    look_up(0)

    def first_loop(block, carry):
        encode(block - 1)
        look_up(block)
        return carry

    lax.fori_loop(1, blocks, first_loop, 0)
    encode(blocks - 1)
    for copy in copies:
        copy.wait()
    def gates_loop(block, carry):
        gates(block)
        return carry

    def candidate_loop(block, carry):
        candidate(block)
        return carry

    lax.fori_loop(0, blocks, gates_loop, 0, unroll=True)
    lax.fori_loop(0, blocks, candidate_loop, 0, unroll=True)


def edge_update(bands, source, state, inject, w_place, w_gates, w_cand, w_head):
    pixels, channels = source.shape
    width = w_head.shape[0]
    ways = len(bands) // 2
    vmem = pl.BlockSpec(memory_space=pltpu.VMEM)
    hbm = pl.BlockSpec(memory_space=pl.ANY)
    bf, f32 = jnp.bfloat16, jnp.float32
    tables = [jnp.asarray(x, bf) for x in (PERM.T, MASK, *POOLS)]
    return pl.pallas_call(
        lambda *refs: edge_kernel(ways, *refs),
        out_shape=[
            jax.ShapeDtypeStruct((pixels, width), bf),
            jax.ShapeDtypeStruct((w_head.shape[1], pixels), f32),
        ],
        in_specs=[vmem] * (2 * ways + 5 + len(tables)) + [hbm] * 2,
        out_specs=[vmem, vmem],
        scratch_shapes=[pltpu.VMEM((PAD_ROWS[l] * PITCH[l], channels), bf) for l in range(LEVELS)]
        + [pltpu.VMEM((pixels, TOTAL), bf)]
        + [pltpu.VMEM(((HGT + 2) * WID, width), bf)] * 3
        + [
            pltpu.VMEM((pixels, width), f32),
            pltpu.VMEM(w_gates.shape, bf),
            pltpu.VMEM(w_cand.shape, bf),
            pltpu.SemaphoreType.DMA((2,)),
        ],
        compiler_params=pltpu.CompilerParams(vmem_limit_bytes=48 << 20),
        name="edge_update",
    )(*bands, source, state, inject, w_place, w_head.T, *tables, w_gates, w_cand)


def ring_place(frame, size):
    if size % 2:
        return frame
    return jnp.where(frame % 2 == 0, frame // 2, size - (frame + 1) // 2)


def ring_place_of(frame, size):
    if size % 2:
        return frame
    half = frame >> 1
    return jnp.where((frame & 1) == 0, half, size - 1 - half)


def pack_kernel(target_ref, pose_ref, band_ref, first_ref, second_ref, asked_ref, row_ref, sems):
    half = second_ref.shape[0]
    first = pl.multiple_of(lax.axis_index("edges") * 2 * half, 2 * half)
    copies = [
        pltpu.make_async_copy(
            band_ref.at[0, pl.ds(first + i * half, half), :], ref.at[pl.ds(0, half), :], sems.at[i]
        )
        for i, ref in enumerate((first_ref, second_ref))
    ]
    for copy in copies:
        copy.start()
    sublane = lax.broadcasted_iota(jnp.int32, (SUB, LANES), 0)
    row_ref[...] = jnp.zeros(row_ref.shape, jnp.float32)
    row_ref[0:1, 0:POSE] = pose_ref[...]
    pose = jnp.broadcast_to(row_ref[0:1, :], (SUB, LANES))
    high = pose.astype(jnp.bfloat16).astype(jnp.float32)
    mid = (pose - high).astype(jnp.bfloat16).astype(jnp.float32)
    low = pose - high - mid
    tail = jnp.where(sublane == 0, high, jnp.where(sublane == 1, mid, jnp.where(sublane == 2, low, 0.0)))
    tail = jnp.concatenate([tail, jnp.zeros((SUB, LANES), jnp.float32)], axis=0)
    first_ref[half:, :] = tail.astype(jnp.bfloat16)
    asked_ref[...] = jnp.full(asked_ref.shape, target_ref[0], jnp.int32)
    for copy in copies:
        copy.wait()


def pack(targets, pose_row, fmap, share):
    vmem = pl.BlockSpec(memory_space=pltpu.VMEM)
    return pl.pallas_call(
        pack_kernel,
        out_shape=[
            jax.ShapeDtypeStruct((share // 2 + 16, fmap.shape[2]), jnp.bfloat16),
            jax.ShapeDtypeStruct((share // 2, fmap.shape[2]), jnp.bfloat16),
            jax.ShapeDtypeStruct((SUB, LANES), jnp.int32),
        ],
        in_specs=[pl.BlockSpec(memory_space=pltpu.SMEM), vmem, pl.BlockSpec(memory_space=pl.ANY)],
        out_specs=[vmem] * 3,
        scratch_shapes=[pltpu.VMEM((SUB, LANES), jnp.float32), pltpu.SemaphoreType.DMA((2,))],
        name="pack",
    )(targets, pose_row, fmap)


def ring_distances(asked, size):
    here = ring_place(lax.axis_index("frames"), size)
    apart = [ring_place_of(a, size) - here for a in asked]
    return [jnp.where(d < 0, d + size, d) for d in apart]


def asked_tiles(refs):
    return [jnp.full((SUB, LANES), refs[0][0], jnp.int32)] + [ref[...] for ref in refs[1:]]


def pick_kernel(size, ways, *refs):
    asked, blocks, outs = refs[:ways], (None,) + refs[ways : ways + size - 1], refs[ways + size - 1 :]
    far = ring_distances(asked_tiles(asked), size)
    rows = outs[0].shape[0]
    tile = 2 * SUB
    chosen = []
    for s in range(ways):
        ones = [jnp.where(far[s] == d, 1.0, 0.0) for d in range(size)]
        chosen.append([jnp.concatenate([w, w], axis=0).astype(jnp.bfloat16) for w in ones])

    def step(index, carry):
        at = pl.ds(pl.multiple_of(index * tile, tile), tile)
        values = [None] + [block[at, :] for block in blocks[1:]]
        for s in range(ways):
            total = values[1] * chosen[s][1]
            for d in range(2, size):
                total = total + values[d] * chosen[s][d]
            outs[s][at, :] = total
        return carry

    lax.fori_loop(0, rows // tile, step, 0, unroll=2)


def pick(asked, blocks, rows):
    ways, size = len(asked), len(blocks)
    vmem = pl.BlockSpec(memory_space=pltpu.VMEM)
    return pl.pallas_call(
        lambda *refs: pick_kernel(size, ways, *refs),
        out_shape=[jax.ShapeDtypeStruct((rows, blocks[0].shape[1]), jnp.bfloat16)] * ways,
        in_specs=[pl.BlockSpec(memory_space=pltpu.SMEM)] + [vmem] * (ways + size - 2),
        out_specs=[vmem] * ways,
        compiler_params=pltpu.CompilerParams(vmem_limit_bytes=16 << 20),
        name="pick",
    )(*asked, *blocks[1:])


def index_kernel(size, ways, *refs):
    asked, blocks = refs[:ways], refs[ways : ways + size]
    rel_ref, place_ref, lift_ref, spread_ref, table = refs[ways + size :]
    group, edge_slot = lax.axis_index("frames"), lax.axis_index("edges")
    asked = asked_tiles(asked)
    far = ring_distances(asked, size)
    unknowns, width = lift_ref.shape[0], place_ref.shape[1]
    rows = POSE * SUB
    sublane = lax.broadcasted_iota(jnp.int32, (SUB, LANES), 0)
    lane = lax.broadcasted_iota(jnp.int32, (SUB, LANES), 1)
    wide_sub = lax.broadcasted_iota(jnp.int32, (SUB, width), 0)
    wide_lane = lax.broadcasted_iota(jnp.int32, (SUB, width), 1)
    place = [jnp.zeros((SUB, width), jnp.float32) for _ in range(POSE)]
    lift = [jnp.zeros((SUB, LANES), jnp.float32) for _ in range(unknowns // SUB)]
    for slot in range(ways):
        edge, target = peer(edge_slot, slot, ways), asked[slot]
        wide = jnp.concatenate([target] * (width // LANES), axis=1)
        for c in range(POSE):
            at_target = (wide_lane == c * size + wide).astype(jnp.float32)
            at_source = (wide_lane == c * size + group).astype(jnp.float32)
            place[c] = jnp.where(wide_sub == edge, at_target - at_source, place[c])
        for g in range(unknowns // SUB):
            c, n = divmod(g * SUB, size)
            frame = sublane + n
            hit = (frame == target).astype(jnp.float32) - (frame == group).astype(jnp.float32)
            lift[g] = jnp.where(lane == c * SUB + edge, hit, lift[g])
    for c in range(POSE):
        place_ref[c * SUB : (c + 1) * SUB, :] = place[c]
        spread_ref[c * SUB : (c + 1) * SUB, :] = place[c]
    spread_ref[rows : rows + SUB, :] = ((wide_lane == unknowns) & (wide_sub == 0)).astype(jnp.float32)
    spread_ref[rows + SUB :, :] = jnp.zeros((LANES - rows - SUB, width), jnp.float32)
    for g in range(unknowns // SUB):
        lift_ref[g * SUB : (g + 1) * SUB, :] = lift[g]
    for d in range(size):
        terms = blocks[d][blocks[d].shape[0] - 16 :, :].astype(jnp.float32)
        table[d : d + 1, :] = terms[0:1, :] + terms[1:2, :] + terms[2:3, :]
    apart = jnp.zeros((SUB, LANES), jnp.float32)
    for slot in range(ways):
        pose = jnp.zeros((SUB, LANES), jnp.float32)
        for d in range(size):
            pose = jnp.where(far[slot] == d, table[d : d + 1, :], pose)
        apart = jnp.where(sublane == peer(edge_slot, slot, ways), pose - table[0:1, :], apart)
    for c in range(POSE):
        rel_ref[c * SUB : (c + 1) * SUB, :] = jnp.broadcast_to(apart[:, c : c + 1], (SUB, LANES))


def index_tables(asked, blocks, width):
    ways, size = len(asked), len(blocks)
    rows, unknowns = POSE * SUB, POSE * size
    shapes = [(rows, LANES), (rows, width), (unknowns, LANES), (LANES, width)]
    return call(
        lambda *refs: index_kernel(size, ways, *refs),
        shapes,
        (*asked, *blocks),
        "index",
        smem=(0,),
        scratch=[(-(-size // SUB) * SUB, LANES)],
    )


def gauss_newton_terms(heads, depth_ref, rel, lift_ref, spread_ref, gram_ref, damp_ref, total_ref):
    pixels = depth_ref.shape[1]
    rows = POSE * SUB
    sublane = lax.broadcasted_iota(jnp.int32, (SUB, LANES), 0)
    lane = lax.broadcasted_iota(jnp.int32, (SUB, LANES), 1)
    col_pos = (lane % WID).astype(jnp.float32)
    lane_row = lane // WID
    center_x = (WID - 1) / 2.0
    center_y = (HGT - 1) / 2.0
    ray_x = (col_pos - center_x) / focal
    move_x, move_y, move_z, turn_x, turn_y, turn_z = rel
    pairs_u = [(a, b) for a in (0, 2, 3, 4, 5) for b in (0, 2, 3, 4, 5) if a <= b]
    pairs_v = [(a, b) for a in (1, 2, 3, 4, 5) for b in (1, 2, 3, 4, 5) if a <= b]
    keys = sorted(set(pairs_u) | set(pairs_v))

    def chunk(index, carry):
        hess, grad = dict(zip(keys, carry[0])), list(carry[1])
        at = pl.ds(pl.multiple_of(index * LANES, LANES), LANES)
        depth = jnp.broadcast_to(depth_ref[:, at], (SUB, LANES))
        flow_u, flow_v, weight_u, weight_v = [heads[i, :, at] for i in range(4)]
        row_pos = (lane_row + index * (LANES // WID)).astype(jnp.float32)
        ray_y = (row_pos - center_y) / focal
        point_x = ray_x + turn_y - turn_z * ray_y + depth * move_x
        point_y = ray_y + turn_z * ray_x - turn_x + depth * move_y
        point_z = 1.0 + turn_x * ray_y - turn_y * ray_x + depth * move_z
        inverse_z = 1.0 / point_z
        slope = focal * inverse_z
        shift_u = slope * point_x
        shift_v = slope * point_y
        bend_u = -shift_u * inverse_z
        bend_v = -shift_v * inverse_z
        resid_u = col_pos + flow_u - (shift_u + center_x)
        resid_v = row_pos + flow_v - (shift_v + center_y)
        jac_u = [depth * slope, None, depth * bend_u, bend_u * ray_y, slope - bend_u * ray_x, -slope * ray_y]
        jac_v = [None, jac_u[0], depth * bend_v, bend_v * ray_y - slope, -bend_v * ray_x, slope * ray_x]
        depth_u = slope * move_x + bend_u * move_z
        depth_v = slope * move_y + bend_v * move_z
        scaled_u = [None if j is None else weight_u * j for j in jac_u]
        scaled_v = [None if j is None else weight_v * j for j in jac_v]
        for a, b in pairs_u:
            hess[a, b] = hess[a, b] + scaled_u[a] * jac_u[b]
        for a, b in pairs_v:
            hess[a, b] = hess[a, b] + scaled_v[a] * jac_v[b]
        for c in range(POSE):
            cross = None
            for scaled, resid, along in ((scaled_u, resid_u, depth_u), (scaled_v, resid_v, depth_v)):
                if scaled[c] is not None:
                    grad[c] = grad[c] + scaled[c] * resid
                    term = scaled[c] * along
                    cross = term if cross is None else cross + term
            gram_ref[c * SUB : (c + 1) * SUB, at] = cross
        pull_u = weight_u * depth_u
        pull_v = weight_v * depth_v
        curve = jnp.sum(pull_u * depth_u + pull_v * depth_v, axis=0, keepdims=True)
        slide = jnp.sum(pull_u * resid_u + pull_v * resid_v, axis=0, keepdims=True)
        gram_ref[rows : rows + SUB, at] = jnp.where(sublane == 0, slide, 0.0)
        damp_ref[:, at] = (1.0 + depth_damping) * curve + depth_floor
        return tuple(hess[k] for k in keys), tuple(grad)

    zero = jnp.zeros((SUB, LANES), jnp.float32)
    hess, grad = lax.fori_loop(
        0, pixels // LANES, chunk, (tuple(zero for _ in keys), tuple(zero for _ in range(POSE))), unroll=True
    )
    table = {k: jnp.sum(h, axis=1, keepdims=True) for k, h in zip(keys, hess)}
    slabs = []
    for c in range(POSE):
        slab = jnp.where(lane == rows, jnp.sum(grad[c], axis=1, keepdims=True), 0.0)
        for other in range(POSE):
            key = (min(c, other), max(c, other))
            if key in table:
                slab = jnp.where(lane == sublane + other * SUB, table[key], slab)
        slabs.append(slab)
    local = jnp.concatenate(slabs, axis=0)
    gram = gram_ref[...]
    scaled = gram[0:rows, :] / damp_ref[...]
    schur = nt_dot(scaled, gram, precision=highest)
    schur = jnp.concatenate([schur, jnp.zeros((rows, LANES - rows - SUB), jnp.float32)], axis=1)
    lifted = nn_dot(lift_ref[:, :rows], local - schur, precision=highest)
    total_ref[...] = nn_dot(lifted, spread_ref[...], precision=highest)


def solve_step(parts, unknowns):
    system = parts[0][...]
    for part in parts[1:]:
        system = system + part[...]
    width = system.shape[1]
    lane = lax.broadcasted_iota(jnp.int32, (SUB, width), 1)
    sublane = lax.broadcasted_iota(jnp.int32, (SUB, width), 0)
    groups = []
    for g in range(unknowns // SUB):
        block = system[g * SUB : (g + 1) * SUB, :]
        block = jnp.where(lane == sublane + g * SUB, block * (1.0 + pose_damping) + pose_floor, block)
        groups.append(block)
    for k in range(0, unknowns, PIVOTS):
        g, s = divmod(k, SUB)
        columns = [[jnp.broadcast_to(b[:, k + j : k + j + 1], b.shape) for b in groups] for j in range(PIVOTS)]
        tops = [groups[g][s + i : s + i + 1, :] for i in range(PIVOTS)]
        mult = [[columns[j][g][s + i : s + i + 1, :] for j in range(PIVOTS)] for i in range(PIVOTS)]
        for p in range(PIVOTS):
            inverse = 1.0 / mult[p][p]
            tops[p] = tops[p] * inverse
            for j in range(p + 1, PIVOTS):
                mult[p][j] = mult[p][j] * inverse
            for i in range(PIVOTS):
                if i != p:
                    tops[i] = tops[i] - mult[i][p] * tops[p]
                    for j in range(p + 1, PIVOTS):
                        mult[i][j] = mult[i][j] - mult[i][p] * mult[p][j]
        wide = [jnp.broadcast_to(t, groups[0].shape) for t in tops]
        for i in range(len(groups)):
            update = groups[i]
            for j in range(PIVOTS):
                update = update - columns[j][i] * wide[j]
            if i == g:
                for j in range(PIVOTS):
                    update = jnp.where(sublane == s + j, wide[j], update)
            groups[i] = update
    return jnp.concatenate([jnp.broadcast_to(b[:, unknowns : unknowns + 1], (SUB, LANES)) for b in groups], axis=0)


def split_rel(rel_ref):
    return [rel_ref[c * SUB : (c + 1) * SUB, :] for c in range(POSE)]


def first_kernel(ways, *refs):
    slots, refs = refs[:ways], refs[ways:]
    depth_ref, rel_ref, lift_ref, spread_ref, heads, gram_ref, damp_ref, total_ref = refs
    edge_slot = lax.axis_index("edges")
    if ways < SUB:
        heads[...] = jnp.zeros(heads.shape, jnp.float32)
    for slot in range(ways):
        edge = peer(edge_slot, slot, ways)
        for i in range(4):
            value = slots[slot][i : i + 1, :]
            if i >= 2:
                value = jax.nn.sigmoid(value)
            heads[i, pl.ds(edge, 1), :] = value
    gauss_newton_terms(heads, depth_ref, split_rel(rel_ref), lift_ref, spread_ref, gram_ref, damp_ref, total_ref)


def take_step(parts, place_ref, gram_ref, damp_ref, depth_ref, out_depth_ref):
    unknowns = parts[0].shape[0]
    step = solve_step(parts, unknowns)
    edge_step = nn_dot(place_ref[:, :unknowns], step, precision=highest)
    slices = [edge_step[c * SUB : (c + 1) * SUB, :] for c in range(POSE)]
    rows = POSE * SUB

    def chunk(index, carry):
        at = pl.ds(pl.multiple_of(index * LANES, LANES), LANES)
        total = slices[0] * gram_ref[0:SUB, at]
        for c in range(1, POSE):
            total = total + slices[c] * gram_ref[c * SUB : (c + 1) * SUB, at]
        along = jnp.sum(total, axis=0, keepdims=True)
        out_depth_ref[:, at] = depth_ref[:, at] + (gram_ref[rows : rows + 1, at] - along) / damp_ref[:, at]
        return carry

    lax.fori_loop(0, depth_ref.shape[1] // LANES, chunk, 0, unroll=4)
    return step, edge_step


def middle_kernel(count, *refs):
    parts, refs = refs[:count], refs[count:]
    (heads, gram_ref, damp_ref, depth_ref, rel_ref, place_ref, lift_ref, spread_ref,
     out_gram, out_damp, out_total, out_depth, out_step, out_rel) = refs
    step, edge_step = take_step(parts, place_ref, gram_ref, damp_ref, depth_ref, out_depth)
    out_step[...] = step
    out_rel[...] = rel_ref[...] + edge_step
    gauss_newton_terms(heads, out_depth, split_rel(out_rel), lift_ref, spread_ref, out_gram, out_damp, out_total)


def last_kernel(count, *refs):
    own_ref, parts, refs = refs[0], refs[1 : count + 1], refs[count + 1 :]
    before, refs = refs[: ITERS - 1], refs[ITERS - 1 :]
    gram_ref, damp_ref, depth_ref, place_ref, out_depth, out_pose, held = refs
    step, _ = take_step(parts, place_ref, gram_ref, damp_ref, depth_ref, out_depth)
    for other in before:
        step = step + other[...]
    held[...] = step
    frames, group = lax.axis_size("frames"), lax.axis_index("frames")
    lane = lax.broadcasted_iota(jnp.int32, (1, LANES), 1)
    moved = jnp.zeros((1, LANES), jnp.float32)
    for c in range(POSE):
        moved = jnp.where(lane == c, held[pl.ds(c * frames + group, 1), :], moved)
    out_pose[...] = own_ref[...] + moved[:, :POSE]


def call(kernel, shapes, inputs, name, smem=(), scratch=()):
    vmem = pl.BlockSpec(memory_space=pltpu.VMEM)
    f32 = lambda shape: jax.ShapeDtypeStruct(shape, jnp.float32)
    return pl.pallas_call(
        kernel,
        out_shape=[f32(s) for s in shapes],
        in_specs=[
            pl.BlockSpec(memory_space=pltpu.SMEM if i in smem else pltpu.VMEM) for i in range(len(inputs))
        ],
        out_specs=[vmem] * len(shapes),
        scratch_shapes=[pltpu.VMEM(s, jnp.float32) for s in scratch],
        compiler_params=pltpu.CompilerParams(vmem_limit_bytes=32 << 20),
        name=name,
    )(*inputs)


def sum_over(value, axis):
    size = lax.axis_size(axis)
    if size & (size - 1):
        parts = [value]
        for s in range(1, size):
            parts.append(lax.ppermute(value, axis, [(i, (i + s) % size) for i in range(size)]))
        return parts
    radices, left = [], size
    while left > 1:
        radix = 4 if left % 4 == 0 else 2
        radices.append(radix)
        left //= radix
    stride, parts = 1, [value]
    for radix in radices:
        value = sum(parts[1:], parts[0])
        parts = [value]
        for s in range(1, radix):
            parts.append(lax.ppermute(value, axis, [(i, i ^ (s * stride)) for i in range(size)]))
        stride *= radix
    return parts


def peer(index, slot, size):
    return index ^ slot if size & (size - 1) == 0 else (index + slot) % size


def exchange(values, axis):
    size = lax.axis_size(axis)
    out = [values[0]]
    for s in range(1, size):
        if size & (size - 1) == 0:
            pairs = [(i, i ^ s) for i in range(size)]
        else:
            pairs = [((i + s) % size, i) for i in range(size)]
        out.append(lax.ppermute(values[s], axis, pairs))
    return out


def ring_order(size):
    if size % 2:
        return list(range(size))
    return list(range(0, size, 2)) + list(range(size - 1, 0, -2))


def ring_gather(values, axis):
    size = lax.axis_size(axis)
    order = ring_order(size)
    ahead = [(order[(i + 1) % size], order[i]) for i in range(size)]
    behind = [(order[i], order[(i + 1) % size]) for i in range(size)]
    out = [[value] + [None] * (size - 1) for value in values]
    up, down = list(values), list(values)
    for s in range(1, size // 2 + 1):
        for i in range(len(values)):
            if 2 * s < size or i % 2 == 0:
                up[i] = out[i][s] = lax.ppermute(up[i], axis, ahead)
            if size - s > size // 2 or (2 * s == size and i % 2):
                down[i] = out[i][size - s] = lax.ppermute(down[i], axis, behind)
    return out


def per_device(fmap, context, poses, inv_depth, targets, w_corr, w_gates, w_cand, w_head):
    ways = lax.axis_size("edges")
    frames_total = lax.axis_size("frames")
    pixel_count = fmap.shape[1]
    share = pixel_count // ways
    bf = jnp.bfloat16
    first_band, second_band, target = pack(targets, poses.T, fmap, share)
    first, second = ring_gather((first_band, second_band), "frames")
    late_target, _ = lax.optimization_barrier((target, first[min(2, frames_total // 2)]))
    asked = [targets] + exchange([late_target] * ways, "edges")[1:]
    unknowns = POSE * frames_total
    width = -(-(unknowns + 1) // LANES) * LANES
    rows = POSE * SUB
    early, late = pick(asked, second, share // 2), pick(asked, first, share // 2)
    bands = exchange(late, "edges") + exchange(early, "edges")
    rel, place, lift, spread = index_tables(asked, first, width)

    own_source, own_context, own_corr, _ = lax.optimization_barrier((fmap[0], context[0], w_corr, late[0]))
    w_place = jnp.dot(jnp.asarray(PLACE, bf), own_corr, preferred_element_type=jnp.float32).astype(bf)
    w_place = jnp.concatenate([w_place[:TOTAL], w_place[TOTAL:]], axis=1)
    source, state, inject = prepare(own_source, own_context)
    hidden, heads = edge_update(bands, source, state, inject, w_place, w_gates, w_cand, w_head)
    slots = exchange([heads] * ways, "edges")

    big, line = (rows + SUB, pixel_count), (1, pixel_count)
    heads_all, gram, damp, total = call(
        lambda *refs: first_kernel(ways, *refs),
        [(4, SUB, pixel_count), big, line, (unknowns, width)],
        (*slots, inv_depth, rel, lift, spread),
        "terms",
    )
    depth = inv_depth
    steps = []
    for index in range(ITERS - 1):
        parts = sum_over(total, "frames")
        count = len(parts)
        gram, damp, total, depth, step, rel = call(
            lambda *refs: middle_kernel(count, *refs),
            [big, line, (unknowns, width), line, (unknowns, LANES), (rows, LANES)],
            (*parts, heads_all, gram, damp, depth, rel, place, lift, spread),
            "step",
        )
        steps.append(step)
    parts = sum_over(total, "frames")
    count = len(parts)
    depth, new_poses = call(
        lambda *refs: last_kernel(count, *refs),
        [line, (1, POSE)],
        (poses.T, *parts, *steps, gram, damp, depth, place),
        "final",
        scratch=[(unknowns, LANES)],
    )
    return (new_poses.T, depth, hidden[None])


def solution(mesh):
    return jax.shard_map(
        per_device,
        mesh=mesh,
        in_specs=(
            P("frames", None, None),
            P("frames", None, None),
            P(None, "frames"),
            P("frames", None),
            P(("frames", "edges")),
            P(),
            P(),
            P(),
            P(),
        ),
        out_specs=(P(None, "frames"), P("frames", None), P(("frames", "edges"), None, None)),
        check_vma=False,
    )
```

```python
import math

import numpy as np
import jax
import jax.numpy as jnp
from jax import lax
from jax.experimental import pallas as pl
from jax.experimental.pallas import tpu as pltpu
from jax.sharding import PartitionSpec as P

HGT = 48
WID = 64
LEVELS = 4
RADIUS = 3
ITERS = 2
SPAN = 2 * RADIUS + 1
POSE = 6
LANES = 128
SUB = 8
PIVOTS = 8

focal = 50.0
pose_damping = 0.1
pose_floor = 1.0
depth_damping = 0.1
depth_floor = 1.0
highest = lax.Precision.HIGHEST


PITCH = (64, 32, 16, 16)
WINDOW = tuple(8 * p for p in PITCH)
START = (0, 512, 768, 896)
TOTAL = 1024
PAD_ROWS = (54, 31, 19, 13)


def column_order():
    slot = np.arange(WID)
    return 8 * (7 - slot % 8) + slot // 8


def lookup_tables():
    cols = column_order()
    perm = np.zeros((2 * WID, 2 * WID), np.float32)
    for half in range(2):
        perm[half * WID + np.arange(WID), half * WID + cols] = 1.0
    mask = np.zeros((LEVELS, 2 * WID, LANES), np.float32)
    place = np.zeros((2 * TOTAL, LEVELS * SPAN * SPAN), np.float32)
    for level in range(LEVELS):
        pitch, width = PITCH[level], WID >> level
        per_block = LANES // pitch
        for y in range(8):
            block, first = y // per_block, (y % per_block) * pitch
            for b in range(-RADIUS, RADIUS + 1):
                lane = (first + b) % LANES
                reach = (cols >> level) + b
                ok = ((reach >= 0) & (reach < width)).astype(np.float32)
                mask[level, :, lane] = np.concatenate([ok, ok])
                row = START[level] + block * LANES + lane
                for odd in range(2):
                    a = y - RADIUS - (odd if level == 0 else 0)
                    if -RADIUS <= a <= RADIUS:
                        source = level * SPAN * SPAN + (a + RADIUS) * SPAN + b + RADIUS
                        place[odd * TOTAL + row, source] = 1.0
    pools = []
    for level in range(1, LEVELS):
        step = 1 << level
        pool = np.zeros((PITCH[level], step * WID), np.float32)
        for col in range(WID):
            pool[col // step, np.arange(step) * WID + col] = 1.0 / (step * step)
        pools.append(pool)
    return perm, mask, place, pools


PERM, MASK, PLACE, POOLS = lookup_tables()


def nt_dot(a, b, **kw):
    return lax.dot_general(a, b, (((1,), (1,)), ((), ())), preferred_element_type=jnp.float32, **kw)


def nn_dot(a, b, **kw):
    return lax.dot_general(a, b, (((1,), (0,)), ((), ())), preferred_element_type=jnp.float32, **kw)


def prepare_kernel(src_ref, ctx_ref, perm_ref, out_src, out_state, out_inject):
    width = out_state.shape[1]
    perm = perm_ref[...]

    def pair_loop(index, carry):
        at = pl.ds(pl.multiple_of(index * 2 * WID, 2 * WID), 2 * WID)
        out_src[at, :] = nn_dot(perm, src_ref[at, :]).astype(jnp.bfloat16)
        context = nn_dot(perm, ctx_ref[at, :])
        out_state[at, :] = jnp.tanh(context[:, :width]).astype(jnp.bfloat16)
        out_inject[at, :] = jnp.maximum(context[:, width:], 0.0).astype(jnp.bfloat16)
        return carry

    lax.fori_loop(0, HGT // 2, pair_loop, 0, unroll=4)


def prepare(source, context):
    vmem = pl.BlockSpec(memory_space=pltpu.VMEM)
    pixels, channels = source.shape
    half = context.shape[1] // 2
    return pl.pallas_call(
        prepare_kernel,
        out_shape=[jax.ShapeDtypeStruct((pixels, n), jnp.bfloat16) for n in (channels, half, half)],
        in_specs=[vmem] * 3,
        out_specs=[vmem] * 3,
        compiler_params=pltpu.CompilerParams(vmem_limit_bytes=16 << 20),
        name="prepare",
    )(source, context, jnp.asarray(PERM, jnp.bfloat16))


def edge_kernel(ways, *refs):
    band_refs, refs = refs[: 2 * ways], refs[2 * ways :]
    (src_ref, state_in, inject_ref, w_ref, head_ref, back_ref, mask_ref, pool1_ref, pool2_ref, pool3_ref, gates_hbm,
     cand_hbm, out_ref, heads_ref, pad0, pad1, pad2, pad3, corr_ref, state_ref, motion_ref, reset_ref, update_ref,
     gates_ref, cand_ref, sems) = refs
    copies = [
        pltpu.make_async_copy(gates_hbm, gates_ref, sems.at[0]),
        pltpu.make_async_copy(cand_hbm, cand_ref, sems.at[1]),
    ]
    for copy in copies:
        copy.start()
    width = out_ref.shape[1]
    edge = lax.axis_index("edges")
    half_share = band_refs[0].shape[0]
    scale = 1.0 / math.sqrt(src_ref.shape[1])
    pads = (pad0, pad1, pad2, pad3)
    for level, pad in enumerate(pads):
        lead = RADIUS * PITCH[level]
        body = (HGT >> level) * PITCH[level]
        pad[0:lead] = jnp.zeros((lead, pad.shape[1]), pad.dtype)
        pad[lead + body :] = jnp.zeros((pad.shape[0] - lead - body, pad.shape[1]), pad.dtype)
    for ref in (state_ref, motion_ref, reset_ref):
        ref[0:WID, :] = jnp.zeros((WID, width), ref.dtype)
        ref[(HGT + 1) * WID :, :] = jnp.zeros((WID, width), ref.dtype)
    state_ref[WID : (HGT + 1) * WID, :] = state_in[...]
    for slot in range(ways):
        for half in range(2):
            at = pl.multiple_of((peer(edge, slot, ways) * 2 + half) * half_share + RADIUS * WID, WID)
            pad0[pl.ds(at, half_share), :] = band_refs[half * ways + slot][...]
    for level, pool_ref in ((1, pool1_ref), (2, pool2_ref), (3, pool3_ref)):
        rows = 1 << level
        pool = pool_ref[...]
        for row in range(HGT >> level):
            first = (RADIUS + row * rows) * WID
            pooled = nn_dot(pool, pad0[first : first + rows * WID, :])
            at = (RADIUS + row) * PITCH[level]
            pads[level][at : at + PITCH[level], :] = pooled.astype(jnp.bfloat16)

    tile = 8 * WID
    blocks = HGT // 8
    start = lambda block: block * tile if isinstance(block, int) else pl.multiple_of(block * tile, tile)

    def look_up(block):
        for inner in range(4):
            pair = block * 4 + inner
            first = start(block) + inner * 2 * WID
            source = src_ref[pl.ds(first, 2 * WID), :]
            for level in range(LEVELS):
                shift = max(level - 1, 0)
                base = (pair >> shift) * PITCH[level] * (2 if level == 0 else 1)
                base = base if isinstance(base, int) else pl.multiple_of(base, 16)
                volume = nt_dot(source, pads[level][pl.ds(base, WINDOW[level]), :]) * scale
                keep = mask_ref[level]
                for lanes in range(WINDOW[level] // LANES):
                    part = volume[:, lanes * LANES : (lanes + 1) * LANES]
                    rolled = []
                    for group in range(2 * SUB):
                        turn = (8 >> level) * 7 + ((group % SUB) >> level)
                        rolled.append(
                            pltpu.roll(
                                part[group * SUB : (group + 1) * SUB, :],
                                (LANES - turn) % LANES,
                                1,
                                stride=8 >> level,
                                stride_axis=0,
                            )
                        )
                    value = jnp.concatenate(rolled, axis=0).astype(jnp.bfloat16) * keep
                    at = START[level] + lanes * LANES
                    corr_ref[pl.ds(first, 2 * WID), at : at + LANES] = value

    def encode(block):
        first = start(block)
        both = nn_dot(corr_ref[pl.ds(first, tile), :], w_ref[...])
        both = both.reshape(4, 2, WID, 2 * width)
        encoded = jnp.concatenate([both[:, :1, :, :width], both[:, 1:, :, width:]], axis=1).reshape(tile, width)
        inject = inject_ref[pl.ds(first, tile), :].astype(jnp.float32)
        motion_ref[pl.ds(first + WID, tile), :] = (jnp.maximum(encoded, 0.0) + inject).astype(jnp.bfloat16)

    sub = lax.broadcasted_iota(jnp.int32, (8, SUB, width), 1)

    def convolve(block, left_ref, right_ref, weights, columns):
        first = start(block)
        inputs = []
        for row in range(3):
            at = pl.ds(first + row * WID, tile)
            inputs.append(jnp.concatenate([left_ref[at, :], right_ref[at, :]], axis=1))
        taps = []
        for cols in columns:
            total = None
            for row in range(3):
                mats = [weights(row, col) for col in cols]
                mat = mats[0] if len(mats) == 1 else jnp.concatenate(mats, axis=1)
                part = nn_dot(inputs[row], mat)
                total = part if total is None else total + part
            size = total.shape[1] // len(cols)
            taps += [total[:, i * size : (i + 1) * size] for i in range(len(cols))]
        out = []
        for half in range(taps[0].shape[1] // width):
            left, mid, right = [t[:, half * width : (half + 1) * width].reshape(8, WID, width) for t in taps]
            wrapped = jnp.where(sub == SUB - 1, 0.0, jnp.roll(left[:, WID - SUB :], -1, axis=1))
            before = jnp.concatenate([wrapped, left[:, : WID - SUB]], axis=1)
            wrapped = jnp.where(sub == 0, 0.0, jnp.roll(right[:, :SUB], 1, axis=1))
            after = jnp.concatenate([right[:, SUB:], wrapped], axis=1)
            out.append((mid + before + after).reshape(tile, width))
        return out

    def gates(block):
        first = start(block)
        update, reset = convolve(
            block, state_ref, motion_ref, lambda r, c: gates_ref[r, c], ((0,), (1,), (2,))
        )
        update_ref[pl.ds(first, tile), :] = jax.nn.sigmoid(update)
        state = state_ref[pl.ds(first + WID, tile), :].astype(jnp.float32)
        reset_ref[pl.ds(first + WID, tile), :] = (jax.nn.sigmoid(reset) * state).astype(jnp.bfloat16)

    def candidate(block):
        first = start(block)
        (total,) = convolve(block, reset_ref, motion_ref, lambda r, c: cand_ref[r, c], ((0, 1), (2,)))
        update = update_ref[pl.ds(first, tile), :]
        state = state_ref[pl.ds(first + WID, tile), :].astype(jnp.float32)
        hidden = ((1.0 - update) * state + update * jnp.tanh(total)).astype(jnp.bfloat16)
        for inner in range(4):
            at = inner * 2 * WID
            ordered = nn_dot(back_ref[...], hidden[at : at + 2 * WID, :]).astype(jnp.bfloat16)
            out_ref[pl.ds(first + at, 2 * WID), :] = ordered
            heads_ref[:, pl.ds(first + at, 2 * WID)] = nt_dot(head_ref[...], ordered)

    look_up(0)

    def first_loop(block, carry):
        encode(block - 1)
        look_up(block)
        return carry

    lax.fori_loop(1, blocks, first_loop, 0)
    encode(blocks - 1)
    for copy in copies:
        copy.wait()
    def gates_loop(block, carry):
        gates(block)
        return carry

    def candidate_loop(block, carry):
        candidate(block)
        return carry

    lax.fori_loop(0, blocks, gates_loop, 0, unroll=3)
    lax.fori_loop(0, blocks, candidate_loop, 0, unroll=3)


def edge_update(bands, source, state, inject, w_place, w_gates, w_cand, w_head):
    pixels, channels = source.shape
    width = w_head.shape[0]
    ways = len(bands) // 2
    vmem = pl.BlockSpec(memory_space=pltpu.VMEM)
    hbm = pl.BlockSpec(memory_space=pl.ANY)
    bf, f32 = jnp.bfloat16, jnp.float32
    tables = [jnp.asarray(x, bf) for x in (PERM.T, MASK, *POOLS)]
    return pl.pallas_call(
        lambda *refs: edge_kernel(ways, *refs),
        out_shape=[
            jax.ShapeDtypeStruct((pixels, width), bf),
            jax.ShapeDtypeStruct((w_head.shape[1], pixels), f32),
        ],
        in_specs=[vmem] * (2 * ways + 5 + len(tables)) + [hbm] * 2,
        out_specs=[vmem, vmem],
        scratch_shapes=[pltpu.VMEM((PAD_ROWS[l] * PITCH[l], channels), bf) for l in range(LEVELS)]
        + [pltpu.VMEM((pixels, TOTAL), bf)]
        + [pltpu.VMEM(((HGT + 2) * WID, width), bf)] * 3
        + [
            pltpu.VMEM((pixels, width), f32),
            pltpu.VMEM(w_gates.shape, bf),
            pltpu.VMEM(w_cand.shape, bf),
            pltpu.SemaphoreType.DMA((2,)),
        ],
        compiler_params=pltpu.CompilerParams(vmem_limit_bytes=48 << 20),
        name="edge_update",
    )(*bands, source, state, inject, w_place, w_head.T, *tables, w_gates, w_cand)


def ring_place(frame, size):
    if size % 2:
        return frame
    return jnp.where(frame % 2 == 0, frame // 2, size - (frame + 1) // 2)


def ring_place_of(frame, size):
    if size % 2:
        return frame
    half = frame >> 1
    return jnp.where((frame & 1) == 0, half, size - 1 - half)


def pack_kernel(target_ref, pose_ref, band_ref, first_ref, second_ref, asked_ref, row_ref, sems):
    half = second_ref.shape[0]
    first = pl.multiple_of(lax.axis_index("edges") * 2 * half, 2 * half)
    copies = [
        pltpu.make_async_copy(
            band_ref.at[0, pl.ds(first + i * half, half), :], ref.at[pl.ds(0, half), :], sems.at[i]
        )
        for i, ref in enumerate((first_ref, second_ref))
    ]
    for copy in copies:
        copy.start()
    sublane = lax.broadcasted_iota(jnp.int32, (SUB, LANES), 0)
    row_ref[...] = jnp.zeros(row_ref.shape, jnp.float32)
    row_ref[0:1, 0:POSE] = pose_ref[...]
    pose = jnp.broadcast_to(row_ref[0:1, :], (SUB, LANES))
    high = pose.astype(jnp.bfloat16).astype(jnp.float32)
    mid = (pose - high).astype(jnp.bfloat16).astype(jnp.float32)
    low = pose - high - mid
    tail = jnp.where(sublane == 0, high, jnp.where(sublane == 1, mid, jnp.where(sublane == 2, low, 0.0)))
    tail = jnp.concatenate([tail, jnp.zeros((SUB, LANES), jnp.float32)], axis=0)
    first_ref[half:, :] = tail.astype(jnp.bfloat16)
    asked_ref[...] = jnp.full(asked_ref.shape, target_ref[0], jnp.int32)
    for copy in copies:
        copy.wait()


def pack(targets, pose_row, fmap, share):
    vmem = pl.BlockSpec(memory_space=pltpu.VMEM)
    return pl.pallas_call(
        pack_kernel,
        out_shape=[
            jax.ShapeDtypeStruct((share // 2 + 16, fmap.shape[2]), jnp.bfloat16),
            jax.ShapeDtypeStruct((share // 2, fmap.shape[2]), jnp.bfloat16),
            jax.ShapeDtypeStruct((SUB, LANES), jnp.int32),
        ],
        in_specs=[pl.BlockSpec(memory_space=pltpu.SMEM), vmem, pl.BlockSpec(memory_space=pl.ANY)],
        out_specs=[vmem] * 3,
        scratch_shapes=[pltpu.VMEM((SUB, LANES), jnp.float32), pltpu.SemaphoreType.DMA((2,))],
        name="pack",
    )(targets, pose_row, fmap)


def ring_distances(asked, size):
    here = ring_place(lax.axis_index("frames"), size)
    apart = [ring_place_of(a, size) - here for a in asked]
    return [jnp.where(d < 0, d + size, d) for d in apart]


def asked_tiles(refs):
    return [jnp.full((SUB, LANES), refs[0][0], jnp.int32)] + [ref[...] for ref in refs[1:]]


def pick_kernel(size, ways, *refs):
    asked, blocks, outs = refs[:ways], (None,) + refs[ways : ways + size - 1], refs[ways + size - 1 :]
    far = ring_distances(asked_tiles(asked), size)
    rows = outs[0].shape[0]
    tile = 2 * SUB
    chosen = []
    for s in range(ways):
        ones = [jnp.where(far[s] == d, 1.0, 0.0) for d in range(size)]
        chosen.append([jnp.concatenate([w, w], axis=0).astype(jnp.bfloat16) for w in ones])

    def step(index, carry):
        at = pl.ds(pl.multiple_of(index * tile, tile), tile)
        values = [None] + [block[at, :] for block in blocks[1:]]
        for s in range(ways):
            total = values[1] * chosen[s][1]
            for d in range(2, size):
                total = total + values[d] * chosen[s][d]
            outs[s][at, :] = total
        return carry

    lax.fori_loop(0, rows // tile, step, 0, unroll=2)


def pick(asked, blocks, rows):
    ways, size = len(asked), len(blocks)
    vmem = pl.BlockSpec(memory_space=pltpu.VMEM)
    return pl.pallas_call(
        lambda *refs: pick_kernel(size, ways, *refs),
        out_shape=[jax.ShapeDtypeStruct((rows, blocks[0].shape[1]), jnp.bfloat16)] * ways,
        in_specs=[pl.BlockSpec(memory_space=pltpu.SMEM)] + [vmem] * (ways + size - 2),
        out_specs=[vmem] * ways,
        compiler_params=pltpu.CompilerParams(vmem_limit_bytes=16 << 20),
        name="pick",
    )(*asked, *blocks[1:])


def index_kernel(size, ways, *refs):
    asked, blocks = refs[:ways], refs[ways : ways + size]
    rel_ref, place_ref, lift_ref, spread_ref, table = refs[ways + size :]
    group, edge_slot = lax.axis_index("frames"), lax.axis_index("edges")
    asked = asked_tiles(asked)
    far = ring_distances(asked, size)
    unknowns, width = lift_ref.shape[0], place_ref.shape[1]
    rows = POSE * SUB
    sublane = lax.broadcasted_iota(jnp.int32, (SUB, LANES), 0)
    lane = lax.broadcasted_iota(jnp.int32, (SUB, LANES), 1)
    wide_sub = lax.broadcasted_iota(jnp.int32, (SUB, width), 0)
    wide_lane = lax.broadcasted_iota(jnp.int32, (SUB, width), 1)
    place = [jnp.zeros((SUB, width), jnp.float32) for _ in range(POSE)]
    lift = [jnp.zeros((SUB, LANES), jnp.float32) for _ in range(unknowns // SUB)]
    for slot in range(ways):
        edge, target = peer(edge_slot, slot, ways), asked[slot]
        wide = jnp.concatenate([target] * (width // LANES), axis=1)
        for c in range(POSE):
            at_target = (wide_lane == c * size + wide).astype(jnp.float32)
            at_source = (wide_lane == c * size + group).astype(jnp.float32)
            place[c] = jnp.where(wide_sub == edge, at_target - at_source, place[c])
        for g in range(unknowns // SUB):
            c, n = divmod(g * SUB, size)
            frame = sublane + n
            hit = (frame == target).astype(jnp.float32) - (frame == group).astype(jnp.float32)
            lift[g] = jnp.where(lane == c * SUB + edge, hit, lift[g])
    for c in range(POSE):
        place_ref[c * SUB : (c + 1) * SUB, :] = place[c]
        spread_ref[c * SUB : (c + 1) * SUB, :] = place[c]
    spread_ref[rows : rows + SUB, :] = ((wide_lane == unknowns) & (wide_sub == 0)).astype(jnp.float32)
    spread_ref[rows + SUB :, :] = jnp.zeros((LANES - rows - SUB, width), jnp.float32)
    for g in range(unknowns // SUB):
        lift_ref[g * SUB : (g + 1) * SUB, :] = lift[g]
    for d in range(size):
        terms = blocks[d][blocks[d].shape[0] - 16 :, :].astype(jnp.float32)
        table[d : d + 1, :] = terms[0:1, :] + terms[1:2, :] + terms[2:3, :]
    apart = jnp.zeros((SUB, LANES), jnp.float32)
    for slot in range(ways):
        pose = jnp.zeros((SUB, LANES), jnp.float32)
        for d in range(size):
            pose = jnp.where(far[slot] == d, table[d : d + 1, :], pose)
        apart = jnp.where(sublane == peer(edge_slot, slot, ways), pose - table[0:1, :], apart)
    for c in range(POSE):
        rel_ref[c * SUB : (c + 1) * SUB, :] = jnp.broadcast_to(apart[:, c : c + 1], (SUB, LANES))


def index_tables(asked, blocks, width):
    ways, size = len(asked), len(blocks)
    rows, unknowns = POSE * SUB, POSE * size
    shapes = [(rows, LANES), (rows, width), (unknowns, LANES), (LANES, width)]
    return call(
        lambda *refs: index_kernel(size, ways, *refs),
        shapes,
        (*asked, *blocks),
        "index",
        smem=(0,),
        scratch=[(-(-size // SUB) * SUB, LANES)],
    )


def gauss_newton_terms(heads, depth_ref, rel, lift_ref, spread_ref, gram_ref, damp_ref, total_ref):
    pixels = depth_ref.shape[1]
    rows = POSE * SUB
    sublane = lax.broadcasted_iota(jnp.int32, (SUB, LANES), 0)
    lane = lax.broadcasted_iota(jnp.int32, (SUB, LANES), 1)
    col_pos = (lane % WID).astype(jnp.float32)
    lane_row = lane // WID
    center_x = (WID - 1) / 2.0
    center_y = (HGT - 1) / 2.0
    ray_x = (col_pos - center_x) / focal
    move_x, move_y, move_z, turn_x, turn_y, turn_z = rel
    pairs_u = [(a, b) for a in (0, 2, 3, 4, 5) for b in (0, 2, 3, 4, 5) if a <= b]
    pairs_v = [(a, b) for a in (1, 2, 3, 4, 5) for b in (1, 2, 3, 4, 5) if a <= b]
    keys = sorted(set(pairs_u) | set(pairs_v))

    def chunk(index, carry):
        hess, grad = dict(zip(keys, carry[0])), list(carry[1])
        at = pl.ds(pl.multiple_of(index * LANES, LANES), LANES)
        depth = jnp.broadcast_to(depth_ref[:, at], (SUB, LANES))
        flow_u, flow_v, weight_u, weight_v = [heads[i, :, at] for i in range(4)]
        row_pos = (lane_row + index * (LANES // WID)).astype(jnp.float32)
        ray_y = (row_pos - center_y) / focal
        point_x = ray_x + turn_y - turn_z * ray_y + depth * move_x
        point_y = ray_y + turn_z * ray_x - turn_x + depth * move_y
        point_z = 1.0 + turn_x * ray_y - turn_y * ray_x + depth * move_z
        inverse_z = 1.0 / point_z
        slope = focal * inverse_z
        shift_u = slope * point_x
        shift_v = slope * point_y
        bend_u = -shift_u * inverse_z
        bend_v = -shift_v * inverse_z
        resid_u = col_pos + flow_u - (shift_u + center_x)
        resid_v = row_pos + flow_v - (shift_v + center_y)
        jac_u = [depth * slope, None, depth * bend_u, bend_u * ray_y, slope - bend_u * ray_x, -slope * ray_y]
        jac_v = [None, jac_u[0], depth * bend_v, bend_v * ray_y - slope, -bend_v * ray_x, slope * ray_x]
        depth_u = slope * move_x + bend_u * move_z
        depth_v = slope * move_y + bend_v * move_z
        scaled_u = [None if j is None else weight_u * j for j in jac_u]
        scaled_v = [None if j is None else weight_v * j for j in jac_v]
        for a, b in pairs_u:
            hess[a, b] = hess[a, b] + scaled_u[a] * jac_u[b]
        for a, b in pairs_v:
            hess[a, b] = hess[a, b] + scaled_v[a] * jac_v[b]
        for c in range(POSE):
            cross = None
            for scaled, resid, along in ((scaled_u, resid_u, depth_u), (scaled_v, resid_v, depth_v)):
                if scaled[c] is not None:
                    grad[c] = grad[c] + scaled[c] * resid
                    term = scaled[c] * along
                    cross = term if cross is None else cross + term
            gram_ref[c * SUB : (c + 1) * SUB, at] = cross
        pull_u = weight_u * depth_u
        pull_v = weight_v * depth_v
        curve = jnp.sum(pull_u * depth_u + pull_v * depth_v, axis=0, keepdims=True)
        slide = jnp.sum(pull_u * resid_u + pull_v * resid_v, axis=0, keepdims=True)
        gram_ref[rows : rows + SUB, at] = jnp.where(sublane == 0, slide, 0.0)
        damp_ref[:, at] = (1.0 + depth_damping) * curve + depth_floor
        return tuple(hess[k] for k in keys), tuple(grad)

    zero = jnp.zeros((SUB, LANES), jnp.float32)
    hess, grad = lax.fori_loop(
        0, pixels // LANES, chunk, (tuple(zero for _ in keys), tuple(zero for _ in range(POSE))), unroll=True
    )
    table = {k: jnp.sum(h, axis=1, keepdims=True) for k, h in zip(keys, hess)}
    slabs = []
    for c in range(POSE):
        slab = jnp.where(lane == rows, jnp.sum(grad[c], axis=1, keepdims=True), 0.0)
        for other in range(POSE):
            key = (min(c, other), max(c, other))
            if key in table:
                slab = jnp.where(lane == sublane + other * SUB, table[key], slab)
        slabs.append(slab)
    local = jnp.concatenate(slabs, axis=0)
    gram = gram_ref[...]
    scaled = gram[0:rows, :] / damp_ref[...]
    schur = nt_dot(scaled, gram, precision=highest)
    schur = jnp.concatenate([schur, jnp.zeros((rows, LANES - rows - SUB), jnp.float32)], axis=1)
    lifted = nn_dot(lift_ref[:, :rows], local - schur, precision=highest)
    total_ref[...] = nn_dot(lifted, spread_ref[...], precision=highest)


def solve_step(parts, unknowns):
    system = parts[0][...]
    for part in parts[1:]:
        system = system + part[...]
    width = system.shape[1]
    lane = lax.broadcasted_iota(jnp.int32, (SUB, width), 1)
    sublane = lax.broadcasted_iota(jnp.int32, (SUB, width), 0)
    groups = []
    for g in range(unknowns // SUB):
        block = system[g * SUB : (g + 1) * SUB, :]
        block = jnp.where(lane == sublane + g * SUB, block * (1.0 + pose_damping) + pose_floor, block)
        groups.append(block)
    for k in range(0, unknowns, PIVOTS):
        g, s = divmod(k, SUB)
        columns = [[jnp.broadcast_to(b[:, k + j : k + j + 1], b.shape) for b in groups] for j in range(PIVOTS)]
        tops = [groups[g][s + i : s + i + 1, :] for i in range(PIVOTS)]
        mult = [[columns[j][g][s + i : s + i + 1, :] for j in range(PIVOTS)] for i in range(PIVOTS)]
        for p in range(PIVOTS):
            inverse = 1.0 / mult[p][p]
            tops[p] = tops[p] * inverse
            for j in range(p + 1, PIVOTS):
                mult[p][j] = mult[p][j] * inverse
            for i in range(PIVOTS):
                if i != p:
                    tops[i] = tops[i] - mult[i][p] * tops[p]
                    for j in range(p + 1, PIVOTS):
                        mult[i][j] = mult[i][j] - mult[i][p] * mult[p][j]
        wide = [jnp.broadcast_to(t, groups[0].shape) for t in tops]
        for i in range(len(groups)):
            update = groups[i]
            for j in range(PIVOTS):
                update = update - columns[j][i] * wide[j]
            if i == g:
                for j in range(PIVOTS):
                    update = jnp.where(sublane == s + j, wide[j], update)
            groups[i] = update
    return jnp.concatenate([jnp.broadcast_to(b[:, unknowns : unknowns + 1], (SUB, LANES)) for b in groups], axis=0)


def split_rel(rel_ref):
    return [rel_ref[c * SUB : (c + 1) * SUB, :] for c in range(POSE)]


def first_kernel(ways, *refs):
    slots, refs = refs[:ways], refs[ways:]
    depth_ref, rel_ref, lift_ref, spread_ref, heads, gram_ref, damp_ref, total_ref = refs
    edge_slot = lax.axis_index("edges")
    if ways < SUB:
        heads[...] = jnp.zeros(heads.shape, jnp.float32)
    for slot in range(ways):
        edge = peer(edge_slot, slot, ways)
        for i in range(4):
            value = slots[slot][i : i + 1, :]
            if i >= 2:
                value = jax.nn.sigmoid(value)
            heads[i, pl.ds(edge, 1), :] = value
    gauss_newton_terms(heads, depth_ref, split_rel(rel_ref), lift_ref, spread_ref, gram_ref, damp_ref, total_ref)


def take_step(parts, place_ref, gram_ref, damp_ref, depth_ref, out_depth_ref):
    unknowns = parts[0].shape[0]
    step = solve_step(parts, unknowns)
    edge_step = nn_dot(place_ref[:, :unknowns], step, precision=highest)
    slices = [edge_step[c * SUB : (c + 1) * SUB, :] for c in range(POSE)]
    rows = POSE * SUB

    def chunk(index, carry):
        at = pl.ds(pl.multiple_of(index * LANES, LANES), LANES)
        total = slices[0] * gram_ref[0:SUB, at]
        for c in range(1, POSE):
            total = total + slices[c] * gram_ref[c * SUB : (c + 1) * SUB, at]
        along = jnp.sum(total, axis=0, keepdims=True)
        out_depth_ref[:, at] = depth_ref[:, at] + (gram_ref[rows : rows + 1, at] - along) / damp_ref[:, at]
        return carry

    lax.fori_loop(0, depth_ref.shape[1] // LANES, chunk, 0, unroll=4)
    return step, edge_step


def middle_kernel(count, *refs):
    parts, refs = refs[:count], refs[count:]
    (heads, gram_ref, damp_ref, depth_ref, rel_ref, place_ref, lift_ref, spread_ref,
     out_gram, out_damp, out_total, out_depth, out_step, out_rel) = refs
    step, edge_step = take_step(parts, place_ref, gram_ref, damp_ref, depth_ref, out_depth)
    out_step[...] = step
    out_rel[...] = rel_ref[...] + edge_step
    gauss_newton_terms(heads, out_depth, split_rel(out_rel), lift_ref, spread_ref, out_gram, out_damp, out_total)


def last_kernel(count, *refs):
    own_ref, parts, refs = refs[0], refs[1 : count + 1], refs[count + 1 :]
    before, refs = refs[: ITERS - 1], refs[ITERS - 1 :]
    gram_ref, damp_ref, depth_ref, place_ref, out_depth, out_pose, held = refs
    step, _ = take_step(parts, place_ref, gram_ref, damp_ref, depth_ref, out_depth)
    for other in before:
        step = step + other[...]
    held[...] = step
    frames, group = lax.axis_size("frames"), lax.axis_index("frames")
    lane = lax.broadcasted_iota(jnp.int32, (1, LANES), 1)
    moved = jnp.zeros((1, LANES), jnp.float32)
    for c in range(POSE):
        moved = jnp.where(lane == c, held[pl.ds(c * frames + group, 1), :], moved)
    out_pose[...] = own_ref[...] + moved[:, :POSE]


def call(kernel, shapes, inputs, name, smem=(), scratch=()):
    vmem = pl.BlockSpec(memory_space=pltpu.VMEM)
    f32 = lambda shape: jax.ShapeDtypeStruct(shape, jnp.float32)
    return pl.pallas_call(
        kernel,
        out_shape=[f32(s) for s in shapes],
        in_specs=[
            pl.BlockSpec(memory_space=pltpu.SMEM if i in smem else pltpu.VMEM) for i in range(len(inputs))
        ],
        out_specs=[vmem] * len(shapes),
        scratch_shapes=[pltpu.VMEM(s, jnp.float32) for s in scratch],
        compiler_params=pltpu.CompilerParams(vmem_limit_bytes=32 << 20),
        name=name,
    )(*inputs)


def sum_over(value, axis):
    size = lax.axis_size(axis)
    if size & (size - 1):
        parts = [value]
        for s in range(1, size):
            parts.append(lax.ppermute(value, axis, [(i, (i + s) % size) for i in range(size)]))
        return parts
    radices, left = [], size
    while left > 1:
        radix = 4 if left % 4 == 0 else 2
        radices.append(radix)
        left //= radix
    stride, parts = 1, [value]
    for radix in radices:
        value = sum(parts[1:], parts[0])
        parts = [value]
        for s in range(1, radix):
            parts.append(lax.ppermute(value, axis, [(i, i ^ (s * stride)) for i in range(size)]))
        stride *= radix
    return parts


def peer(index, slot, size):
    return index ^ slot if size & (size - 1) == 0 else (index + slot) % size


def exchange(values, axis):
    size = lax.axis_size(axis)
    out = [values[0]]
    for s in range(1, size):
        if size & (size - 1) == 0:
            pairs = [(i, i ^ s) for i in range(size)]
        else:
            pairs = [((i + s) % size, i) for i in range(size)]
        out.append(lax.ppermute(values[s], axis, pairs))
    return out


def ring_order(size):
    if size % 2:
        return list(range(size))
    return list(range(0, size, 2)) + list(range(size - 1, 0, -2))


def ring_gather(values, axis):
    size = lax.axis_size(axis)
    order = ring_order(size)
    ahead = [(order[(i + 1) % size], order[i]) for i in range(size)]
    behind = [(order[i], order[(i + 1) % size]) for i in range(size)]
    out = [[value] + [None] * (size - 1) for value in values]
    up, down = list(values), list(values)
    for s in range(1, size // 2 + 1):
        for i in range(len(values)):
            if 2 * s < size or i % 2 == 0:
                up[i] = out[i][s] = lax.ppermute(up[i], axis, ahead)
            if size - s > size // 2 or (2 * s == size and i % 2):
                down[i] = out[i][size - s] = lax.ppermute(down[i], axis, behind)
    return out


def per_device(fmap, context, poses, inv_depth, targets, w_corr, w_gates, w_cand, w_head):
    ways = lax.axis_size("edges")
    frames_total = lax.axis_size("frames")
    pixel_count = fmap.shape[1]
    share = pixel_count // ways
    bf = jnp.bfloat16
    first_band, second_band, target = pack(targets, poses.T, fmap, share)
    first, second = ring_gather((first_band, second_band), "frames")
    late_target, _ = lax.optimization_barrier((target, first[min(2, frames_total // 2)]))
    asked = [targets] + exchange([late_target] * ways, "edges")[1:]
    unknowns = POSE * frames_total
    width = -(-(unknowns + 1) // LANES) * LANES
    rows = POSE * SUB
    early, late = pick(asked, second, share // 2), pick(asked, first, share // 2)
    bands = exchange(late, "edges") + exchange(early, "edges")
    rel, place, lift, spread = index_tables(asked, first, width)

    own_source, own_context, own_corr, _ = lax.optimization_barrier((fmap[0], context[0], w_corr, late[0]))
    w_place = jnp.dot(jnp.asarray(PLACE, bf), own_corr, preferred_element_type=jnp.float32).astype(bf)
    w_place = jnp.concatenate([w_place[:TOTAL], w_place[TOTAL:]], axis=1)
    source, state, inject = prepare(own_source, own_context)
    hidden, heads = edge_update(bands, source, state, inject, w_place, w_gates, w_cand, w_head)
    slots = exchange([heads] * ways, "edges")

    big, line = (rows + SUB, pixel_count), (1, pixel_count)
    heads_all, gram, damp, total = call(
        lambda *refs: first_kernel(ways, *refs),
        [(4, SUB, pixel_count), big, line, (unknowns, width)],
        (*slots, inv_depth, rel, lift, spread),
        "terms",
    )
    depth = inv_depth
    steps = []
    for index in range(ITERS - 1):
        parts = sum_over(total, "frames")
        count = len(parts)
        gram, damp, total, depth, step, rel = call(
            lambda *refs: middle_kernel(count, *refs),
            [big, line, (unknowns, width), line, (unknowns, LANES), (rows, LANES)],
            (*parts, heads_all, gram, damp, depth, rel, place, lift, spread),
            "step",
        )
        steps.append(step)
    parts = sum_over(total, "frames")
    count = len(parts)
    depth, new_poses = call(
        lambda *refs: last_kernel(count, *refs),
        [line, (1, POSE)],
        (poses.T, *parts, *steps, gram, damp, depth, place),
        "final",
        scratch=[(unknowns, LANES)],
    )
    return (new_poses.T, depth, hidden[None])


def solution(mesh):
    return jax.shard_map(
        per_device,
        mesh=mesh,
        in_specs=(
            P("frames", None, None),
            P("frames", None, None),
            P(None, "frames"),
            P("frames", None),
            P(("frames", "edges")),
            P(),
            P(),
            P(),
            P(),
        ),
        out_specs=(P(None, "frames"), P("frames", None), P(("frames", "edges"), None, None)),
        check_vma=False,
    )
```
